32 devices in a mesh: fsdp: 32 (over z, y, x, core).
Axes of the slice: x: 2, y: 2, z: 4, core: 2. Of those that a mesh axis runs over, the one named last changes fastest.
Arguments:
- inputs: bfloat16 [2, 32, 128, 1024], P(None, 'fsdp'), may hold values from -6 to 6
- lengths: int32 [2, 32], P(None, 'fsdp'), may hold values from 32 to 128, as said below
- cotangent: bfloat16 [2, 32, 128, 1024], P(None, 'fsdp'), may hold values from -6 to 6
- v_weight: bfloat16 [1024, 2048], P('fsdp'), may hold values from -0.1875 to 0.1875
- mx_weight: bfloat16 [1024, 4224], P('fsdp'), may hold values from -0.1875 to 0.1875
- h_weight: bfloat16 [2048, 1024], P('fsdp'), may hold values from -0.5 to 0.5
- up_weight: bfloat16 [1024, 4096], P('fsdp'), may hold values from -0.1875 to 0.1875
- down_weight: bfloat16 [4096, 1024], P('fsdp'), may hold values from -0.09375 to 0.09375
- small_params: bfloat16 [83712], P('fsdp'), may hold values from -4 to 4
Outputs:
- outputs: bfloat16 [2, 32, 128, 1024], P(None, 'fsdp')
- input_grads: bfloat16 [2, 32, 128, 1024], P(None, 'fsdp')
- v_weight_grad: float32 [1024, 2048], P('fsdp')
- mx_weight_grad: float32 [1024, 4224], P('fsdp')
- h_weight_grad: float32 [2048, 1024], P('fsdp')
- up_weight_grad: float32 [1024, 4096], P('fsdp')
- down_weight_grad: float32 [4096, 1024], P('fsdp')
- small_params_grad: float32 [83712], P('fsdp')
The draws below stay inside these ranges and needn't reach their ends.
Inputs may be any that keep to these rules, and one draw needn't show every extreme that they name: lengths[i, s] counts the valid slots of sequence s of micro-batch i from its first slot; some sequence has 128 and some 32.
All inputs are finite; a program needn't handle non-finite values.
Results may differ from the reference program's by a relative error of at most 0.011.
Values may be sent and summed in bfloat16 or wider, within the bound.
A program may use at most 320 MiB of HBM per device.

```python
import math
import jax
import jax.numpy as jnp
from jax import lax

D = 1024
Z = 128
VALUE_WIDTH = 2048
H = 16
FF = 4096
STRETCH = 128
MICRO = 2
SEQ = 128
SEQS = 32
LEN_MIN = 32


def draw_lengths(key, part):
    total = MICRO * SEQS
    key_values, key_longest, key_offset = jax.random.split(key, 3)
    values = jax.random.randint(key_values, (total,), LEN_MIN, SEQ + 1)
    longest = jax.random.randint(key_longest, (), 0, total)
    offset = jax.random.randint(key_offset, (), 1, total)
    shortest = (longest + offset) % total
    places = jnp.arange(total)
    values = jnp.where(places == longest, SEQ, values)
    values = jnp.where(places == shortest, LEN_MIN, values)
    return values.reshape(MICRO, SEQS).astype(jnp.int32)


def normal_piece(key, count, scale):
    return jnp.clip(scale * jax.random.normal(key, (count,), jnp.float32), -4.0, 4.0)


def uniform_piece(key, count, lower, upper):
    return jax.random.uniform(key, (count,), jnp.float32, lower, upper)


def draw_small_params(key, part):
    subkeys = [jax.random.fold_in(key, index) for index in range(10)]
    gains = 1.0 + jnp.clip(normal_piece(subkeys[0], 2 * D, 0.1), -0.4, 0.4)
    shifts = normal_piece(subkeys[1], 2 * D, 0.3)
    omega_scale = normal_piece(subkeys[2], D, 1.0)
    delta = uniform_piece(subkeys[8], D * H, -4.0, -1.0)
    alpha = uniform_piece(subkeys[9], D * H, -4.0, -1.0)
    affine = normal_piece(subkeys[3], 4 * Z, 0.3)
    relative = normal_piece(subkeys[4], STRETCH, 0.5)
    biases = normal_piece(subkeys[5], 2 * VALUE_WIDTH + 4 * D + Z + FF, 0.3)
    beta = normal_piece(subkeys[6], D * H, 1.0)
    eta = normal_piece(subkeys[7], D * H, 1.0)
    joined = jnp.concatenate([gains, shifts, omega_scale, affine, relative, biases, delta, alpha, beta, eta])
    return joined.astype(jnp.bfloat16)


def block_levels(rng, dims, shards, least, high):
    def one(position, parts):
        heights = jax.random.uniform(jax.random.fold_in(jax.random.fold_in(rng, 6), position), (parts,), jnp.float32, least / len(shards), high / len(shards))
        return jnp.repeat(jnp.exp(heights), dims[position] // parts).reshape((-1,) + (1,) * (len(dims) - position - 1))

    loudness = one(*shards[0])
    for cut in shards[1:]:
        loudness = loudness * one(*cut)
    return loudness


def centred(own_key, shape, width, most, cuts=(), dtype=jnp.bfloat16):
    level = block_levels(own_key, shape, cuts, -0.22, 0.18) if cuts else 1.0
    values = jax.random.normal(own_key, shape, jnp.float32) * width * level
    return jnp.minimum(jnp.maximum(values, -most), most).astype(dtype)


def setup_inputs(seed: int = 0) -> dict:
    splits = jax.random.split(jax.random.key(seed), 10)
    return {
        "inputs": centred(splits[0], (MICRO, SEQS, SEQ, D), 1.0, 6.0, ((1, 32),)),
        "lengths": draw_lengths(jax.random.fold_in(splits[9], 71), 0),
        "cotangent": centred(splits[2], (MICRO, SEQS, SEQ, D), 1.0, 6.0, ((1, 32),)),
        "v_weight": centred(splits[3], (D, VALUE_WIDTH), D ** -0.5, 0.1875, ((0, 32),)),
        "mx_weight": centred(splits[4], (D, 2 * D + Z + VALUE_WIDTH), D ** -0.5, 0.1875, ((0, 32),)),
        "h_weight": centred(splits[5], (VALUE_WIDTH, D), (VALUE_WIDTH // 16) ** -0.5, 0.5, ((0, 32),)),
        "up_weight": centred(splits[6], (D, FF), D ** -0.5, 0.1875, ((0, 32),)),
        "down_weight": centred(splits[7], (FF, D), FF ** -0.5, 0.09375, ((0, 32),)),
        "small_params": draw_small_params(jax.random.fold_in(splits[9], 71), 0),
    }


@jax.custom_vjp
def reduced_precision(v):
    return lax.optimization_barrier(v.astype(jnp.bfloat16)).astype(jnp.float32)

@jax.custom_vjp
def reduced_precision_backward(v):
    return v

def low_keep(v):
    return (reduced_precision(v), None)

def low_pass(kept, grad):
    return (grad,)

def back_keep(v):
    return (v, None)

def back_low(kept, grad):
    return (reduced_precision(grad),)
reduced_precision.defvjp(low_keep, low_pass)
reduced_precision_backward.defvjp(back_keep, back_low)
epsilon = 1e-05
highest_precision = lax.Precision.HIGHEST

def product(left_side, right_side):
    return jnp.dot(left_side, right_side, precision=highest_precision)

def split_vector(flat_vector):
    extents = (2 * D, 2 * D, D, 4 * Z, STRETCH, VALUE_WIDTH, 2 * D + Z + VALUE_WIDTH, D, FF, D, 4 * D * H)
    pieces = []
    offset = 0
    for extent in extents:
        pieces.append(flat_vector[offset:offset + extent])
        offset = offset + extent
    return pieces

def normalize(features, norm_gain, norm_shift):
    average = lax.optimization_barrier(jnp.mean(features, axis=-1, keepdims=True))
    centered = features - average
    spread = lax.optimization_barrier(jnp.mean(centered * centered, axis=-1, keepdims=True))
    return centered * lax.rsqrt(spread + epsilon) * norm_gain + norm_shift

def ema_filter(signal, ema_params):
    sequence_length = signal.shape[0]
    gate_rate = jax.nn.sigmoid(ema_params[0])
    retain = 1.0 - gate_rate * jax.nn.sigmoid(ema_params[1])
    weight = gate_rate * ema_params[2] * ema_params[3] * (1.0 / math.sqrt(H))
    lag_steps = jnp.arange(sequence_length).astype(jnp.float32)
    powers = jnp.exp(lag_steps[None, None, :] * jnp.log(retain)[:, :, None])
    kernel = lax.optimization_barrier(jnp.sum(weight[:, :, None] * powers, axis=1))
    padded = 2 * sequence_length
    spectrum = jnp.fft.rfft(signal.T, n=padded, axis=-1) * jnp.fft.rfft(kernel, n=padded, axis=-1)
    return jnp.fft.irfft(spectrum, n=padded, axis=-1)[:, :sequence_length].T

def offset_table(relative):
    places = jnp.arange(STRETCH).astype(jnp.int32)
    offsets = places[:, None] - places[None, :]
    onehot = (offsets[:, :, None] == places[None, None, :]).astype(jnp.float32)
    table = product(onehot.reshape(STRETCH * STRETCH, STRETCH), relative).reshape(STRETCH, STRETCH)
    return (table, offsets >= 0)

def attention_weights(raw_scores, relative):
    table, causal = offset_table(relative)
    scores = jnp.where(causal, raw_scores * (1.0 / math.sqrt(Z)) + table, -1e+30)
    largest = lax.optimization_barrier(jnp.max(scores, axis=-1, keepdims=True))
    raised = jnp.exp(scores - largest)
    return raised / lax.optimization_barrier(jnp.sum(raised, axis=-1, keepdims=True))

def forward(inputs_row, valid, weights):
    v_full, mx_full, h_full, up_full, down_full, small_full = weights
    gains, shifts, omega_scale, affine, relative, v_bias, mx_bias, h_bias, up_bias, down_bias, ema_flat = split_vector(small_full)
    gains = gains.reshape(2, D)
    shifts = shifts.reshape(2, D)
    affine = affine.reshape(4, Z)
    sequence_length = inputs_row.shape[0]
    blocks = sequence_length // STRETCH
    normed = normalize(inputs_row, gains[0], shifts[0])
    masked = normed * valid
    mixed = jax.nn.silu(ema_filter(masked, ema_flat.reshape(4, D, H)) + omega_scale * masked)
    values = jax.nn.silu(reduced_precision_backward(product(reduced_precision(normed), v_full)) + v_bias)
    base = reduced_precision_backward(product(reduced_precision(mixed), mx_full)) + mx_bias
    update = jax.nn.sigmoid(base[:, :D])
    shared = jax.nn.silu(base[:, D:D + Z + VALUE_WIDTH])
    hidden_x = base[:, D + Z + VALUE_WIDTH:]
    latent = shared[:, :Z]
    reset = shared[:, Z:]
    query = reduced_precision(latent * (1.0 + affine[0]) + affine[2]).reshape(blocks, STRETCH, Z)
    keys = reduced_precision(latent * (1.0 + affine[1]) + affine[3]).reshape(blocks, STRETCH, Z)
    raw_scores = reduced_precision_backward(jnp.einsum('nqz,nkz->nqk', query, keys, precision=highest_precision))
    softmax_probs = attention_weights(raw_scores, relative)
    values_reduced = reduced_precision(values).reshape(blocks, STRETCH, VALUE_WIDTH)
    attended_values = reduced_precision_backward(jnp.einsum('dug,dgl->dul', reduced_precision(softmax_probs), values_reduced, precision=highest_precision)).reshape(sequence_length, VALUE_WIDTH)
    hidden = jax.nn.silu(hidden_x + reduced_precision_backward(product(reduced_precision(attended_values * reset), h_full)) + h_bias)
    first = inputs_row + valid * update * (hidden - inputs_row)
    second = normalize(first, gains[1], shifts[1])
    inner = jax.nn.silu(reduced_precision_backward(product(reduced_precision(second), up_full)) + up_bias)
    return first + valid * (reduced_precision_backward(product(reduced_precision(inner), down_full)) + down_bias)

def reference(inputs, lengths, cotangent, v_weight, mx_weight, h_weight, up_weight, down_weight, small_params):
    params = tuple((item.astype(jnp.float32) for item in (v_weight, mx_weight, h_weight, up_weight, down_weight, small_params)))
    group = math.gcd(SEQS, max(1, 4096 // SEQ))
    rounds = MICRO * SEQS // group
    rows = inputs.reshape(rounds, group, SEQ, D)
    spans = lengths.reshape(rounds, group)
    cots = cotangent.reshape(rounds, group, SEQ, D)
    positions = jnp.arange(SEQ).astype(jnp.int32)

    def one_round(totals, pieces):
        rows_block, span_block, cot_block = pieces
        valid = (positions[None, :] < span_block[:, None]).astype(jnp.float32)[:, :, None]

        def run(weights, rows_float):
            return jax.vmap(forward, in_axes=(0, 0, None))(rows_float, valid, weights)
        result, pullback = jax.vjp(run, params, rows_block.astype(jnp.float32))
        weight_grads, row_grads = pullback(cot_block.astype(jnp.float32))
        totals = jax.tree.map(jnp.add, totals, weight_grads)
        return (totals, (result.astype(jnp.bfloat16), row_grads.astype(jnp.bfloat16)))
    start = tuple((jnp.zeros(item.shape, jnp.float32) for item in params))
    totals, (results, row_grads) = lax.scan(one_round, start, (rows, spans, cots))
    return (results.reshape(MICRO, SEQS, SEQ, D), row_grads.reshape(MICRO, SEQS, SEQ, D), totals[0], totals[1], totals[2], totals[3], totals[4], totals[5])
```

```python
import functools
from functools import partial
import math

import jax
import jax.numpy as jnp
from jax import lax
from jax.experimental import pallas as pl
from jax.experimental.pallas import tpu as pltpu
from jax.sharding import PartitionSpec as P

D = 1024
Z = 128
VALUE_WIDTH = 2048
H = 16
FF = 4096
STRETCH = 128


epsilon = 1e-05
highest_precision = lax.Precision.HIGHEST


MESH = pl.DeviceIdType.MESH

class Place:
    def __init__(self, dims):
        self.Z, self.Y, self.X = dims
        me = lax.axis_index("fsdp")
        self.me = me
        self.c = me % 2
        self.x = (me // 2) % self.X
        self.y = (me // (2 * self.X)) % self.Y
        self.z = me // (2 * self.X * self.Y)
        self.nx = self.dev(self.z, self.y, 1 - self.x, self.c)
        self.ny = self.dev(self.z, 1 - self.y, self.x, self.c)
        self.nc = self.dev(self.z, self.y, self.x, 1 - self.c)
        self.has_down = self.z > 0
        self.has_up = self.z < self.Z - 1
        self.down = self.dev(jnp.maximum(self.z - 1, 0), self.y, self.x, self.c)
        self.up = self.dev(jnp.minimum(self.z + 1, self.Z - 1), self.y, self.x, self.c)
    def dev(self, z, y, x, c):
        return ((z * self.Y + y) * self.X + x) * 2 + c
    def barrier(self):
        bar = pltpu.get_barrier_semaphore()
        def tell(d):
            pl.semaphore_signal(bar, inc=1, device_id=(d,), device_id_type=MESH)
        for d in (self.nx, self.ny, self.nc):
            tell(d)
        pl.when(self.has_down)(lambda: tell(self.down))
        pl.when(self.has_up)(lambda: tell(self.up))
        pl.semaphore_wait(bar, 3 + jnp.where(self.has_down, 1, 0) + jnp.where(self.has_up, 1, 0))

def when(cond, f):
    if cond is None: f()
    else: pl.when(cond)(f)

class Gather:
    def __init__(self, place, ins, outs, send_sem, recv_sem):
        self.p, self.ins, self.outs = place, ins, outs
        self.ss, self.rs = send_sem, recv_sem
        self.ids, self.pend = {}, []
    def rows(self, k, h):
        n = self.ins[k].shape[0]
        return (0, n) if h == 2 else (h * (n // 2), n // 2)
    def copy(self, key, k, shard, h, to, own=False):
        i = self.ids.setdefault((key, k), len(self.ids))
        r, n = self.rows(k, h)
        full = self.ins[k].shape[0]
        dst = self.outs[k].at[pl.ds(shard * full + r, n)]
        src = self.ins[k].at[pl.ds(r, n)] if own else dst
        return pltpu.make_async_remote_copy(src_ref=src, dst_ref=dst, send_sem=self.ss.at[i], recv_sem=self.rs.at[i], device_id=(to,), device_id_type=MESH)
    def send(self, cond, *a):
        when(cond, lambda: self.copy(*a).start())
        self.pend.append((cond, lambda: self.copy(*a).wait_send()))
    def recv(self, cond, key, k, shard, h):
        when(cond, lambda: self.copy(key, k, shard, h, self.p.me).wait_recv())
    def col(self, o):
        p = self.p
        if o == 0: return None, p.z
        if o > 0: return p.z - o >= 0, jnp.maximum(p.z - o, 0)
        return p.z - o <= p.Z - 1, jnp.minimum(p.z - o, p.Z - 1)
    def offs(self, s):
        return (0,) if s == 0 else (s, -s)
    def stage(self, k, s):
        p = self.p
        L = p.Z
        if s < L:
            for o in self.offs(s):
                cond, zz = self.col(o)
                sh = p.dev(zz, p.y, p.x, p.c)
                own = o == 0
                if not own:
                    self.recv(cond, ("z", o), k, sh, 2)
                if s + 1 < L:
                    both = lambda c1: c1 if cond is None else jnp.logical_and(cond, c1)
                    if o >= 0: self.send(both(p.has_up), ("z", s + 1), k, sh, 2, p.up, own)
                    if o <= 0: self.send(both(p.has_down), ("z", -(s + 1)), k, sh, 2, p.down, own)
                self.send(cond, ("x", o), k, sh, 2, p.nx, own)
                self.send(cond, ("y", o), k, sh, 2, p.ny, own)
                self.send(cond, ("c", o), k, sh, 2, p.nc, own)
        if 1 <= s <= L:
            for o in self.offs(s - 1):
                cond, zz = self.col(o)
                sx, sy = p.dev(zz, p.y, 1 - p.x, p.c), p.dev(zz, 1 - p.y, p.x, p.c)
                self.recv(cond, ("x", o), k, sx, 2)
                self.send(cond, ("xy", o), k, sx, 0, p.ny)
                self.send(cond, ("cx", o), k, sx, 2, p.nc)
                self.recv(cond, ("y", o), k, sy, 2)
                self.send(cond, ("yx", o), k, sy, 1, p.nx)
                self.send(cond, ("cy", o), k, sy, 2, p.nc)
        if 2 <= s <= L + 1:
            for o in self.offs(s - 2):
                cond, zz = self.col(o)
                sd = p.dev(zz, 1 - p.y, 1 - p.x, p.c)
                self.recv(cond, ("xy", o), k, sd, 0)
                self.recv(cond, ("yx", o), k, sd, 1)
                self.send(cond, ("cd", o), k, sd, 2, p.nc)
        if s == L + 2:
            for t in range(L):
                for o in self.offs(t):
                    cond, zz = self.col(o)
                    for key, yy, xx in (("c", p.y, p.x), ("cx", p.y, 1 - p.x), ("cy", 1 - p.y, p.x), ("cd", 1 - p.y, 1 - p.x)):
                        self.recv(cond, (key, o), k, p.dev(zz, yy, xx, 1 - p.c), 2)
    def stages(self):
        return self.p.Z + 3
    def finish(self):
        for cond, f in self.pend:
            when(cond, f)

def sems_needed(dims, K):
    Z = dims[0]
    offs = 2 * Z - 1
    return K * (2 * (Z - 1) + 8 * offs)

def ag_kernel(dims, K, *refs):
    ins, outs = refs[:K], refs[K:2 * K]
    own, ss, rs = refs[2 * K:]
    p = Place(dims)
    p.barrier()
    g = Gather(p, ins, outs, ss, rs)
    cps = [pltpu.make_async_copy(ins[k], outs[k].at[pl.ds(p.me * ins[k].shape[0], ins[k].shape[0])], own.at[k]) for k in range(K)]
    for cp in cps: cp.start()
    S = g.stages()
    for t in range(K + S - 1):
        for k in range(K):
            if 0 <= t - k < S: g.stage(k, t - k)
    g.finish()
    for cp in cps: cp.wait()

def gather(dims, n, arrays, cid):
    K = len(arrays)
    ns = sems_needed(dims, K)
    return pl.pallas_call(functools.partial(ag_kernel, dims, K),
        out_shape=[jax.ShapeDtypeStruct((n * a.shape[0],) + a.shape[1:], a.dtype) for a in arrays],
        in_specs=[pl.BlockSpec(memory_space=pl.ANY)] * K, out_specs=[pl.BlockSpec(memory_space=pl.ANY)] * K,
        scratch_shapes=[pltpu.SemaphoreType.DMA((K,)), pltpu.SemaphoreType.DMA((ns,)), pltpu.SemaphoreType.DMA((ns,))],
        compiler_params=pltpu.CompilerParams(collective_id=cid, has_side_effects=True))(*arrays)


def grid_of(n):
    chips = n // 2
    return (chips // 4, 2, 2)


def gather_all(n, weights, small):
    if n != 32:
        return tuple(lax.all_gather(w, "fsdp", axis=0, tiled=True) for w in weights + (small,))
    dims = grid_of(n)
    rows = -(-small.shape[0] // 128)
    rows = -(-rows // 32) * 32
    padded = jnp.pad(small, (0, rows * 128 - small.shape[0])).reshape(rows, 128)
    (packed,) = gather(dims, n, (padded,), 0)
    full = gather(dims, n, weights, 1)
    flat = packed.reshape(n, rows * 128)[:, : small.shape[0]].reshape(-1)
    return tuple(full) + (flat,)


def split_vector(flat_vector):
    extents = (
        2 * D,
        2 * D,
        D,
        4 * Z,
        STRETCH,
        VALUE_WIDTH,
        2 * D + Z + VALUE_WIDTH,
        D,
        FF,
        D,
        4 * D * H,
    )
    pieces = []
    offset = 0
    for extent in extents:
        pieces.append(flat_vector[offset : offset + extent])
        offset = offset + extent
    return pieces


def normalize(features, norm_gain, norm_shift):
    average = jnp.mean(features, axis=-1, keepdims=True)
    centered = features - average
    spread = jnp.mean(centered * centered, axis=-1, keepdims=True)
    return centered * lax.rsqrt(spread + epsilon) * norm_gain + norm_shift


def smooth_signal(signal, ema_params):
    sequence_length, width_all = signal.shape
    block = min(32, sequence_length)
    count = sequence_length // block
    gate_rate = jax.nn.sigmoid(ema_params[0])
    retain = 1.0 - gate_rate * jax.nn.sigmoid(ema_params[1])
    weight = gate_rate * ema_params[2] * ema_params[3] * (1.0 / math.sqrt(ema_params.shape[2]))
    lag_steps = jnp.arange(block).astype(jnp.float32)
    powers = jnp.exp(lag_steps[:, None, None] * jnp.log(retain)[None, :, :])
    kernel = jnp.einsum("jch,ch->cj", powers, weight, precision=highest_precision)
    pattern = jnp.concatenate(
        [kernel[:, :1], jnp.zeros((width_all, block - 1), jnp.float32), kernel[:, 1:][:, ::-1]],
        axis=1,
    )
    tiled = jnp.tile(pattern, (1, block))[:, : block * (2 * block - 2)]
    toeplitz = tiled.reshape(width_all, block, 2 * block - 2)[:, :, :block]
    blocks = signal.reshape(count, block, width_all)
    inside = jnp.einsum("cts,nsc->ntc", toeplitz, blocks, precision=highest_precision)
    local_sums = jnp.einsum("nsc,sch->nch", blocks, powers[::-1], precision=highest_precision)
    whole_decay = powers[-1] * retain

    def advance(state, piece):
        return (whole_decay * state + piece, state)

    final_state, starts = lax.scan(advance, jnp.zeros(retain.shape, jnp.float32), local_sums)
    carried = jnp.einsum(
        "nch,tch->ntc", starts * weight, powers * retain[None], precision=highest_precision
    )
    return (inside + carried).reshape(sequence_length, width_all)


def offset_table(relative):
    places = jnp.arange(STRETCH)
    offsets = places[:, None] - places[None, :]
    onehot = (offsets[:, :, None] == places[None, None, :]).astype(jnp.float32)
    table = jnp.dot(
        onehot.reshape(STRETCH * STRETCH, STRETCH), relative, precision=highest_precision
    ).reshape(STRETCH, STRETCH)
    return (table, offsets >= 0)


def attention_weights(raw_scores, relative):
    table, causal = offset_table(relative)
    scores = jnp.where(causal, raw_scores * (1.0 / math.sqrt(Z)) + table, -1e30)
    largest = jnp.max(scores, axis=-1, keepdims=True)
    raised = jnp.exp(scores - largest)
    return raised / jnp.sum(raised, axis=-1, keepdims=True)


def first_piece(valid, inputs_row, gain_one, shift_one, omega_scale, ema_params):
    normed = normalize(inputs_row, gain_one, shift_one)
    masked = normed * valid
    mixed = jax.nn.silu(smooth_signal(masked, ema_params) + omega_scale * masked)
    return (normed, mixed)


def second_piece(values_mm, v_bias, base_mm, mx_bias, affine):
    values = jax.nn.silu(values_mm + v_bias)
    base = base_mm + mx_bias
    update = jax.nn.sigmoid(base[:, :D])
    shared = jax.nn.silu(base[:, D : D + Z + VALUE_WIDTH])
    hidden_x = base[:, D + Z + VALUE_WIDTH :]
    latent = shared[:, :Z]
    reset = shared[:, Z:]
    query = latent * (1.0 + affine[0]) + affine[2]
    keys_float = latent * (1.0 + affine[1]) + affine[3]
    return (values, update, reset, hidden_x, query, keys_float)


def fifth_piece(valid, hidden_mm, hidden_x, h_bias, update, inputs_row, gain_two, shift_two):
    hidden = jax.nn.silu(hidden_x + hidden_mm + h_bias)
    first = inputs_row + valid * update * (hidden - inputs_row)
    return (first, normalize(first, gain_two, shift_two))


def activate(up_mm, up_bias):
    return jax.nn.silu(up_mm + up_bias)


def forward_rows(inputs_row, valid, weights):
    v_full, mx_full, h_full, up_full, down_full, small_full = weights
    parts = [piece.astype(jnp.float32) for piece in split_vector(small_full)]
    (
        gains,
        shifts,
        omega_scale,
        affine,
        relative,
        v_bias,
        mx_bias,
        h_bias,
        up_bias,
        down_bias,
        ema_flat,
    ) = parts
    gains = gains.reshape(2, D)
    shifts = shifts.reshape(2, D)
    affine = affine.reshape(4, Z)
    sequence_length = inputs_row.shape[0]
    blocks = sequence_length // STRETCH
    row_float = inputs_row.astype(jnp.float32)
    (normed, mixed), pull_first = jax.vjp(
        partial(first_piece, valid),
        row_float,
        gains[0],
        shifts[0],
        omega_scale,
        ema_flat.reshape(4, D, H),
    )
    normed_low = normed.astype(jnp.bfloat16)
    mixed_low = mixed.astype(jnp.bfloat16)
    values_mm = jnp.dot(normed_low, v_full, preferred_element_type=jnp.float32)
    base_mm = jnp.dot(mixed_low, mx_full, preferred_element_type=jnp.float32)
    (values, update, reset, hidden_x, query, keys_float), pull_second = jax.vjp(
        second_piece, values_mm, v_bias, base_mm, mx_bias, affine
    )
    query_low = query.astype(jnp.bfloat16).reshape(blocks, STRETCH, Z)
    keys_low = keys_float.astype(jnp.bfloat16).reshape(blocks, STRETCH, Z)
    values_reduced = values.astype(jnp.bfloat16).reshape(blocks, STRETCH, VALUE_WIDTH)
    raw_scores = jnp.einsum("nqz,nkz->nqk", query_low, keys_low, preferred_element_type=jnp.float32)
    softmax_probs, pull_third = jax.vjp(attention_weights, raw_scores, relative)
    softmax_probs_reduced = softmax_probs.astype(jnp.bfloat16)
    attended_values = jnp.einsum(
        "dug,dgl->dul", softmax_probs_reduced, values_reduced, preferred_element_type=jnp.float32
    ).reshape(sequence_length, VALUE_WIDTH)
    gated_low = (attended_values * reset).astype(jnp.bfloat16)
    hidden_mm = jnp.dot(gated_low, h_full, preferred_element_type=jnp.float32)
    (first, second), pull_fifth = jax.vjp(
        partial(fifth_piece, valid),
        hidden_mm,
        hidden_x,
        h_bias,
        update,
        row_float,
        gains[1],
        shifts[1],
    )
    second_low = second.astype(jnp.bfloat16)
    up_mm = jnp.dot(second_low, up_full, preferred_element_type=jnp.float32)
    inner, pull_sixth = jax.vjp(activate, up_mm, up_bias)
    inner_low = inner.astype(jnp.bfloat16)
    down_mm = jnp.dot(inner_low, down_full, preferred_element_type=jnp.float32)
    result = (first + valid * (down_mm + down_bias)).astype(jnp.bfloat16)
    kept = (
        valid,
        normed_low,
        mixed_low,
        query_low,
        keys_low,
        values_reduced,
        softmax_probs_reduced,
        attended_values,
        reset,
        gated_low,
        second_low,
        inner_low,
        pull_first,
        pull_second,
        pull_third,
        pull_fifth,
        pull_sixth,
    )
    return (result, kept)


def backward_rows(kept, cot_row, weights):
    v_full, mx_full, h_full, up_full, down_full, small_full = weights
    (
        valid,
        normed_low,
        mixed_low,
        query_low,
        keys_low,
        values_reduced,
        softmax_probs_reduced,
        attended_values,
        reset,
        gated_low,
        second_low,
        inner_low,
        pull_first,
        pull_second,
        pull_third,
        pull_fifth,
        pull_sixth,
    ) = kept
    sequence_length = cot_row.shape[0]
    blocks = sequence_length // STRETCH
    grad_out = cot_row.astype(jnp.float32)
    down_grad = valid * grad_out
    down_bias_grad = jnp.sum(down_grad, axis=0)
    down_low = down_grad.astype(jnp.bfloat16)
    down_weight_grad = jnp.einsum(
        "ti,td->id", inner_low, down_low, preferred_element_type=jnp.float32
    )
    inner_grad = jnp.einsum("td,id->ti", down_low, down_full, preferred_element_type=jnp.float32)
    up_grad, up_bias_grad = pull_sixth(inner_grad)
    up_low = up_grad.astype(jnp.bfloat16)
    up_weight_grad = jnp.einsum("td,tf->df", second_low, up_low, preferred_element_type=jnp.float32)
    second_grad = jnp.einsum("tf,df->td", up_low, up_full, preferred_element_type=jnp.float32)
    (
        hidden_mm_grad,
        hidden_x_grad,
        h_bias_grad,
        update_grad,
        row_grad_first,
        gain_two_grad,
        shift_two_grad,
    ) = pull_fifth((grad_out, second_grad))
    hidden_low = hidden_mm_grad.astype(jnp.bfloat16)
    h_weight_grad = jnp.einsum(
        "tv,td->vd", gated_low, hidden_low, preferred_element_type=jnp.float32
    )
    gated_grad = jnp.einsum("td,vd->tv", hidden_low, h_full, preferred_element_type=jnp.float32)
    attended_values_reduced = (
        (gated_grad * reset).astype(jnp.bfloat16).reshape(blocks, STRETCH, VALUE_WIDTH)
    )
    reset_grad = gated_grad * attended_values
    soft_grad = jnp.einsum(
        "uoz,ufz->uof", attended_values_reduced, values_reduced, preferred_element_type=jnp.float32
    )
    values_grad = jnp.einsum(
        "mul,mur->mlr",
        softmax_probs_reduced,
        attended_values_reduced,
        preferred_element_type=jnp.float32,
    ).reshape(sequence_length, VALUE_WIDTH)
    raw_grad, relative_grad = pull_third(soft_grad)
    raw_low = raw_grad.astype(jnp.bfloat16)
    query_grad = jnp.einsum(
        "nqk,nkz->nqz", raw_low, keys_low, preferred_element_type=jnp.float32
    ).reshape(sequence_length, Z)
    keys_grad = jnp.einsum(
        "nqk,nqz->nkz", raw_low, query_low, preferred_element_type=jnp.float32
    ).reshape(sequence_length, Z)
    values_mm_grad, v_bias_grad, base_mm_grad, mx_bias_grad, affine_grad = pull_second(
        (values_grad, update_grad, reset_grad, hidden_x_grad, query_grad, keys_grad)
    )
    base_low = base_mm_grad.astype(jnp.bfloat16)
    mx_weight_grad = jnp.einsum(
        "td,te->de", mixed_low, base_low, preferred_element_type=jnp.float32
    )
    mixed_grad = jnp.einsum("te,de->td", base_low, mx_full, preferred_element_type=jnp.float32)
    values_mm_low = values_mm_grad.astype(jnp.bfloat16)
    v_weight_grad = jnp.einsum(
        "td,tv->dv", normed_low, values_mm_low, preferred_element_type=jnp.float32
    )
    normed_grad = jnp.einsum("tv,dv->td", values_mm_low, v_full, preferred_element_type=jnp.float32)
    row_grad_second, gain_one_grad, shift_one_grad, omega_grad, ema_grad = pull_first(
        (normed_grad, mixed_grad)
    )
    grad_row = (row_grad_first + row_grad_second).astype(jnp.bfloat16)
    small_grad = jnp.concatenate(
        [
            gain_one_grad,
            gain_two_grad,
            shift_one_grad,
            shift_two_grad,
            omega_grad,
            affine_grad.reshape(-1),
            relative_grad,
            v_bias_grad,
            mx_bias_grad,
            h_bias_grad,
            up_bias_grad,
            down_bias_grad,
            ema_grad.reshape(-1),
        ]
    )
    return (
        (
            v_weight_grad,
            mx_weight_grad,
            h_weight_grad,
            up_weight_grad,
            down_weight_grad,
            small_grad,
        ),
        grad_row,
    )


def per_device(
    n, inputs, lengths, cotangent, v_weight, mx_weight, h_weight, up_weight, down_weight, small_params
):
    sequence_length = inputs.shape[2]
    positions = jnp.arange(sequence_length)
    gathered = gather_all(n, (v_weight, mx_weight, h_weight, up_weight, down_weight), small_params)
    totals = None
    results_all = []
    grads_all = []
    for micro in range(inputs.shape[0]):
        member = 0
        valid = (positions < lengths[micro, member]).astype(jnp.float32)[:, None]
        result, kept = forward_rows(inputs[micro, member], valid, gathered)
        results_micro = [result]
        saved = [kept]
        local_grads = None
        member = 0
        member_grads, grad_row = backward_rows(saved[member], cotangent[micro, member], gathered)
        grads_micro = [grad_row]
        local_grads = member_grads
        if totals is None:
            totals = local_grads
        else:
            totals = jax.tree.map(jnp.add, totals, local_grads)
        results_all.append(jnp.stack(results_micro))
        grads_all.append(jnp.stack(grads_micro))
    totals = (
        lax.psum_scatter(totals[0], "fsdp", scatter_dimension=0, tiled=True),
        lax.psum_scatter(totals[1], "fsdp", scatter_dimension=0, tiled=True),
        lax.psum_scatter(totals[2], "fsdp", scatter_dimension=0, tiled=True),
        lax.psum_scatter(totals[3], "fsdp", scatter_dimension=0, tiled=True),
        lax.psum_scatter(totals[4], "fsdp", scatter_dimension=0, tiled=True),
        lax.psum_scatter(totals[5], "fsdp", scatter_dimension=0, tiled=True),
    )
    return (
        jnp.stack(results_all),
        jnp.stack(grads_all),
        totals[0],
        totals[1],
        totals[2],
        totals[3],
        totals[4],
        totals[5],
    )


def solution(mesh):
    return jax.shard_map(
        partial(per_device, mesh.shape["fsdp"]),
        mesh=mesh,
        in_specs=(
            P(None, "fsdp", None, None),
            P(None, "fsdp"),
            P(None, "fsdp", None, None),
            P("fsdp", None),
            P("fsdp", None),
            P("fsdp", None),
            P("fsdp", None),
            P("fsdp", None),
            P("fsdp"),
        ),
        out_specs=(
            P(None, "fsdp", None, None),
            P(None, "fsdp", None, None),
            P("fsdp", None),
            P("fsdp", None),
            P("fsdp", None),
            P("fsdp", None),
            P("fsdp", None),
            P("fsdp"),
        ),
        check_vma=False,
    )
```

```python
import functools
import math

import jax
import jax.numpy as jnp
from jax import lax
from jax.experimental import pallas as pl
from jax.experimental.pallas import tpu as pltpu
from jax.sharding import PartitionSpec as P

D = 1024
Z = 128
VALUE_WIDTH = 2048
H = 16
FF = 4096
STRETCH = 128


epsilon = 1e-05

MESH = pl.DeviceIdType.MESH

class Place:
    def __init__(self, dims):
        self.Z, self.Y, self.X = dims
        me = lax.axis_index("fsdp")
        self.me = me
        self.c = me % 2
        self.x = (me // 2) % self.X
        self.y = (me // (2 * self.X)) % self.Y
        self.z = me // (2 * self.X * self.Y)
        self.nx = self.dev(self.z, self.y, 1 - self.x, self.c)
        self.ny = self.dev(self.z, 1 - self.y, self.x, self.c)
        self.nc = self.dev(self.z, self.y, self.x, 1 - self.c)
        self.has_down = self.z > 0
        self.has_up = self.z < self.Z - 1
        self.down = self.dev(jnp.maximum(self.z - 1, 0), self.y, self.x, self.c)
        self.up = self.dev(jnp.minimum(self.z + 1, self.Z - 1), self.y, self.x, self.c)
    def dev(self, z, y, x, c):
        return ((z * self.Y + y) * self.X + x) * 2 + c
    def barrier(self):
        bar = pltpu.get_barrier_semaphore()
        def tell(d):
            pl.semaphore_signal(bar, inc=1, device_id=(d,), device_id_type=MESH)
        for d in (self.nx, self.ny, self.nc):
            tell(d)
        pl.when(self.has_down)(lambda: tell(self.down))
        pl.when(self.has_up)(lambda: tell(self.up))
        pl.semaphore_wait(bar, 3 + jnp.where(self.has_down, 1, 0) + jnp.where(self.has_up, 1, 0))

def when(cond, f):
    if cond is None: f()
    else: pl.when(cond)(f)

class Gather:
    def __init__(self, place, ins, outs, send_sem, recv_sem):
        self.p, self.ins, self.outs = place, ins, outs
        self.ss, self.rs = send_sem, recv_sem
        self.ids, self.pend = {}, []
    def rows(self, k, h):
        n = self.ins[k].shape[0]
        return (0, n) if h == 2 else (h * (n // 2), n // 2)
    def copy(self, key, k, shard, h, to, own=False):
        i = self.ids.setdefault((key, k), len(self.ids))
        r, n = self.rows(k, h)
        full = self.ins[k].shape[0]
        dst = self.outs[k].at[pl.ds(shard * full + r, n)]
        src = self.ins[k].at[pl.ds(r, n)] if own else dst
        return pltpu.make_async_remote_copy(src_ref=src, dst_ref=dst, send_sem=self.ss.at[i], recv_sem=self.rs.at[i], device_id=(to,), device_id_type=MESH)
    def send(self, cond, *a):
        when(cond, lambda: self.copy(*a).start())
        self.pend.append((cond, lambda: self.copy(*a).wait_send()))
    def recv(self, cond, key, k, shard, h):
        when(cond, lambda: self.copy(key, k, shard, h, self.p.me).wait_recv())
    def col(self, o):
        p = self.p
        if o == 0: return None, p.z
        if o > 0: return p.z - o >= 0, jnp.maximum(p.z - o, 0)
        return p.z - o <= p.Z - 1, jnp.minimum(p.z - o, p.Z - 1)
    def offs(self, s):
        return (0,) if s == 0 else (s, -s)
    def stage(self, k, s):
        p = self.p
        L = p.Z
        if s < L:
            for o in self.offs(s):
                cond, zz = self.col(o)
                sh = p.dev(zz, p.y, p.x, p.c)
                own = o == 0
                if not own:
                    self.recv(cond, ("z", o), k, sh, 2)
                if s + 1 < L:
                    both = lambda c1: c1 if cond is None else jnp.logical_and(cond, c1)
                    if o >= 0: self.send(both(p.has_up), ("z", s + 1), k, sh, 2, p.up, own)
                    if o <= 0: self.send(both(p.has_down), ("z", -(s + 1)), k, sh, 2, p.down, own)
                self.send(cond, ("x", o), k, sh, 2, p.nx, own)
                self.send(cond, ("y", o), k, sh, 2, p.ny, own)
                self.send(cond, ("c", o), k, sh, 2, p.nc, own)
        if 1 <= s <= L:
            for o in self.offs(s - 1):
                cond, zz = self.col(o)
                sx, sy = p.dev(zz, p.y, 1 - p.x, p.c), p.dev(zz, 1 - p.y, p.x, p.c)
                self.recv(cond, ("x", o), k, sx, 2)
                self.send(cond, ("xy", o), k, sx, 0, p.ny)
                self.send(cond, ("cx", o), k, sx, 2, p.nc)
                self.recv(cond, ("y", o), k, sy, 2)
                self.send(cond, ("yx", o), k, sy, 1, p.nx)
                self.send(cond, ("cy", o), k, sy, 2, p.nc)
        if 2 <= s <= L + 1:
            for o in self.offs(s - 2):
                cond, zz = self.col(o)
                sd = p.dev(zz, 1 - p.y, 1 - p.x, p.c)
                self.recv(cond, ("xy", o), k, sd, 0)
                self.recv(cond, ("yx", o), k, sd, 1)
                self.send(cond, ("cd", o), k, sd, 2, p.nc)
        if s == L + 2:
            for t in range(L):
                for o in self.offs(t):
                    cond, zz = self.col(o)
                    for key, yy, xx in (("c", p.y, p.x), ("cx", p.y, 1 - p.x), ("cy", 1 - p.y, p.x), ("cd", 1 - p.y, 1 - p.x)):
                        self.recv(cond, (key, o), k, p.dev(zz, yy, xx, 1 - p.c), 2)
    def stages(self):
        return self.p.Z + 3
    def finish(self):
        for cond, f in self.pend:
            when(cond, f)

def sems_needed(dims, K):
    Z = dims[0]
    offs = 2 * Z - 1
    return K * (2 * (Z - 1) + 8 * offs)

def ag_kernel(dims, K, *refs):
    ins, outs = refs[:K], refs[K:2 * K]
    own, ss, rs = refs[2 * K:]
    p = Place(dims)
    p.barrier()
    g = Gather(p, ins, outs, ss, rs)
    cps = [pltpu.make_async_copy(ins[k], outs[k].at[pl.ds(p.me * ins[k].shape[0], ins[k].shape[0])], own.at[k]) for k in range(K)]
    for cp in cps: cp.start()
    S = g.stages()
    for t in range(K + S - 1):
        for k in range(K):
            if 0 <= t - k < S: g.stage(k, t - k)
    g.finish()
    for cp in cps: cp.wait()

def gather(dims, n, arrays, cid):
    K = len(arrays)
    ns = sems_needed(dims, K)
    return pl.pallas_call(functools.partial(ag_kernel, dims, K),
        out_shape=[jax.ShapeDtypeStruct((n * a.shape[0],) + a.shape[1:], a.dtype) for a in arrays],
        in_specs=[pl.BlockSpec(memory_space=pl.ANY)] * K, out_specs=[pl.BlockSpec(memory_space=pl.ANY)] * K,
        scratch_shapes=[pltpu.SemaphoreType.DMA((K,)), pltpu.SemaphoreType.DMA((ns,)), pltpu.SemaphoreType.DMA((ns,))],
        compiler_params=pltpu.CompilerParams(collective_id=cid, has_side_effects=True))(*arrays)


F32, BF16 = jnp.float32, jnp.bfloat16
TILE = 256
O_GAIN, O_SHIFT, O_OMEGA, O_AFF, O_REL = 0, 2 * D, 4 * D, 5 * D, 5 * D + 4 * Z
O_VB = O_REL + STRETCH
O_MXB = O_VB + VALUE_WIDTH
MXW = 2 * D + Z + VALUE_WIDTH
O_HB = O_MXB + MXW
O_UPB = O_HB + D
O_DNB = O_UPB + FF
O_EMA = O_DNB + D
C_LAT, C_RES, C_HX = D, D + Z, D + Z + VALUE_WIDTH


def sigmoid(v):
    return 0.5 * jnp.tanh(0.5 * v) + 0.5


def silu_slope(v, s):
    return s * (1.0 + v * (1.0 - s))


def col_sum(v):
    return jnp.sum(v, axis=0, keepdims=True)


def dot(a, b, ca=1, cb=0):
    return lax.dot_general(a, b, (((ca,), (cb,)), ((), ())), preferred_element_type=F32)


def tiles(lo, hi, step, f):
    @pl.loop(0, (hi - lo) // step)
    def _(i):
        f(pl.multiple_of(lo + i * step, 128))


def lane_block(l):
    return pl.ds(pl.multiple_of(l * 128, 128), 128)


def center(xf):
    c = xf - jnp.mean(xf, axis=-1, keepdims=True)
    r = lax.rsqrt(jnp.mean(c * c, axis=-1, keepdims=True) + epsilon)
    return c * r, r


def ema_rates(ema):
    gate, a = sigmoid(ema[0]), sigmoid(ema[1])
    retain = 1.0 - gate * a
    weight = gate * ema[2] * ema[3] * (1.0 / math.sqrt(H))
    return gate, a, retain, weight


def rel_table(rel_row):
    wide = jnp.broadcast_to(rel_row, (STRETCH, STRETCH))
    return pltpu.roll(wide, 0, 1, stride=1, stride_axis=0)


def causal():
    i = lax.broadcasted_iota(jnp.int32, (STRETCH, STRETCH), 0)
    j = lax.broadcasted_iota(jnp.int32, (STRETCH, STRETCH), 1)
    return j <= i


class Forward:
    def __init__(self, x, valid, prow, ema, rel, w, s):
        self.x, self.valid, self.prow, self.ema, self.rel, self.w, self.s = x, valid, prow, ema, rel, w, s
        self.m = x.shape[0]
        self.seqs = self.m // STRETCH

    def p(self, lo, n):
        return self.prow[:, lo : lo + n]

    def pd(self, lo, col, n):
        return self.prow[:, pl.ds(pl.multiple_of(lo + col, 128), n)]

    def norm_one(self):
        s = self.s
        g, b = self.p(O_GAIN, D), self.p(O_SHIFT, D)
        for q in range(self.seqs):
            s.mpad[q, 0:8, :] = jnp.zeros((8, D), F32)

            @pl.loop(0, STRETCH // 32)
            def _(i):
                r = pl.ds(q * STRETCH + i * 32, 32)
                xhat, _ = center(self.x[r, :].astype(F32))
                n = xhat * g + b
                s.normed[r, :] = n.astype(BF16)
                s.mpad[q, pl.ds(8 + i * 32, 32), :] = n * self.valid[r, 0:1]

    def ema_kernel(self):
        _, _, retain, weight = ema_rates(self.ema)

        def step(j, p):
            self.s.kern[pl.ds(j, 1), :] = col_sum(p)
            return p * retain

        lax.fori_loop(0, STRETCH, step, weight)

    def smooth(self):
        s = self.s
        omega = self.p(O_OMEGA, D)
        for q in range(self.seqs):

            @pl.loop(0, D // 128)
            def _(l):
                lb = lane_block(l)
                om = self.prow[:, pl.ds(pl.multiple_of(O_OMEGA + l * 128, 128), 128)]
                nb = STRETCH // 8
                acc = [om * s.mpad[q, 8 + 8 * i : 16 + 8 * i, lb] for i in range(nb)]
                for b in range(8):
                    sh = [s.mpad[q, 8 - b + 8 * i : 16 - b + 8 * i, lb] for i in range(nb)]
                    for a in range(nb):
                        kb = jnp.broadcast_to(s.kern[8 * a + b : 8 * a + b + 1, lb], (8, 128))
                        for i in range(a, nb):
                            acc[i] = acc[i] + kb * sh[i - a]
                for i in range(nb):
                    r = slice(q * STRETCH + 8 * i, q * STRETCH + 8 * i + 8)
                    s.e[r, lb] = acc[i]

    def mix(self):
        s = self.s

        @pl.loop(0, self.m // 32)
        def _(i):
            r = pl.ds(i * 32, 32)
            e = s.e[r, :]
            s.mixed[r, :] = (e * sigmoid(e)).astype(BF16)

    def values(self):
        s = self.s

        def one(col):
            cols = pl.ds(col, TILE)
            v = dot(s.normed[...], self.w.v[:, cols]) + self.pd(O_VB, col, TILE)
            s.vpre[:, cols] = v
            s.val[:, cols] = (v * sigmoid(v)).astype(BF16)

        tiles(0, VALUE_WIDTH, TILE, one)

    def base(self):
        s = self.s

        def one(width):
            def f(col):
                cols = pl.ds(col, width)
                s.base[:, cols] = dot(s.mixed[...], self.w.mx[:, cols]) + self.pd(O_MXB, col, width)

            return f

        tiles(0, D, TILE, one(TILE))
        tiles(C_LAT, C_RES, Z, one(Z))
        tiles(C_RES, MXW, TILE, one(TILE))

    def attend(self):
        s = self.s
        table, mask = rel_table(self.rel[...]), causal()
        for q in range(self.seqs):
            r = slice(q * STRETCH, (q + 1) * STRETCH)
            b = s.base[r, C_LAT:C_RES]
            lat = b * sigmoid(b)
            query = (lat * (1.0 + self.p(O_AFF, Z)) + self.p(O_AFF + 2 * Z, Z)).astype(BF16)
            keys = (lat * (1.0 + self.p(O_AFF + Z, Z)) + self.p(O_AFF + 3 * Z, Z)).astype(BF16)
            sc = jnp.where(mask, dot(query, keys, 1, 1) * (1.0 / math.sqrt(Z)) + table, -1e30)
            ex = jnp.exp(sc - jnp.max(sc, axis=-1, keepdims=True))
            pr = ex / jnp.sum(ex, axis=-1, keepdims=True)
            s.probs[r, :] = pr
            s.query[r, :] = query
            s.keys[r, :] = keys
            low = pr.astype(BF16)

            def one(col):
                cols = pl.ds(col, TILE)
                at = dot(low, s.val[r, cols])
                s.att[r, cols] = at
                bb = s.base[r, pl.ds(pl.multiple_of(C_RES + col, 128), TILE)]
                s.gated[r, cols] = (at * (bb * sigmoid(bb))).astype(BF16)

            tiles(0, VALUE_WIDTH, TILE, one)

    def hidden(self):
        s = self.s

        def one(col):
            cols = pl.ds(col, TILE)
            h = dot(s.gated[...], self.w.h[:, cols]) + self.pd(O_HB, col, TILE)
            h = h + s.base[:, pl.ds(pl.multiple_of(C_HX + col, 128), TILE)]
            s.hpre[:, cols] = h
            xf = self.x[:, cols].astype(F32)
            u = sigmoid(s.base[:, cols])
            s.first[:, cols] = xf + self.valid[:, 0:1] * u * (h * sigmoid(h) - xf)

        tiles(0, D, TILE, one)

    def norm_two(self):
        s = self.s
        g, b = self.p(O_GAIN + D, D), self.p(O_SHIFT + D, D)

        @pl.loop(0, self.m // 32)
        def _(i):
            r = pl.ds(i * 32, 32)
            xhat, _ = center(s.first[r, :])
            s.second[r, :] = (xhat * g + b).astype(BF16)

    def up(self):
        s = self.s

        def one(col):
            cols = pl.ds(col, TILE)
            u = dot(s.second[...], self.w.up[:, cols]) + self.pd(O_UPB, col, TILE)
            s.upre[:, cols] = u
            s.inner[:, cols] = (u * sigmoid(u)).astype(BF16)

        tiles(0, FF, TILE, one)

    def down(self, out):
        s = self.s

        def one(col):
            cols = pl.ds(col, TILE)
            d = dot(s.inner[...], self.w.down[:, cols]) + self.pd(O_DNB, col, TILE)
            out[:, cols] = (s.first[:, cols] + self.valid[:, 0:1] * d).astype(BF16)

        tiles(0, D, TILE, one)


class Backward:
    def __init__(self, x, g, valid, prow, ema, rel, w, s, t, grow, gema):
        self.x, self.g, self.valid, self.prow, self.ema, self.rel = x, g, valid, prow, ema, rel
        self.w, self.s, self.t, self.grow, self.gema = w, s, t, grow, gema
        self.m = x.shape[0]
        self.seqs = self.m // STRETCH

    p, pd = Forward.p, Forward.pd

    def put(self, lo, col, n, v):
        self.grow[:, pl.ds(pl.multiple_of(lo + col, 128), n)] = v

    def cot(self):
        def one(col):
            cols = pl.ds(col, TILE)
            d = self.valid[:, 0:1] * self.g[:, cols].astype(F32)
            self.put(O_DNB, col, TILE, col_sum(d))
            self.t.dd[:, cols] = d.astype(BF16)

        tiles(0, D, TILE, one)

    def d_up(self):
        s, t = self.s, self.t

        def one(col):
            cols = pl.ds(col, TILE)
            di = dot(t.dd[...], self.w.down[cols, :], 1, 1)
            u = s.upre[:, cols]
            du = di * silu_slope(u, sigmoid(u))
            self.put(O_UPB, col, TILE, col_sum(du))
            t.dup[:, cols] = du.astype(BF16)

        tiles(0, FF, TILE, one)

    def d_second(self):
        t = self.t

        def one(col):
            cols = pl.ds(col, TILE)
            t.dsec[:, cols] = dot(t.dup[...], self.w.up[cols, :], 1, 1)

        tiles(0, D, TILE, one)

    def norm_two(self):
        s, t = self.s, self.t
        g = self.p(O_GAIN + D, D)
        t.acc[...] = jnp.zeros(t.acc.shape, F32)

        def add(k, v):
            t.acc[k] += jnp.sum(v.reshape(v.shape[0] // 8, 8, D), axis=0)

        @pl.loop(0, self.m // 32)
        def _(i):
            r = pl.ds(i * 32, 32)
            xhat, rstd = center(s.first[r, :])
            ds = t.dsec[r, :]
            add(0, ds * xhat)
            add(1, ds)
            dh = ds * g
            dn = rstd * (dh - jnp.mean(dh, axis=-1, keepdims=True) - xhat * jnp.mean(dh * xhat, axis=-1, keepdims=True))
            df = self.g[r, :].astype(F32) + dn
            v = self.valid[r, 0:1]
            u = sigmoid(s.base[r, 0:D])
            hp = s.hpre[r, :]
            sh = sigmoid(hp)
            xf = self.x[r, :].astype(F32)
            vu = v * u
            t.dx[r, :] = df - df * vu
            db = df * v * (hp * sh - xf) * u * (1.0 - u)
            add(2, db)
            t.dbase[r, 0:D] = db.astype(BF16)
            dhp = df * vu * silu_slope(hp, sh)
            add(3, dhp)
            t.dbase[r, C_HX:MXW] = dhp.astype(BF16)

        for k, lo in enumerate((O_GAIN + D, O_SHIFT + D, O_MXB, O_HB)):
            self.grow[:, lo : lo + D] = col_sum(t.acc[k])
        self.grow[:, O_MXB + C_HX : O_MXB + MXW] = col_sum(t.acc[3])

    def d_gated(self):
        s, t = self.s, self.t

        def one(col):
            cols = pl.ds(col, TILE)
            bcols = pl.ds(pl.multiple_of(C_RES + col, 128), TILE)
            dg = dot(t.dbase[:, C_HX:MXW], self.w.h[cols, :], 1, 1)
            b = s.base[:, bcols]
            sb = sigmoid(b)
            t.datt[:, cols] = (dg * (b * sb)).astype(BF16)
            db = dg * s.att[:, cols] * silu_slope(b, sb)
            self.put(O_MXB + C_RES, col, TILE, col_sum(db))
            t.dbase[:, bcols] = db.astype(BF16)

        tiles(0, VALUE_WIDTH, TILE, one)

    def attend(self):
        s, t = self.s, self.t
        mask = causal()
        lows, drel = [], None
        aff = [0.0, 0.0, 0.0, 0.0]
        lat_bias = 0.0
        for q in range(self.seqs):
            r = slice(q * STRETCH, (q + 1) * STRETCH)
            pr = s.probs[r, :]
            lows.append(pr.astype(BF16))
            dp = dot(t.datt[r, :], s.val[r, :], 1, 1)
            ds = pr * (dp - jnp.sum(pr * dp, axis=-1, keepdims=True))
            ds = jnp.where(mask, ds, 0.0)
            drel = ds if drel is None else drel + ds
            raw = (ds * (1.0 / math.sqrt(Z))).astype(BF16)
            dq = dot(raw, s.keys[r, :])
            dk = dot(raw, s.query[r, :], 0, 0)
            b = s.base[r, C_LAT:C_RES]
            sb = sigmoid(b)
            lat = b * sb
            for k, v in enumerate((dq * lat, dk * lat, dq, dk)):
                aff[k] = aff[k] + col_sum(v)
            dl = dq * (1.0 + self.p(O_AFF, Z)) + dk * (1.0 + self.p(O_AFF + Z, Z))
            db = dl * silu_slope(b, sb)
            lat_bias = lat_bias + col_sum(db)
            t.dbase[r, C_LAT:C_RES] = db.astype(BF16)
        for k in range(4):
            self.grow[:, O_AFF + k * Z : O_AFF + (k + 1) * Z] = aff[k]
        self.grow[:, O_MXB + C_LAT : O_MXB + C_RES] = lat_bias
        eight = 0.0
        for i in range(0, STRETCH, 8):
            eight = eight + pltpu.roll(drel[i : i + 8, :], (STRETCH - i) % STRETCH, 1)
        back = 0.0
        for i in range(8):
            back = back + pltpu.roll(eight[i : i + 1, :], (STRETCH - i) % STRETCH, 1)
        self.grow[:, O_REL : O_REL + STRETCH] = back

        def one(col):
            cols = pl.ds(col, TILE)
            bias = 0.0
            for q in range(self.seqs):
                r = slice(q * STRETCH, (q + 1) * STRETCH)
                dv = dot(lows[q], t.datt[r, cols], 0, 0)
                v = s.vpre[r, cols]
                dv = dv * silu_slope(v, sigmoid(v))
                bias = bias + col_sum(dv)
                t.dv[r, cols] = dv.astype(BF16)
            self.put(O_VB, col, TILE, bias)

        tiles(0, VALUE_WIDTH, TILE, one)

    def d_mixed(self):
        s, t = self.s, self.t
        for q in range(self.seqs):
            t.dpad[q, STRETCH : STRETCH + 8, :] = jnp.zeros((8, D), F32)

        def one(col):
            cols = pl.ds(col, TILE)
            dm = dot(t.dbase[...], self.w.mx[cols, :], 1, 1)
            e = s.e[:, cols]
            de = dm * silu_slope(e, sigmoid(e))
            om = 0.0
            for q in range(self.seqs):
                d = de[q * STRETCH : (q + 1) * STRETCH, :]
                t.dpad[q, 0:STRETCH, cols] = d
                om = om + col_sum(d * s.mpad[q, 8 : 8 + STRETCH, cols])
            self.put(O_OMEGA, col, TILE, om)

        tiles(0, D, TILE, one)

    def d_normed(self):
        t = self.t

        def one(col):
            cols = pl.ds(col, TILE)
            t.dn[:, cols] = dot(t.dv[...], self.w.v[cols, :], 1, 1)

        tiles(0, D, TILE, one)

    def smooth(self):
        s, t = self.s, self.t
        nb = STRETCH // 8

        @pl.loop(0, D // 128)
        def _(l):
            lb = lane_block(l)
            om = self.prow[:, pl.ds(pl.multiple_of(O_OMEGA + l * 128, 128), 128)]
            for q in range(self.seqs):
                acc = [om * t.dpad[q, 8 * i : 8 * i + 8, lb] for i in range(nb)]
                for b in range(8):
                    sh = [t.dpad[q, 8 * i + b : 8 * i + b + 8, lb] for i in range(nb)]
                    for a in range(nb):
                        kb = jnp.broadcast_to(s.kern[8 * a + b : 8 * a + b + 1, lb], (8, 128))
                        for i in range(nb - a):
                            acc[i] = acc[i] + kb * sh[i + a]
                for i in range(nb):
                    r = slice(q * STRETCH + 8 * i, q * STRETCH + 8 * i + 8)
                    t.dn[r, lb] = t.dn[r, lb] + self.valid[r, :] * acc[i]

        @pl.loop(0, D // 128)
        def _(l):
            lb = lane_block(l)
            for b in range(8):
                sums = [None] * nb
                for q in range(self.seqs):
                    de = [t.dpad[q, 8 * i : 8 * i + 8, lb] for i in range(nb)]
                    sh = [s.mpad[q, 8 - b + 8 * i : 16 - b + 8 * i, lb] for i in range(nb)]
                    for a in range(nb):
                        for i in range(a, nb):
                            v = de[i] * sh[i - a]
                            sums[a] = v if sums[a] is None else sums[a] + v
                for a in range(nb):
                    t.dkern[8 * a + b : 8 * a + b + 1, lb] = col_sum(sums[a])

    def norm_one(self, out):
        t = self.t
        g = self.p(O_GAIN, D)
        t.acc[...] = jnp.zeros(t.acc.shape, F32)

        def add(k, v):
            t.acc[k] += jnp.sum(v.reshape(v.shape[0] // 8, 8, D), axis=0)

        @pl.loop(0, self.m // 32)
        def _(i):
            r = pl.ds(i * 32, 32)
            xhat, rstd = center(self.x[r, :].astype(F32))
            dn = t.dn[r, :]
            add(0, dn * xhat)
            add(1, dn)
            dh = dn * g
            d = rstd * (dh - jnp.mean(dh, axis=-1, keepdims=True) - xhat * jnp.mean(dh * xhat, axis=-1, keepdims=True))
            out[r, :] = (t.dx[r, :] + d).astype(BF16)

        for k, lo in enumerate((O_GAIN, O_SHIFT)):
            self.grow[:, lo : lo + D] = col_sum(t.acc[k])


    def ema_grads(self):
        t = self.t
        gate, a, retain, weight = ema_rates(self.ema)
        zero = retain - retain

        def step(j, carry):
            power, before, dw, dr = carry
            row = t.dkern[pl.ds(j, 1), :]
            dw = dw + row * power
            dr = dr + (row * j.astype(F32)) * before
            return power * retain, power, dw, dr

        _, _, dw, dr = lax.fori_loop(0, STRETCH, step, (zero + 1.0, zero, zero, zero))
        drate = -dr * weight
        scale = 1.0 / math.sqrt(H)
        dgate = drate * a + dw * self.ema[2] * self.ema[3] * scale
        self.gema[0] = dgate * gate * (1.0 - gate)
        self.gema[1] = drate * gate * a * (1.0 - a)
        self.gema[2] = dw * gate * self.ema[3] * scale
        self.gema[3] = dw * gate * self.ema[2] * scale


class Scatter:
    def __init__(self, place, grads, bufs, outs, send_sem, recv_sem, local_sem):
        self.p, self.grads, self.bufs, self.outs = place, grads, bufs, outs
        self.ss, self.rs, self.ls = send_sem, recv_sem, local_sem
        self.ids, self.pend = {}, []

    def copy(self, key, k, src, dst, to):
        i = self.ids.setdefault((key, k), len(self.ids))
        return pltpu.make_async_remote_copy(src_ref=src, dst_ref=dst, send_sem=self.ss.at[i], recv_sem=self.rs.at[i], device_id=(to,), device_id_type=MESH)

    def send(self, cond, key, k, src, dst, to):
        when(cond, lambda: self.copy(key, k, src, dst, to).start())
        self.pend.append((cond, lambda: self.copy(key, k, src, dst, to).wait_send()))

    def recv(self, cond, key, k, dst):
        when(cond, lambda: self.copy(key, k, dst, dst, self.p.me).wait_recv())

    def own(self, k, z):
        p, b = self.p, self.bufs[k]
        layer = p.Y * p.X
        i = k * p.Z + z
        return pltpu.make_async_copy(self.grads[k].at[pl.ds(z * layer, layer), p.c], b.mine.at[pl.ds(z * layer, layer)], self.ls.at[i])

    def add(self, dst, a, b, r0=0, rows=None):
        n = rows

        @pl.loop(0, n // 16)
        def _(i):
            def at(v, r):
                ref, q, off = v
                return ref.at[q, pl.ds(pl.multiple_of(off + r, 16), 16)]

            r = i * 16
            at(dst, r)[...] = at(a, r)[...] + at(b, r)[...]

    def stage(self, k, s):
        p, b = self.p, self.bufs[k]
        layer = p.Y * p.X
        r = b.sum.shape[1]
        half = r // 2
        chip = lambda z, y, x: (z * p.Y + y) * p.X + x
        col = lambda z: (chip(z, p.y, p.x), chip(z, p.y, 1 - p.x), chip(z, 1 - p.y, p.x), chip(z, 1 - p.y, 1 - p.x))
        order = list(range(p.Z))
        if s == 0:
            for z in order:
                self.send(None, ("c", z), k, self.grads[k].at[pl.ds(z * layer, layer), 1 - p.c], b.sum.at[pl.ds(z * layer, layer)], p.nc)
                self.own(k, z).start()
        if s == 1:
            for z in order:
                self.recv(None, ("c", z), k, b.sum.at[pl.ds(z * layer, layer)])
                self.own(k, z).wait()
                me, nx, ny, nd = col(z)
                self.add((b.sum, nd, 0), (b.sum, nd, 0), (b.mine, nd, 0), rows=r)
                self.send(None, ("dx", z), k, b.sum.at[nd, pl.ds(0, half)], b.dx.at[z], p.nx)
                self.send(None, ("dy", z), k, b.sum.at[nd, pl.ds(half, half)], b.dy.at[z], p.ny)
                for q in (nx, ny, me):
                    self.add((b.sum, q, 0), (b.sum, q, 0), (b.mine, q, 0), rows=r)
        if s == 2:
            for z in order:
                me, nx, ny, nd = col(z)
                self.recv(None, ("dx", z), k, b.dx.at[z])
                self.add((b.sum, ny, 0), (b.sum, ny, 0), (b.dx, z, 0), rows=half)
                self.send(None, ("y", z), k, b.sum.at[ny], b.ry.at[z], p.ny)
                self.recv(None, ("dy", z), k, b.dy.at[z])
                self.add((b.sum, nx, half), (b.sum, nx, half), (b.dy, z, 0), rows=half)
                self.send(None, ("x", z), k, b.sum.at[nx], b.rx.at[z], p.nx)
        if s == 3:
            for z in order:
                me = col(z)[0]
                self.recv(None, ("y", z), k, b.ry.at[z])
                self.add((b.sum, me, 0), (b.sum, me, 0), (b.ry, z, 0), rows=r)
                self.recv(None, ("x", z), k, b.rx.at[z])
                self.add((b.sum, me, 0), (b.sum, me, 0), (b.rx, z, 0), rows=r)
        if s == 4:
            for d in range(1, p.Z):
                for up in (True, False):
                    t = p.Z - d if up else d - 1
                    buf, key = (b.ru, "u") if up else (b.rd, "d")
                    q = chip(t, p.y, p.x)
                    passing = p.z < t if up else p.z > t
                    fed = p.has_down if up else p.has_up

                    def relay(q=q, t=t, buf=buf, key=key):
                        self.copy((key, t), k, buf.at[t], buf.at[t], p.me).wait_recv()
                        self.add((b.sum, q, 0), (b.sum, q, 0), (buf, t, 0), rows=r)

                    pl.when(jnp.logical_and(passing, fed))(relay)
                    self.send(passing, (key, t), k, b.sum.at[q], buf.at[t], p.up if up else p.down)
        if s == 5:
            for cond, buf, key in ((None, None, None), (p.has_down, b.ru, "u"), (p.has_up, b.rd, "d")):
                me = chip(p.z, p.y, p.x)
                out = self.outs[k]
                if buf is None:
                    @pl.loop(0, r // 16)
                    def _(i):
                        rr = pl.ds(pl.multiple_of(i * 16, 16), 16)
                        out[rr, :] = b.sum[me, rr, :].astype(F32)
                    continue

                for t in range(p.Z):
                    def last(buf=buf, key=key, out=out, t=t):
                        self.copy((key, t), k, buf.at[t], buf.at[t], p.me).wait_recv()

                        @pl.loop(0, r // 16)
                        def _(i):
                            rr = pl.ds(pl.multiple_of(i * 16, 16), 16)
                            out[rr, :] += buf[t, rr, :].astype(F32)

                    if (key == "u" and t == 0) or (key == "d" and t == p.Z - 1):
                        continue
                    pl.when(jnp.logical_and(cond, p.z == t))(last)

    def stages(self):
        return 6

    def finish(self):
        for cond, f in self.pend:
            when(cond, f)


class Names:
    def __init__(self, **kw):
        self.__dict__.update(kw)


SCATTER_BUFS = ("mine", "sum", "dx", "dy", "rx", "ry", "ru", "rd")


def scatter_scratch(dims, r, w):
    Z, Y, X = dims
    chips = Z * Y * X
    shapes = ((chips, r, w), (chips, r, w), (Z, r // 2, w), (Z, r // 2, w), (Z, r, w), (Z, r, w), (Z, r, w), (Z, r, w))
    return [pltpu.VMEM(s, BF16) for s in shapes]


def scatter_sems(dims, K):
    Z = dims[0]
    return K * (5 * Z + 2 * (Z - 1))


def rs_kernel(dims, K, *refs):
    grads, outs = refs[:K], refs[K : 2 * K]
    nb = len(SCATTER_BUFS)
    bufs = [Names(**dict(zip(SCATTER_BUFS, refs[2 * K + nb * k : 2 * K + nb * (k + 1)]))) for k in range(K)]
    ss, rs, ls = refs[2 * K + nb * K :]
    p = Place(dims)
    p.barrier()
    sc = Scatter(p, grads, bufs, outs, ss, rs, ls)
    S = sc.stages()
    for t in range(K + S - 1):
        for k in range(K):
            if 0 <= t - k < S:
                sc.stage(k, t - k)
    sc.finish()


def scatter(dims, grads, cid):
    K = len(grads)
    n = 2 * dims[0] * dims[1] * dims[2]
    shaped = [g.reshape(n // 2, 2, g.shape[0] // n, g.shape[1]) for g in grads]
    scratch = []
    for g in shaped:
        scratch += scatter_scratch(dims, g.shape[2], g.shape[3])
    ns = scatter_sems(dims, K)
    return pl.pallas_call(
        functools.partial(rs_kernel, dims, K),
        out_shape=[jax.ShapeDtypeStruct(g.shape[2:], F32) for g in shaped],
        in_specs=[pl.BlockSpec(memory_space=pl.ANY)] * K,
        out_specs=[pl.BlockSpec(memory_space=pltpu.VMEM)] * K,
        scratch_shapes=scratch + [pltpu.SemaphoreType.DMA((ns,)), pltpu.SemaphoreType.DMA((ns,)), pltpu.SemaphoreType.DMA((K * dims[0],))],
        compiler_params=pltpu.CompilerParams(collective_id=cid, has_side_effects=True, vmem_limit_bytes=64 * 1024 * 1024),
    )(*shaped)


KEPT = ("normed", "mpad", "e", "mixed", "kern", "vpre", "val", "base", "probs", "query", "keys", "att", "gated", "hpre", "first", "second", "upre", "inner")


def kept_shapes(m):
    seqs = m // STRETCH
    f, b = (lambda *s: (s, F32)), (lambda *s: (s, BF16))
    return dict(
        normed=b(m, D), mpad=f(seqs, STRETCH + 8, D), e=f(m, D), mixed=b(m, D), kern=f(STRETCH, D),
        vpre=f(m, VALUE_WIDTH), val=b(m, VALUE_WIDTH), base=f(m, MXW), probs=f(m, STRETCH),
        query=b(m, Z), keys=b(m, Z), att=f(m, VALUE_WIDTH), gated=b(m, VALUE_WIDTH), hpre=f(m, D),
        first=f(m, D), second=b(m, D), upre=f(m, FF), inner=b(m, FF),
    )


VM = pltpu.VMEM
LIMIT = 64 * 1024 * 1024


def fwd_kernel(x, valid, prow, ema, rel, v, mx, h, up, down, *refs):
    nk = len(KEPT)
    out, kept = refs[0], refs[1 : 1 + nk]
    wv, wmx, wh, wup, wdown, sem = refs[1 + nk :]
    s = Names(**dict(zip(KEPT, kept)))
    loads = [pltpu.make_async_copy(a, b, sem.at[i]) for i, (a, b) in enumerate(((v, wv), (mx, wmx), (h, wh), (up, wup), (down, wdown)))]
    for c in loads:
        c.start()
    f = Forward(x, valid, prow, ema, rel, Names(v=wv, mx=wmx, h=wh, up=wup, down=wdown), s)
    f.norm_one()
    f.ema_kernel()
    f.smooth()
    f.mix()
    loads[0].wait()
    f.values()
    loads[1].wait()
    f.base()
    f.attend()
    loads[2].wait()
    f.hidden()
    f.norm_two()
    loads[3].wait()
    f.up()
    loads[4].wait()
    f.down(out)


def forward(x, valid, prow, ema, rel, weights):
    m = x.shape[0]
    ks = kept_shapes(m)
    outs = [jax.ShapeDtypeStruct((m, D), BF16)] + [jax.ShapeDtypeStruct(*ks[k]) for k in KEPT]
    vm, hbm = pl.BlockSpec(memory_space=VM), pl.BlockSpec(memory_space=pl.ANY)
    res = pl.pallas_call(
        fwd_kernel,
        out_shape=outs,
        in_specs=[vm] * 5 + [hbm] * 5,
        out_specs=[vm] * len(outs),
        scratch_shapes=[VM(w.shape, BF16) for w in weights] + [pltpu.SemaphoreType.DMA((5,))],
        compiler_params=pltpu.CompilerParams(vmem_limit_bytes=LIMIT),
    )(x, valid, prow, ema, rel, *weights)
    return res[0], res[1:]


def weight_grad(a, b, n, out, stage, sem, lo=0):
    count = out.shape[0] // TILE

    def copy(i, slot):
        return pltpu.make_async_copy(stage.at[slot, :, 0:n], out.at[pl.ds(pl.multiple_of(i * TILE, TILE), TILE)], sem.at[slot])

    @pl.loop(0, count // 2)
    def _(j):
        for slot in range(2):
            i = j * 2 + slot

            @pl.when(j > 0)
            def _():
                copy(i - 2, slot).wait()

            rows = a[:, pl.ds(pl.multiple_of(i * TILE, TILE), TILE)]
            for c in range(0, n, 1024):
                wd = min(1024, n - c)
                stage[slot, :, c : c + wd] = dot(rows, b[:, lo + c : lo + c + wd], 0, 0).astype(BF16)
            copy(i, slot).start()

    for slot in range(2):
        copy(count - 2 + slot, slot).wait()


def own_shapes(m):
    seqs = m // STRETCH
    return dict(
        dd=((m, D), BF16), dup=((m, FF), BF16), dsec=((m, D), F32), acc=((4, 8, D), F32), dx=((m, D), F32),
        dbase=((m, MXW), BF16), datt=((m, VALUE_WIDTH), BF16), dv=((m, VALUE_WIDTH), BF16),
        dpad=((seqs, STRETCH + 8, D), F32), dn=((m, D), F32), dkern=((STRETCH, D), F32),
    )


def bwd_kernel(x, g, valid, prow, ema, rel, *refs):
    nk = len(KEPT)
    s = Names(**dict(zip(KEPT, refs[:nk])))
    v, mx, h, up, down = refs[nk : nk + 5]
    refs = refs[nk + 5 :]
    dxo, grow, gema, gv, gmx, gh, gup, gdown = refs[:8]
    own = own_shapes(x.shape[0])
    t = Names(**dict(zip(own, refs[8 : 8 + len(own)])))
    wr, wc, wv, stage, wsem, ssem = refs[8 + len(own) :]
    cp = pltpu.make_async_copy
    l_down = cp(down, wr, wsem.at[0])
    l_up = cp(up, wc.at[:, 0:FF], wsem.at[1])
    l_v = cp(v, wv, wsem.at[2])
    l_h = cp(h, wr.at[0:VALUE_WIDTH], wsem.at[3])
    l_mx = cp(mx, wc, wsem.at[4])
    l_down.start()
    l_up.start()
    l_v.start()
    w = Names(v=wv, mx=wc, h=wr, up=wc.at[:, 0:FF], down=wr)
    b = Backward(x, g, valid, prow, ema, rel, w, s, t, grow, gema)
    b.cot()
    weight_grad(s.inner, t.dd, D, gdown, stage, ssem)
    l_down.wait()
    b.d_up()
    l_h.start()
    weight_grad(s.second, t.dup, FF, gup, stage, ssem)
    l_up.wait()
    b.d_second()
    l_mx.start()
    b.norm_two()
    weight_grad(s.gated, t.dbase, D, gh, stage, ssem, lo=C_HX)
    l_h.wait()
    b.d_gated()
    b.attend()
    weight_grad(s.mixed, t.dbase, MXW, gmx, stage, ssem)
    weight_grad(s.normed, t.dv, VALUE_WIDTH, gv, stage, ssem)
    l_mx.wait()
    b.d_mixed()
    l_v.wait()
    b.d_normed()
    b.smooth()
    b.norm_one(dxo)
    b.ema_grads()


def backward(x, g, valid, prow, ema, rel, kept, weights):
    m = x.shape[0]
    own = own_shapes(m)
    vm, hbm = pl.BlockSpec(memory_space=VM), pl.BlockSpec(memory_space=pl.ANY)
    outs = [jax.ShapeDtypeStruct((m, D), BF16), jax.ShapeDtypeStruct((1, O_EMA), F32), jax.ShapeDtypeStruct(ema.shape, F32)]
    outs += [jax.ShapeDtypeStruct(w.shape, BF16) for w in weights]
    scratch = [VM(*v) for v in own.values()]
    scratch += [VM((FF, D), BF16), VM((D, MXW), BF16), VM((D, VALUE_WIDTH), BF16), VM((2, TILE, MXW), BF16)]
    scratch += [pltpu.SemaphoreType.DMA((5,)), pltpu.SemaphoreType.DMA((2,))]
    res = pl.pallas_call(
        bwd_kernel,
        out_shape=outs,
        in_specs=[vm] * (6 + len(KEPT)) + [hbm] * 5,
        out_specs=[vm] * 3 + [hbm] * 5,
        scratch_shapes=scratch,
        compiler_params=pltpu.CompilerParams(vmem_limit_bytes=LIMIT),
    )(x, g, valid, prow, ema, rel, *kept, *weights)
    return res[0], res[1], res[2], res[3:]


def unpack_params(flat):
    f = flat.astype(F32)
    prow = f[:O_EMA].reshape(1, O_EMA)
    ema = f[O_EMA:].reshape(4, D, H).transpose(0, 2, 1)
    rel = jnp.roll(f[O_REL : O_REL + STRETCH][::-1], 1).reshape(1, STRETCH)
    return prow, ema, rel


def pack_grads(grow, gema):
    row = grow.reshape(-1)
    drel = jnp.roll(row[O_REL : O_REL + STRETCH][::-1], 1)
    return jnp.concatenate([row[:O_REL], drel, row[O_VB:], gema.transpose(0, 2, 1).reshape(-1)])


def layer(inputs, lengths, cotangent, weights, flat):
    shape = inputs.shape
    m = shape[0] * shape[1] * shape[2]
    x, g = inputs.reshape(m, D), cotangent.reshape(m, D)
    mask = (jnp.arange(shape[2]) < lengths[:, :, None]).astype(F32).reshape(m, 1)
    valid = jnp.broadcast_to(mask, (m, 128))
    prow, ema, rel = unpack_params(flat)
    out, kept = forward(x, valid, prow, ema, rel, weights)
    dx, grow, gema, grads = backward(x, g, valid, prow, ema, rel, kept, weights)
    return out.reshape(shape), dx.reshape(shape), grads, pack_grads(grow, gema)


def grid_of(n):
    return (n // 8, 2, 2)


def pack_rows(v, n):
    rows = -(-v.shape[-1] // (128 * 32)) * 32
    return jnp.pad(v, [(0, 0)] * (v.ndim - 1) + [(0, rows * 128 - v.shape[-1])]).reshape(v.shape[:-1] + (rows, 128))


def per_device(n, inputs, lengths, cotangent, v_weight, mx_weight, h_weight, up_weight, down_weight, small_params):
    weights = (v_weight, mx_weight, h_weight, up_weight, down_weight)
    count = small_params.shape[0]
    if n == 32:
        dims = grid_of(n)
        (packed,) = gather(dims, n, (pack_rows(small_params, n),), 0)
        flat = packed.reshape(n, -1)[:, :count].reshape(-1)
        full = gather(dims, n, weights, 1)
    else:
        flat = lax.all_gather(small_params, "fsdp", axis=0, tiled=True)
        full = [lax.all_gather(w, "fsdp", axis=0, tiled=True) for w in weights]
    out, dx, grads, small = layer(inputs, lengths, cotangent, full, flat)
    if n == 32:
        rows = pack_rows(small.astype(BF16).reshape(n, count), n)
        rows = rows.reshape(n * rows.shape[1], 128)
        gdown, gup, gh, gmx, gv, gs = scatter(dims, (grads[4], grads[3], grads[2], grads[1], grads[0], rows), 2)
        gs = gs.reshape(-1)[:count]
    else:
        gv, gmx, gh, gup, gdown = (lax.psum_scatter(a.astype(F32), "fsdp", scatter_dimension=0, tiled=True) for a in grads)
        gs = lax.psum_scatter(small, "fsdp", scatter_dimension=0, tiled=True)
    return out, dx, gv, gmx, gh, gup, gdown, gs


def solution(mesh):
    rows, cols = P("fsdp", None), P(None, "fsdp", None, None)
    return jax.shard_map(
        functools.partial(per_device, mesh.shape["fsdp"]),
        mesh=mesh,
        in_specs=(cols, P(None, "fsdp"), cols, rows, rows, rows, rows, rows, P("fsdp")),
        out_specs=(cols, cols, rows, rows, rows, rows, rows, P("fsdp")),
        check_vma=False,
    )
```

```python
import functools
import math

import jax
import jax.numpy as jnp
from jax import lax
from jax.experimental import pallas as pl
from jax.experimental.pallas import tpu as pltpu
from jax.sharding import PartitionSpec as P

D = 1024
Z = 128
VALUE_WIDTH = 2048
H = 16
FF = 4096
STRETCH = 128


epsilon = 1e-05

MESH = pl.DeviceIdType.MESH

class Place:
    def __init__(self, dims):
        self.Z, self.Y, self.X = dims
        me = lax.axis_index("fsdp")
        self.me = me
        self.c = me % 2
        self.x = (me // 2) % self.X
        self.y = (me // (2 * self.X)) % self.Y
        self.z = me // (2 * self.X * self.Y)
        self.nx = self.dev(self.z, self.y, 1 - self.x, self.c)
        self.ny = self.dev(self.z, 1 - self.y, self.x, self.c)
        self.nc = self.dev(self.z, self.y, self.x, 1 - self.c)
        self.has_down = self.z > 0
        self.has_up = self.z < self.Z - 1
        self.down = self.dev(jnp.maximum(self.z - 1, 0), self.y, self.x, self.c)
        self.up = self.dev(jnp.minimum(self.z + 1, self.Z - 1), self.y, self.x, self.c)
    def dev(self, z, y, x, c):
        return ((z * self.Y + y) * self.X + x) * 2 + c
    def barrier(self):
        bar = pltpu.get_barrier_semaphore()
        def tell(d):
            pl.semaphore_signal(bar, inc=1, device_id=(d,), device_id_type=MESH)
        for d in (self.nx, self.ny, self.nc):
            tell(d)
        pl.when(self.has_down)(lambda: tell(self.down))
        pl.when(self.has_up)(lambda: tell(self.up))
        pl.semaphore_wait(bar, 3 + jnp.where(self.has_down, 1, 0) + jnp.where(self.has_up, 1, 0))

def when(cond, f):
    if cond is None: f()
    else: pl.when(cond)(f)

class Gather:
    def __init__(self, place, ins, outs, send_sem, recv_sem):
        self.p, self.ins, self.outs = place, ins, outs
        self.ss, self.rs = send_sem, recv_sem
        self.ids, self.pend = {}, []
    def rows(self, k, h):
        n = self.ins[k].shape[0]
        return (0, n) if h == 2 else (h * (n // 2), n // 2)
    def copy(self, key, k, shard, h, to, own=False):
        i = self.ids.setdefault((key, k), len(self.ids))
        r, n = self.rows(k, h)
        full = self.ins[k].shape[0]
        dst = self.outs[k].at[pl.ds(shard * full + r, n)]
        src = self.ins[k].at[pl.ds(r, n)] if own else dst
        return pltpu.make_async_remote_copy(src_ref=src, dst_ref=dst, send_sem=self.ss.at[i], recv_sem=self.rs.at[i], device_id=(to,), device_id_type=MESH)
    def send(self, cond, *a):
        when(cond, lambda: self.copy(*a).start())
        self.pend.append((cond, lambda: self.copy(*a).wait_send()))
    def recv(self, cond, key, k, shard, h):
        when(cond, lambda: self.copy(key, k, shard, h, self.p.me).wait_recv())
    def col(self, o):
        p = self.p
        if o == 0: return None, p.z
        if o > 0: return p.z - o >= 0, jnp.maximum(p.z - o, 0)
        return p.z - o <= p.Z - 1, jnp.minimum(p.z - o, p.Z - 1)
    def offs(self, s):
        return (0,) if s == 0 else (s, -s)
    def stage(self, k, s):
        p = self.p
        L = p.Z
        if s < L:
            for o in self.offs(s):
                cond, zz = self.col(o)
                sh = p.dev(zz, p.y, p.x, p.c)
                own = o == 0
                if not own:
                    self.recv(cond, ("z", o), k, sh, 2)
                if s + 1 < L:
                    both = lambda c1: c1 if cond is None else jnp.logical_and(cond, c1)
                    if o >= 0: self.send(both(p.has_up), ("z", s + 1), k, sh, 2, p.up, own)
                    if o <= 0: self.send(both(p.has_down), ("z", -(s + 1)), k, sh, 2, p.down, own)
                if abs(o) != 1:
                    self.send(cond, ("x", o), k, sh, 2, p.nx, own)
                    self.send(cond, ("y", o), k, sh, 2, p.ny, own)
                self.send(cond, ("c", o), k, sh, 2, p.nc, own)
        if 1 <= s <= L:
            for o in self.offs(s - 1):
                cond, zz = self.col(o)
                sx, sy = p.dev(zz, p.y, 1 - p.x, p.c), p.dev(zz, 1 - p.y, p.x, p.c)
                for key, sh, half, to in (("x", sx, 0, p.ny), ("y", sy, 1, p.nx)):
                    self.recv(cond, (key, o), k, sh, 2)
                    if o == 0:
                        self.send(p.has_up, (key, 1), k, sh, 2, p.up)
                        self.send(p.has_down, (key, -1), k, sh, 2, p.down)
                    self.send(cond, ("d" + key, o), k, sh, half, to)
                    self.send(cond, ("c" + key, o), k, sh, 2, p.nc)
        if 2 <= s <= L + 1:
            for o in self.offs(s - 2):
                cond, zz = self.col(o)
                sd = p.dev(zz, 1 - p.y, 1 - p.x, p.c)
                self.recv(cond, ("dx", o), k, sd, 0)
                self.recv(cond, ("dy", o), k, sd, 1)
                self.send(cond, ("cd", o), k, sd, 2, p.nc)
        if s == L + 2:
            for t in range(L):
                for o in self.offs(t):
                    cond, zz = self.col(o)
                    for key, yy, xx in (("c", p.y, p.x), ("cx", p.y, 1 - p.x), ("cy", 1 - p.y, p.x), ("cd", 1 - p.y, 1 - p.x)):
                        self.recv(cond, (key, o), k, p.dev(zz, yy, xx, 1 - p.c), 2)
    def stages(self):
        return self.p.Z + 3
    def finish(self):
        for cond, f in self.pend:
            when(cond, f)

def sems_needed(dims, K):
    Z = dims[0]
    return K * (2 * (Z - 1) + 12 * (2 * Z - 1))


F32, BF16 = jnp.float32, jnp.bfloat16
TILE = 256
O_GAIN, O_SHIFT, O_OMEGA, O_AFF, O_REL = 0, 2 * D, 4 * D, 5 * D, 5 * D + 4 * Z
O_VB = O_REL + STRETCH
O_MXB = O_VB + VALUE_WIDTH
MXW = 2 * D + Z + VALUE_WIDTH
O_HB = O_MXB + MXW
O_UPB = O_HB + D
O_DNB = O_UPB + FF
O_EMA = O_DNB + D
C_LAT, C_RES, C_HX = D, D + Z, D + Z + VALUE_WIDTH


def sigmoid(v):
    return 0.5 * jnp.tanh(0.5 * v) + 0.5


def silu_slope(v, s):
    return s * (1.0 + v * (1.0 - s))


def col_sum(v):
    return jnp.sum(v, axis=0, keepdims=True)


def dot(a, b, ca=1, cb=0):
    return lax.dot_general(a, b, (((ca,), (cb,)), ((), ())), preferred_element_type=F32)


def tiles(lo, hi, step, f):
    @pl.loop(0, (hi - lo) // step)
    def _(i):
        f(pl.multiple_of(lo + i * step, 128))


def lane_block(l):
    return pl.ds(pl.multiple_of(l * 128, 128), 128)


def center(xf):
    c = xf - jnp.mean(xf, axis=-1, keepdims=True)
    r = lax.rsqrt(jnp.mean(c * c, axis=-1, keepdims=True) + epsilon)
    return c * r, r


def ema_rates(ema):
    gate, a = sigmoid(ema[0]), sigmoid(ema[1])
    retain = 1.0 - gate * a
    weight = gate * ema[2] * ema[3] * (1.0 / math.sqrt(H))
    return gate, a, retain, weight


def rel_table(rel_row):
    wide = jnp.broadcast_to(rel_row, (STRETCH, STRETCH))
    return pltpu.roll(wide, 0, 1, stride=1, stride_axis=0).T


def causal():
    i = lax.broadcasted_iota(jnp.int32, (STRETCH, STRETCH), 0)
    j = lax.broadcasted_iota(jnp.int32, (STRETCH, STRETCH), 1)
    return j <= i


class Forward:
    def __init__(self, x, valid, prow, ema, w, s):
        self.x, self.valid, self.prow, self.ema, self.w, self.s = x, valid, prow, ema, w, s
        self.m = x.shape[0]
        self.seqs = self.m // STRETCH

    def p(self, lo, n):
        return self.prow[:, lo : lo + n]

    def pd(self, lo, col, n):
        return self.prow[:, pl.ds(pl.multiple_of(lo + col, 128), n)]

    def norm_one(self):
        s = self.s
        g, b = self.p(O_GAIN, D), self.p(O_SHIFT, D)
        for q in range(self.seqs):
            s.mpad[q, 0:8, :] = jnp.zeros((8, D), F32)

            @pl.loop(0, STRETCH // 32)
            def _(i):
                r = pl.ds(q * STRETCH + i * 32, 32)
                xhat, _ = center(self.x[r, :].astype(F32))
                n = xhat * g + b
                s.normed[r, :] = n.astype(BF16)
                s.mpad[q, pl.ds(8 + i * 32, 32), :] = n * self.valid[r, 0:1]

    def ema_kernel(self):
        _, _, retain, weight = ema_rates(self.ema)

        def step(j, p):
            self.s.kern[pl.ds(j, 1), :] = col_sum(p)
            return p * retain

        lax.fori_loop(0, STRETCH, step, weight)

    def smooth(self):
        s = self.s
        omega = self.p(O_OMEGA, D)
        for q in range(self.seqs):

            @pl.loop(0, D // 128)
            def _(l):
                lb = lane_block(l)
                om = self.prow[:, pl.ds(pl.multiple_of(O_OMEGA + l * 128, 128), 128)]
                nb = STRETCH // 8
                acc = [om * s.mpad[q, 8 + 8 * i : 16 + 8 * i, lb] for i in range(nb)]
                for b in range(8):
                    sh = [s.mpad[q, 8 - b + 8 * i : 16 - b + 8 * i, lb] for i in range(nb)]
                    for a in range(nb):
                        kb = jnp.broadcast_to(s.kern[8 * a + b : 8 * a + b + 1, lb], (8, 128))
                        for i in range(a, nb):
                            acc[i] = acc[i] + kb * sh[i - a]
                for i in range(nb):
                    r = slice(q * STRETCH + 8 * i, q * STRETCH + 8 * i + 8)
                    s.e[r, lb] = acc[i]

    def mix(self):
        s = self.s

        @pl.loop(0, self.m // 32)
        def _(i):
            r = pl.ds(i * 32, 32)
            e = s.e[r, :]
            s.mixed[r, :] = (e * sigmoid(e)).astype(BF16)

    def values(self):
        s = self.s

        def one(col):
            cols = pl.ds(col, TILE)
            v = dot(s.normed[...], self.w.v[:, cols]) + self.pd(O_VB, col, TILE)
            sv = sigmoid(v)
            s.vslope[:, cols] = silu_slope(v, sv).astype(BF16)
            s.val[:, cols] = (v * sv).astype(BF16)

        tiles(0, VALUE_WIDTH, TILE, one)

    def base(self):
        s = self.s

        def one(width):
            def f(col):
                cols = pl.ds(col, width)
                s.base[:, cols] = dot(s.mixed[...], self.w.mx[:, cols]) + self.pd(O_MXB, col, width)

            return f

        tiles(0, D, TILE, one(TILE))
        tiles(C_LAT, C_RES, Z, one(Z))
        tiles(C_RES, MXW, TILE, one(TILE))

    def attend(self):
        s = self.s
        table, mask = rel_table(self.p(O_REL, STRETCH)), causal()
        for q in range(self.seqs):
            r = slice(q * STRETCH, (q + 1) * STRETCH)
            b = s.base[r, C_LAT:C_RES]
            lat = b * sigmoid(b)
            query = (lat * (1.0 + self.p(O_AFF, Z)) + self.p(O_AFF + 2 * Z, Z)).astype(BF16)
            keys = (lat * (1.0 + self.p(O_AFF + Z, Z)) + self.p(O_AFF + 3 * Z, Z)).astype(BF16)
            sc = jnp.where(mask, dot(query, keys, 1, 1) * (1.0 / math.sqrt(Z)) + table, -1e30)
            ex = jnp.exp(sc - jnp.max(sc, axis=-1, keepdims=True))
            pr = ex / jnp.sum(ex, axis=-1, keepdims=True)
            s.probs[r, :] = pr
            s.query[r, :] = query
            s.keys[r, :] = keys
            low = pr.astype(BF16)

            def one(col):
                cols = pl.ds(col, TILE)
                at = dot(low, s.val[r, cols])
                s.att[r, cols] = at
                bb = s.base[r, pl.ds(pl.multiple_of(C_RES + col, 128), TILE)]
                s.gated[r, cols] = (at * (bb * sigmoid(bb))).astype(BF16)

            tiles(0, VALUE_WIDTH, TILE, one)

    def hidden(self):
        s = self.s

        def one(col):
            cols = pl.ds(col, TILE)
            h = dot(s.gated[...], self.w.h[:, cols]) + self.pd(O_HB, col, TILE)
            h = h + s.base[:, pl.ds(pl.multiple_of(C_HX + col, 128), TILE)]
            s.hpre[:, cols] = h
            xf = self.x[:, cols].astype(F32)
            u = sigmoid(s.base[:, cols])
            s.first[:, cols] = xf + self.valid[:, 0:1] * u * (h * sigmoid(h) - xf)

        tiles(0, D, TILE, one)

    def norm_two(self):
        s = self.s
        g, b = self.p(O_GAIN + D, D), self.p(O_SHIFT + D, D)

        @pl.loop(0, self.m // 32)
        def _(i):
            r = pl.ds(i * 32, 32)
            xhat, _ = center(s.first[r, :])
            s.second[r, :] = (xhat * g + b).astype(BF16)

    def up(self):
        s = self.s

        def one(col):
            cols = pl.ds(col, TILE)
            u = dot(s.second[...], self.w.up[:, cols]) + self.pd(O_UPB, col, TILE)
            su = sigmoid(u)
            s.uslope[:, cols] = silu_slope(u, su).astype(BF16)
            s.inner[:, cols] = (u * su).astype(BF16)

        tiles(0, FF, TILE, one)

    def down(self, out):
        s = self.s

        def one(col):
            cols = pl.ds(col, TILE)
            d = dot(s.inner[...], self.w.down[:, cols]) + self.pd(O_DNB, col, TILE)
            out[:, cols] = (s.first[:, cols] + self.valid[:, 0:1] * d).astype(BF16)

        tiles(0, D, TILE, one)


class Backward:
    def __init__(self, x, g, valid, prow, ema, w, s, t, grow, gema):
        self.x, self.g, self.valid, self.prow, self.ema = x, g, valid, prow, ema
        self.w, self.s, self.t, self.grow, self.gema = w, s, t, grow, gema
        self.m = x.shape[0]
        self.seqs = self.m // STRETCH

    p, pd = Forward.p, Forward.pd

    def put(self, lo, col, n, v):
        self.grow[:, pl.ds(pl.multiple_of(lo + col, 128), n)] = v

    def cot(self):
        def one(col):
            cols = pl.ds(col, TILE)
            d = self.valid[:, 0:1] * self.g[:, cols].astype(F32)
            self.put(O_DNB, col, TILE, col_sum(d))
            self.t.dd[:, cols] = d.astype(BF16)

        tiles(0, D, TILE, one)

    def d_up(self):
        s, t = self.s, self.t

        def one(col):
            cols = pl.ds(col, TILE)
            di = dot(t.dd[...], self.w.down[cols, :], 1, 1)
            du = di * s.uslope[:, cols].astype(F32)
            self.put(O_UPB, col, TILE, col_sum(du))
            t.dup[:, cols] = du.astype(BF16)

        tiles(0, FF, TILE, one)

    def d_second(self):
        t = self.t

        def one(col):
            cols = pl.ds(col, TILE)
            t.dsec[:, cols] = dot(t.dup[...], self.w.up[cols, :], 1, 1)

        tiles(0, D, TILE, one)

    def norm_two(self):
        s, t = self.s, self.t
        g = self.p(O_GAIN + D, D)
        t.acc[...] = jnp.zeros(t.acc.shape, F32)

        def add(k, v):
            t.acc[k] += jnp.sum(v.reshape(v.shape[0] // 8, 8, D), axis=0)

        @pl.loop(0, self.m // 32)
        def _(i):
            r = pl.ds(i * 32, 32)
            xhat, rstd = center(s.first[r, :])
            ds = t.dsec[r, :]
            add(0, ds * xhat)
            add(1, ds)
            dh = ds * g
            dn = rstd * (dh - jnp.mean(dh, axis=-1, keepdims=True) - xhat * jnp.mean(dh * xhat, axis=-1, keepdims=True))
            df = self.g[r, :].astype(F32) + dn
            v = self.valid[r, 0:1]
            u = sigmoid(s.base[r, 0:D])
            hp = s.hpre[r, :]
            sh = sigmoid(hp)
            xf = self.x[r, :].astype(F32)
            vu = v * u
            t.dx[r, :] = df - df * vu
            db = df * v * (hp * sh - xf) * u * (1.0 - u)
            add(2, db)
            t.dbase[r, 0:D] = db.astype(BF16)
            dhp = df * vu * silu_slope(hp, sh)
            add(3, dhp)
            t.dbase[r, C_HX:MXW] = dhp.astype(BF16)

        for k, lo in enumerate((O_GAIN + D, O_SHIFT + D, O_MXB, O_HB)):
            self.grow[:, lo : lo + D] = col_sum(t.acc[k])
        self.grow[:, O_MXB + C_HX : O_MXB + MXW] = col_sum(t.acc[3])

    def d_gated(self):
        s, t = self.s, self.t

        def one(col):
            cols = pl.ds(col, TILE)
            bcols = pl.ds(pl.multiple_of(C_RES + col, 128), TILE)
            dg = dot(t.dbase[:, C_HX:MXW], self.w.h[cols, :], 1, 1)
            b = s.base[:, bcols]
            sb = sigmoid(b)
            t.datt[:, cols] = (dg * (b * sb)).astype(BF16)
            db = dg * s.att[:, cols] * silu_slope(b, sb)
            self.put(O_MXB + C_RES, col, TILE, col_sum(db))
            t.dbase[:, bcols] = db.astype(BF16)

        tiles(0, VALUE_WIDTH, TILE, one)

    def attend(self):
        s, t = self.s, self.t
        mask = causal()
        lows, drel = [], None
        aff = [0.0, 0.0, 0.0, 0.0]
        lat_bias = 0.0
        for q in range(self.seqs):
            r = slice(q * STRETCH, (q + 1) * STRETCH)
            pr = s.probs[r, :]
            lows.append(pr.astype(BF16))
            dp = dot(t.datt[r, :], s.val[r, :], 1, 1)
            ds = pr * (dp - jnp.sum(pr * dp, axis=-1, keepdims=True))
            ds = jnp.where(mask, ds, 0.0)
            drel = ds if drel is None else drel + ds
            raw = (ds * (1.0 / math.sqrt(Z))).astype(BF16)
            dq = dot(raw, s.keys[r, :])
            dk = dot(raw, s.query[r, :], 0, 0)
            b = s.base[r, C_LAT:C_RES]
            sb = sigmoid(b)
            lat = b * sb
            for k, v in enumerate((dq * lat, dk * lat, dq, dk)):
                aff[k] = aff[k] + col_sum(v)
            dl = dq * (1.0 + self.p(O_AFF, Z)) + dk * (1.0 + self.p(O_AFF + Z, Z))
            db = dl * silu_slope(b, sb)
            lat_bias = lat_bias + col_sum(db)
            t.dbase[r, C_LAT:C_RES] = db.astype(BF16)
        for k in range(4):
            self.grow[:, O_AFF + k * Z : O_AFF + (k + 1) * Z] = aff[k]
        self.grow[:, O_MXB + C_LAT : O_MXB + C_RES] = lat_bias
        drel = drel.T
        eight = 0.0
        for i in range(0, STRETCH, 8):
            eight = eight + pltpu.roll(drel[i : i + 8, :], (STRETCH - i) % STRETCH, 1)
        back = 0.0
        for i in range(8):
            back = back + pltpu.roll(eight[i : i + 1, :], (STRETCH - i) % STRETCH, 1)
        self.grow[:, O_REL : O_REL + STRETCH] = back

        def one(col):
            cols = pl.ds(col, TILE)
            bias = 0.0
            for q in range(self.seqs):
                r = slice(q * STRETCH, (q + 1) * STRETCH)
                dv = dot(lows[q], t.datt[r, cols], 0, 0)
                dv = dv * s.vslope[r, cols].astype(F32)
                bias = bias + col_sum(dv)
                t.dv[r, cols] = dv.astype(BF16)
            self.put(O_VB, col, TILE, bias)

        tiles(0, VALUE_WIDTH, TILE, one)

    def d_mixed(self):
        s, t = self.s, self.t
        for q in range(self.seqs):
            t.dpad[q, STRETCH : STRETCH + 8, :] = jnp.zeros((8, D), F32)

        def one(col):
            cols = pl.ds(col, TILE)
            dm = dot(t.dbase[...], self.w.mx[cols, :], 1, 1)
            e = s.e[:, cols]
            de = dm * silu_slope(e, sigmoid(e))
            om = 0.0
            for q in range(self.seqs):
                d = de[q * STRETCH : (q + 1) * STRETCH, :]
                t.dpad[q, 0:STRETCH, cols] = d
                om = om + col_sum(d * s.mpad[q, 8 : 8 + STRETCH, cols])
            self.put(O_OMEGA, col, TILE, om)

        tiles(0, D, TILE, one)

    def d_normed(self):
        t = self.t

        def one(col):
            cols = pl.ds(col, TILE)
            t.dn[:, cols] = dot(t.dv[...], self.w.v[cols, :], 1, 1)

        tiles(0, D, TILE, one)

    def smooth(self):
        s, t = self.s, self.t
        nb = STRETCH // 8

        @pl.loop(0, D // 128)
        def _(l):
            lb = lane_block(l)
            om = self.prow[:, pl.ds(pl.multiple_of(O_OMEGA + l * 128, 128), 128)]
            for q in range(self.seqs):
                acc = [om * t.dpad[q, 8 * i : 8 * i + 8, lb] for i in range(nb)]
                for b in range(8):
                    sh = [t.dpad[q, 8 * i + b : 8 * i + b + 8, lb] for i in range(nb)]
                    for a in range(nb):
                        kb = jnp.broadcast_to(s.kern[8 * a + b : 8 * a + b + 1, lb], (8, 128))
                        for i in range(nb - a):
                            acc[i] = acc[i] + kb * sh[i + a]
                for i in range(nb):
                    r = slice(q * STRETCH + 8 * i, q * STRETCH + 8 * i + 8)
                    t.dn[r, lb] = t.dn[r, lb] + self.valid[r, :] * acc[i]

        @pl.loop(0, D // 128)
        def _(l):
            lb = lane_block(l)
            for b in range(8):
                sums = [None] * nb
                for q in range(self.seqs):
                    de = [t.dpad[q, 8 * i : 8 * i + 8, lb] for i in range(nb)]
                    sh = [s.mpad[q, 8 - b + 8 * i : 16 - b + 8 * i, lb] for i in range(nb)]
                    for a in range(nb):
                        for i in range(a, nb):
                            v = de[i] * sh[i - a]
                            sums[a] = v if sums[a] is None else sums[a] + v
                for a in range(nb):
                    t.dkern[8 * a + b : 8 * a + b + 1, lb] = col_sum(sums[a])

    def norm_one(self, out):
        t = self.t
        g = self.p(O_GAIN, D)
        t.acc[...] = jnp.zeros(t.acc.shape, F32)

        def add(k, v):
            t.acc[k] += jnp.sum(v.reshape(v.shape[0] // 8, 8, D), axis=0)

        @pl.loop(0, self.m // 32)
        def _(i):
            r = pl.ds(i * 32, 32)
            xhat, rstd = center(self.x[r, :].astype(F32))
            dn = t.dn[r, :]
            add(0, dn * xhat)
            add(1, dn)
            dh = dn * g
            d = rstd * (dh - jnp.mean(dh, axis=-1, keepdims=True) - xhat * jnp.mean(dh * xhat, axis=-1, keepdims=True))
            out[r, :] = (t.dx[r, :] + d).astype(BF16)

        for k, lo in enumerate((O_GAIN, O_SHIFT)):
            self.grow[:, lo : lo + D] = col_sum(t.acc[k])


    def ema_grads(self):
        t = self.t
        gate, a, retain, weight = ema_rates(self.ema)
        zero = retain - retain

        def step(j, carry):
            power, before, dw, dr = carry
            row = t.dkern[pl.ds(j, 1), :]
            dw = dw + row * power
            dr = dr + (row * j.astype(F32)) * before
            return power * retain, power, dw, dr

        _, _, dw, dr = lax.fori_loop(0, STRETCH, step, (zero + 1.0, zero, zero, zero))
        drate = -dr * weight
        scale = 1.0 / math.sqrt(H)
        dgate = drate * a + dw * self.ema[2] * self.ema[3] * scale
        self.gema[0] = dgate * gate * (1.0 - gate)
        self.gema[1] = drate * gate * a * (1.0 - a)
        self.gema[2] = dw * gate * self.ema[3] * scale
        self.gema[3] = dw * gate * self.ema[2] * scale


class Scatter:
    def __init__(self, place, grads, bufs, outs, send_sem, recv_sem, local_sem):
        self.p, self.grads, self.bufs, self.outs = place, grads, bufs, outs
        self.ss, self.rs, self.ls = send_sem, recv_sem, local_sem
        self.ids, self.pend = {}, []

    def copy(self, key, k, src, dst, to):
        i = self.ids.setdefault((key, k), len(self.ids))
        return pltpu.make_async_remote_copy(src_ref=src, dst_ref=dst, send_sem=self.ss.at[i], recv_sem=self.rs.at[i], device_id=(to,), device_id_type=MESH)

    def send(self, cond, key, k, src, dst, to):
        when(cond, lambda: self.copy(key, k, src, dst, to).start())
        self.pend.append((cond, lambda: self.copy(key, k, src, dst, to).wait_send()))

    def recv(self, cond, key, k, dst):
        when(cond, lambda: self.copy(key, k, dst, dst, self.p.me).wait_recv())

    def own(self, k, z):
        p, b = self.p, self.bufs[k]
        layer = p.Y * p.X
        i = k * p.Z + z
        return pltpu.make_async_copy(self.grads[k].at[pl.ds(z * layer, layer), p.c], b.mine.at[pl.ds(z * layer, layer)], self.ls.at[i])

    def add(self, dst, a, b, r0=0, rows=None):
        n = rows

        @pl.loop(0, n // 16)
        def _(i):
            def at(v, r):
                ref, q, off = v
                return ref.at[q, pl.ds(pl.multiple_of(off + r, 16), 16)]

            r = i * 16
            at(dst, r)[...] = at(a, r)[...] + at(b, r)[...]

    def stage(self, k, s):
        p, b = self.p, self.bufs[k]
        layer = p.Y * p.X
        r = b.sum.shape[1]
        half = r // 2
        chip = lambda z, y, x: (z * p.Y + y) * p.X + x
        col = lambda z: (chip(z, p.y, p.x), chip(z, p.y, 1 - p.x), chip(z, 1 - p.y, p.x), chip(z, 1 - p.y, 1 - p.x))
        order = list(range(p.Z))
        if s == 0:
            for z in order:
                self.send(None, ("c", z), k, self.grads[k].at[pl.ds(z * layer, layer), 1 - p.c], b.sum.at[pl.ds(z * layer, layer)], p.nc)
                self.own(k, z).start()
        if s == 1:
            for z in order:
                self.recv(None, ("c", z), k, b.sum.at[pl.ds(z * layer, layer)])
                self.own(k, z).wait()
                me, nx, ny, nd = col(z)
                self.add((b.sum, nd, 0), (b.sum, nd, 0), (b.mine, nd, 0), rows=r)
                self.send(None, ("dx", z), k, b.sum.at[nd, pl.ds(0, half)], b.dx.at[z], p.nx)
                self.send(None, ("dy", z), k, b.sum.at[nd, pl.ds(half, half)], b.dy.at[z], p.ny)
                for q in (nx, ny, me):
                    self.add((b.sum, q, 0), (b.sum, q, 0), (b.mine, q, 0), rows=r)
        if s == 2:
            for z in order:
                me, nx, ny, nd = col(z)
                self.recv(None, ("dx", z), k, b.dx.at[z])
                self.add((b.sum, ny, 0), (b.sum, ny, 0), (b.dx, z, 0), rows=half)
                self.send(None, ("y", z), k, b.sum.at[ny], b.ry.at[z], p.ny)
                self.recv(None, ("dy", z), k, b.dy.at[z])
                self.add((b.sum, nx, half), (b.sum, nx, half), (b.dy, z, 0), rows=half)
                self.send(None, ("x", z), k, b.sum.at[nx], b.rx.at[z], p.nx)
        if s == 3:
            for z in order:
                me = col(z)[0]
                self.recv(None, ("y", z), k, b.ry.at[z])
                self.add((b.sum, me, 0), (b.sum, me, 0), (b.ry, z, 0), rows=r)
                self.recv(None, ("x", z), k, b.rx.at[z])
                self.add((b.sum, me, 0), (b.sum, me, 0), (b.rx, z, 0), rows=r)
        if s == 4:
            for d in range(1, p.Z):
                for up in (True, False):
                    t = p.Z - d if up else d - 1
                    buf, key = (b.ru, "u") if up else (b.rd, "d")
                    q = chip(t, p.y, p.x)
                    passing = p.z < t if up else p.z > t
                    fed = p.has_down if up else p.has_up

                    def relay(q=q, t=t, buf=buf, key=key):
                        self.copy((key, t), k, buf.at[t], buf.at[t], p.me).wait_recv()
                        self.add((b.sum, q, 0), (b.sum, q, 0), (buf, t, 0), rows=r)

                    pl.when(jnp.logical_and(passing, fed))(relay)
                    self.send(passing, (key, t), k, b.sum.at[q], buf.at[t], p.up if up else p.down)
        if s == 5:
            for cond, buf, key in ((None, None, None), (p.has_down, b.ru, "u"), (p.has_up, b.rd, "d")):
                me = chip(p.z, p.y, p.x)
                out = self.outs[k]
                if buf is None:
                    @pl.loop(0, r // 16)
                    def _(i):
                        rr = pl.ds(pl.multiple_of(i * 16, 16), 16)
                        out[rr, :] = b.sum[me, rr, :].astype(F32)
                    continue

                for t in range(p.Z):
                    def last(buf=buf, key=key, out=out, t=t):
                        self.copy((key, t), k, buf.at[t], buf.at[t], p.me).wait_recv()

                        @pl.loop(0, r // 16)
                        def _(i):
                            rr = pl.ds(pl.multiple_of(i * 16, 16), 16)
                            out[rr, :] += buf[t, rr, :].astype(F32)

                    if (key == "u" and t == 0) or (key == "d" and t == p.Z - 1):
                        continue
                    pl.when(jnp.logical_and(cond, p.z == t))(last)

    def stages(self):
        return 6

    def finish(self):
        for cond, f in self.pend:
            when(cond, f)


class Names:
    def __init__(self, **kw):
        self.__dict__.update(kw)


SCATTER_BUFS = ("mine", "sum", "dx", "dy", "rx", "ry", "ru", "rd")


def scatter_scratch(dims, r, w):
    Z, Y, X = dims
    chips = Z * Y * X
    shapes = ((chips, r, w), (chips, r, w), (Z, r // 2, w), (Z, r // 2, w), (Z, r, w), (Z, r, w), (Z, r, w), (Z, r, w))
    return [pltpu.VMEM(s, BF16) for s in shapes]


def scatter_sems(dims, K):
    Z = dims[0]
    return K * (5 * Z + 2 * (Z - 1))


def rs_kernel(dims, K, *refs):
    grads, outs = refs[:K], refs[K : 2 * K]
    nb = len(SCATTER_BUFS)
    bufs = [Names(**dict(zip(SCATTER_BUFS, refs[2 * K + nb * k : 2 * K + nb * (k + 1)]))) for k in range(K)]
    ss, rs, ls = refs[2 * K + nb * K :]
    p = Place(dims)
    p.barrier()
    sc = Scatter(p, grads, bufs, outs, ss, rs, ls)
    S = sc.stages()
    for t in range(K + S - 1):
        for k in range(K):
            if 0 <= t - k < S:
                sc.stage(k, t - k)
    sc.finish()


def scatter(dims, grads, cid):
    K = len(grads)
    n = 2 * dims[0] * dims[1] * dims[2]
    shaped = [g.reshape(n // 2, 2, g.shape[0] // n, g.shape[1]) for g in grads]
    scratch = []
    for g in shaped:
        scratch += scatter_scratch(dims, g.shape[2], g.shape[3])
    ns = scatter_sems(dims, K)
    return pl.pallas_call(
        functools.partial(rs_kernel, dims, K),
        out_shape=[jax.ShapeDtypeStruct(g.shape[2:], F32) for g in shaped],
        in_specs=[pl.BlockSpec(memory_space=pl.ANY)] * K,
        out_specs=[pl.BlockSpec(memory_space=pltpu.VMEM)] * K,
        scratch_shapes=scratch + [pltpu.SemaphoreType.DMA((ns,)), pltpu.SemaphoreType.DMA((ns,)), pltpu.SemaphoreType.DMA((K * dims[0],))],
        compiler_params=pltpu.CompilerParams(collective_id=cid, has_side_effects=True, vmem_limit_bytes=64 * 1024 * 1024),
    )(*shaped)


KEPT = ("normed", "mpad", "e", "mixed", "kern", "vslope", "val", "base", "probs", "query", "keys", "att", "gated", "hpre", "first", "second", "uslope", "inner")


def kept_shapes(m):
    seqs = m // STRETCH
    f, b = (lambda *s: (s, F32)), (lambda *s: (s, BF16))
    return dict(
        normed=b(m, D), mpad=f(seqs, STRETCH + 8, D), e=f(m, D), mixed=b(m, D), kern=f(STRETCH, D),
        vslope=b(m, VALUE_WIDTH), val=b(m, VALUE_WIDTH), base=f(m, MXW), probs=f(m, STRETCH),
        query=b(m, Z), keys=b(m, Z), att=f(m, VALUE_WIDTH), gated=b(m, VALUE_WIDTH), hpre=f(m, D),
        first=f(m, D), second=b(m, D), uslope=b(m, FF), inner=b(m, FF),
    )


VM = pltpu.VMEM
LIMIT = 64 * 1024 * 1024


def weight_grad(a, b, n, out, stage, sem, lo=0):
    count = out.shape[0] // TILE

    def copy(i, slot):
        return pltpu.make_async_copy(stage.at[slot, :, 0:n], out.at[pl.ds(pl.multiple_of(i * TILE, TILE), TILE)], sem.at[slot])

    @pl.loop(0, count // 2)
    def _(j):
        for slot in range(2):
            i = j * 2 + slot

            @pl.when(j > 0)
            def _():
                copy(i - 2, slot).wait()

            rows = a[:, pl.ds(pl.multiple_of(i * TILE, TILE), TILE)]
            for c in range(0, n, 1024):
                wd = min(1024, n - c)
                stage[slot, :, c : c + wd] = dot(rows, b[:, lo + c : lo + c + wd], 0, 0).astype(BF16)
            copy(i, slot).start()

    for slot in range(2):
        copy(count - 2 + slot, slot).wait()


def own_shapes(m):
    seqs = m // STRETCH
    return dict(
        dd=((m, D), BF16), acc=((4, 8, D), F32), dx=((m, D), F32),
        dbase=((m, MXW), BF16), datt=((m, VALUE_WIDTH), BF16), dv=((m, VALUE_WIDTH), BF16),
        dpad=((seqs, STRETCH + 8, D), F32), dn=((m, D), F32), dkern=((STRETCH, D), F32),
    )


SMALL_ROWS = 32
FRAME = 24


def frames(n, count):
    return [(count * d) // 128 for d in range(n)]


def spread(k):
    p = lax.broadcasted_iota(jnp.int32, (D, TILE), 0)
    c = lax.broadcasted_iota(jnp.int32, (D, TILE), 1) + k * TILE
    return (c == 8 * (p % 128) + p // 128).astype(BF16)


def unpack_params(n, count, packed, full, prow, ema):
    full[...] = jnp.zeros(full.shape, F32)
    for d, r in enumerate(frames(n, count)):
        full[r : r + FRAME, :] += packed[d * SMALL_ROWS : d * SMALL_ROWS + FRAME, :].astype(F32)
    for i in range(O_EMA // 128):
        prow[:, i * 128 : (i + 1) * 128] = full[i : i + 1, :]
    rows = []
    for j in range(4):
        lo = O_EMA // 128 + j * D * H // 128
        t = full[lo : lo + 128, :].T
        rows.append(jnp.concatenate([t[H * k : H * (k + 1), :] for k in range(8)], axis=1))
    stack = jnp.concatenate(rows, axis=0).astype(BF16)
    for k in range(D // TILE):
        e = dot(stack, spread(k))
        for j in range(4):
            ema[j, :, k * TILE : (k + 1) * TILE] = e[j * H : (j + 1) * H, :]


def pack_grads(n, count, grow, gema, full, out):
    for i in range(O_EMA // 128):
        full[i : i + 1, :] = grow[:, i * 128 : (i + 1) * 128]
    stack = jnp.concatenate([gema[j] for j in range(4)], axis=0).astype(BF16)
    back = 0.0
    for k in range(D // TILE):
        back = back + dot(stack[:, k * TILE : (k + 1) * TILE], spread(k), 1, 1)
    for j in range(4):
        e = back[j * H : (j + 1) * H, :]
        lo = O_EMA // 128 + j * D * H // 128
        full[lo : lo + 128, :] = jnp.concatenate([e[:, k * 128 : (k + 1) * 128] for k in range(8)], axis=0).T
    for d, r in enumerate(frames(n, count)):
        out[d * SMALL_ROWS : d * SMALL_ROWS + FRAME, :] = full[r : r + FRAME, :].astype(BF16)
        out[d * SMALL_ROWS + FRAME : (d + 1) * SMALL_ROWS, :] = jnp.zeros((SMALL_ROWS - FRAME, 128), BF16)


class Skip:
    def step(self):
        pass


def mega_kernel(dims, n, count, K, *refs):
    x, g, valid = refs[:3]
    ins = refs[3 : 3 + K]
    refs = refs[3 + K :]
    out, dxo, gsmall = refs[:3]
    grads = refs[3:8]
    full_w = refs[8 : 8 + K] if dims else ins
    refs = refs[8 + K :] if dims else refs[8:]
    ks, own = KEPT, own_shapes(x.shape[0])
    s = Names(**dict(zip(ks, refs[: len(ks)])))
    refs = refs[len(ks) :]
    t = Names(**dict(zip(own, refs[: len(own)])))
    t.dup, t.dsec = s.inner, t.dn
    refs = refs[len(own) :]
    wr, wc, wv, stage, full, packed, prow, ema, grow, gema, lsem, ssem = refs[:12]
    hsmall, hv, hmx, hh, hup, hdown = full_w

    def loader(i, a, b):
        return pltpu.make_async_copy(a, b, lsem.at[i])

    if dims:
        p = Place(dims)
        p.barrier()
        osem, send_sem, recv_sem = refs[12:]
        gat = Gather(p, ins, full_w, send_sem, recv_sem)
        cps = [pltpu.make_async_copy(ins[k], full_w[k].at[pl.ds(p.me * ins[k].shape[0], ins[k].shape[0])], osem.at[k]) for k in range(K)]
        for cp in cps:
            cp.start()
        S = gat.stages()

        def step(t):
            for k in range(K):
                if 0 <= t - k < S:
                    gat.stage(k, t - k)
                    if t - k == S - 1:
                        cps[k].wait()
    else:
        S = 7

        def step(t):
            pass

    w = Names(v=wv, mx=wc, h=wr.at[0:VALUE_WIDTH], up=wc.at[:, 0:FF], down=wr)
    f = Forward(x, valid, prow, ema, w, s)
    b = Backward(x, g, valid, prow, ema, w, s, t, grow, gema)
    gv, gmx, gh, gup, gdown = grads
    l_small = loader(0, hsmall, packed)
    l_v = loader(1, hv, wv)
    l_mx = loader(2, hmx, wc)
    l_h = loader(3, hh, wr.at[0:VALUE_WIDTH])
    l_up = loader(4, hup, wc.at[:, 0:FF])
    l_down = loader(5, hdown, wr)

    for i in range(S):
        step(i)
    l_small.start()
    l_small.wait()
    unpack_params(n, count, packed, full, prow, ema)
    f.norm_one()
    f.ema_kernel()
    step(S)
    l_v.start()
    f.smooth()
    f.mix()
    l_v.wait()
    step(S + 1)
    l_mx.start()
    f.values()
    l_mx.wait()
    f.base()
    step(S + 2)
    l_h.start()
    f.attend()
    l_h.wait()
    f.hidden()
    f.norm_two()
    step(S + 3)
    l_up.start()
    b.cot()
    l_up.wait()
    f.up()
    weight_grad(s.inner, t.dd, D, gdown, stage, ssem)
    step(S + 4)
    l_down.start()
    l_down.wait()
    f.down(out)
    b.d_up()
    l_h.start()
    weight_grad(s.second, t.dup, FF, gup, stage, ssem)
    b.d_second()
    l_mx.start()
    b.norm_two()
    weight_grad(s.gated, t.dbase, D, gh, stage, ssem, lo=C_HX)
    l_h.wait()
    b.d_gated()
    b.attend()
    weight_grad(s.mixed, t.dbase, MXW, gmx, stage, ssem)
    weight_grad(s.normed, t.dv, VALUE_WIDTH, gv, stage, ssem)
    l_mx.wait()
    b.d_mixed()
    b.d_normed()
    b.smooth()
    b.norm_one(dxo)
    b.ema_grads()
    pack_grads(n, count, grow, gema, full, gsmall)
    if dims:
        gat.finish()


def mega(dims, n, count, x, g, valid, arrays, cid):
    m, K = x.shape[0], len(arrays)
    vm, hbm = pl.BlockSpec(memory_space=VM), pl.BlockSpec(memory_space=pl.ANY)
    whole = [(n * a.shape[0], a.shape[1]) if dims else a.shape for a in arrays]
    outs = [((m, D), BF16), ((m, D), BF16), ((n * SMALL_ROWS, 128), BF16)] + [(s, BF16) for s in whole[1:]]
    specs = [vm] * 3 + [hbm] * 5
    sems = [pltpu.SemaphoreType.DMA((K,)), pltpu.SemaphoreType.DMA((2,))]
    params = dict(vmem_limit_bytes=LIMIT)
    if dims:
        outs += [(s, BF16) for s in whole]
        specs += [hbm] * K
        ns = sems_needed(dims, K)
        sems += [pltpu.SemaphoreType.DMA((K,)), pltpu.SemaphoreType.DMA((ns,)), pltpu.SemaphoreType.DMA((ns,))]
        params.update(collective_id=cid, has_side_effects=True)
    rows = -(-(n * count) // 128) + FRAME
    scratch = [VM(*v) for v in kept_shapes(m).values()] + [VM(*v) for v in own_shapes(m).values()]
    scratch += [VM((FF, D), BF16), VM((D, MXW), BF16), VM((D, VALUE_WIDTH), BF16), VM((2, TILE, MXW), BF16)]
    scratch += [VM((-(-rows // 8) * 8, 128), F32), VM((n * SMALL_ROWS, 128), BF16)]
    scratch += [VM((1, O_EMA), F32), VM((4, H, D), F32), VM((1, O_EMA), F32), VM((4, H, D), F32)]
    res = pl.pallas_call(
        functools.partial(mega_kernel, dims, n, count, K),
        out_shape=[jax.ShapeDtypeStruct(*o) for o in outs],
        in_specs=[vm] * 3 + [hbm] * K,
        out_specs=specs,
        scratch_shapes=scratch + sems,
        compiler_params=pltpu.CompilerParams(**params),
    )(x, g, valid, *arrays)
    return res[0], res[1], res[2], res[3:8]


def frame_in(small, me):
    count = small.shape[0]
    line = lax.dynamic_update_slice(jnp.zeros((FRAME * 128,), small.dtype), small, ((me * count) % 128,))
    return jnp.pad(line.reshape(FRAME, 128), ((0, SMALL_ROWS - FRAME), (0, 0)))


def frame_out(block, me, count):
    return lax.dynamic_slice(block.reshape(-1), ((me * count) % 128,), (count,))


def grid_of(n):
    return (n // 8, 2, 2)


def per_device(n, inputs, lengths, cotangent, v_weight, mx_weight, h_weight, up_weight, down_weight, small_params):
    shape = inputs.shape
    m, count = shape[0] * shape[1] * shape[2], small_params.shape[0]
    me = lax.axis_index("fsdp")
    x, g = inputs.reshape(m, D), cotangent.reshape(m, D)
    mask = (jnp.arange(shape[2]) < lengths[:, :, None]).astype(F32).reshape(m, 1)
    valid = jnp.broadcast_to(mask, (m, 128))
    arrays = (frame_in(small_params, me), v_weight, mx_weight, h_weight, up_weight, down_weight)
    dims = grid_of(n) if n == 32 else None
    if not dims:
        arrays = [lax.all_gather(a, "fsdp", axis=0, tiled=True) for a in arrays]
    out, dx, small, (gv, gmx, gh, gup, gdown) = mega(dims, n, count, x, g, valid, arrays, 0)
    if dims:
        gdown, gup, gh, gmx, gv, gs = scatter(dims, (gdown, gup, gh, gmx, gv, small), 1)
    else:
        gv, gmx, gh, gup, gdown, gs = (
            lax.psum_scatter(a.astype(F32), "fsdp", scatter_dimension=0, tiled=True) for a in (gv, gmx, gh, gup, gdown, small)
        )
    return out.reshape(shape), dx.reshape(shape), gv, gmx, gh, gup, gdown, frame_out(gs, me, count)


def solution(mesh):
    rows, cols = P("fsdp", None), P(None, "fsdp", None, None)
    return jax.shard_map(
        functools.partial(per_device, mesh.shape["fsdp"]),
        mesh=mesh,
        in_specs=(cols, P(None, "fsdp"), cols, rows, rows, rows, rows, rows, P("fsdp")),
        out_specs=(cols, cols, rows, rows, rows, rows, rows, P("fsdp")),
        check_vma=False,
    )
```

```python
import functools
import math

import jax
import jax.numpy as jnp
from jax import lax
from jax.experimental import pallas as pl
from jax.experimental.pallas import tpu as pltpu
from jax.sharding import PartitionSpec as P

D = 1024
Z = 128
VALUE_WIDTH = 2048
H = 16
FF = 4096
STRETCH = 128


epsilon = 1e-05

MESH = pl.DeviceIdType.MESH

class Place:
    def __init__(self, dims):
        self.Z, self.Y, self.X = dims
        me = lax.axis_index("fsdp")
        self.me = me
        self.c = me % 2
        self.x = (me // 2) % self.X
        self.y = (me // (2 * self.X)) % self.Y
        self.z = me // (2 * self.X * self.Y)
        self.nx = self.dev(self.z, self.y, 1 - self.x, self.c)
        self.ny = self.dev(self.z, 1 - self.y, self.x, self.c)
        self.nc = self.dev(self.z, self.y, self.x, 1 - self.c)
        self.has_down = self.z > 0
        self.has_up = self.z < self.Z - 1
        self.down = self.dev(jnp.maximum(self.z - 1, 0), self.y, self.x, self.c)
        self.up = self.dev(jnp.minimum(self.z + 1, self.Z - 1), self.y, self.x, self.c)
    def dev(self, z, y, x, c):
        return ((z * self.Y + y) * self.X + x) * 2 + c
    def barrier(self):
        bar = pltpu.get_barrier_semaphore()
        def tell(d):
            pl.semaphore_signal(bar, inc=1, device_id=(d,), device_id_type=MESH)
        for d in (self.nx, self.ny, self.nc):
            tell(d)
        pl.when(self.has_down)(lambda: tell(self.down))
        pl.when(self.has_up)(lambda: tell(self.up))
        pl.semaphore_wait(bar, 3 + jnp.where(self.has_down, 1, 0) + jnp.where(self.has_up, 1, 0))

    def barrier_all(self, n):
        bar = pltpu.get_barrier_semaphore()

        @pl.loop(1, n)
        def _(i):
            pl.semaphore_signal(bar, inc=1, device_id=((self.me + i) % n,), device_id_type=MESH)

        pl.semaphore_wait(bar, n - 1)

def when(cond, f):
    if cond is None: f()
    else: pl.when(cond)(f)

class Gather:
    def __init__(self, place, ins, outs, send_sem, recv_sem):
        self.p, self.ins, self.outs = place, ins, outs
        self.ss, self.rs = send_sem, recv_sem
        self.ids, self.pend = {}, []
    def rows(self, k, h):
        n = self.ins[k].shape[0]
        return (0, n) if h == 2 else (h * (n // 2), n // 2)
    def copy(self, key, k, shard, h, to, own=False):
        i = self.ids.setdefault((key, k), len(self.ids))
        r, n = self.rows(k, h)
        full = self.ins[k].shape[0]
        dst = self.outs[k].at[pl.ds(shard * full + r, n)]
        src = self.ins[k].at[pl.ds(r, n)] if own else dst
        return pltpu.make_async_remote_copy(src_ref=src, dst_ref=dst, send_sem=self.ss.at[i], recv_sem=self.rs.at[i], device_id=(to,), device_id_type=MESH)
    def send(self, cond, *a):
        when(cond, lambda: self.copy(*a).start())
        self.pend.append((cond, lambda: self.copy(*a).wait_send()))
    def recv(self, cond, key, k, shard, h):
        when(cond, lambda: self.copy(key, k, shard, h, self.p.me).wait_recv())
    def col(self, o):
        p = self.p
        if o == 0: return None, p.z
        if o > 0: return p.z - o >= 0, jnp.maximum(p.z - o, 0)
        return p.z - o <= p.Z - 1, jnp.minimum(p.z - o, p.Z - 1)
    def offs(self, s):
        return (0,) if s == 0 else (s, -s)
    def stage(self, k, s):
        p = self.p
        L = p.Z
        if s < L:
            for o in self.offs(s):
                cond, zz = self.col(o)
                sh = p.dev(zz, p.y, p.x, p.c)
                own = o == 0
                if not own:
                    self.recv(cond, ("z", o), k, sh, 2)
                if s + 1 < L:
                    both = lambda c1: c1 if cond is None else jnp.logical_and(cond, c1)
                    if o >= 0: self.send(both(p.has_up), ("z", s + 1), k, sh, 2, p.up, own)
                    if o <= 0: self.send(both(p.has_down), ("z", -(s + 1)), k, sh, 2, p.down, own)
                if abs(o) != 1:
                    self.send(cond, ("x", o), k, sh, 2, p.nx, own)
                    self.send(cond, ("y", o), k, sh, 2, p.ny, own)
                self.send(cond, ("c", o), k, sh, 2, p.nc, own)
        if 1 <= s <= L:
            for o in self.offs(s - 1):
                cond, zz = self.col(o)
                sx, sy = p.dev(zz, p.y, 1 - p.x, p.c), p.dev(zz, 1 - p.y, p.x, p.c)
                for key, sh, half, to in (("x", sx, 0, p.ny), ("y", sy, 1, p.nx)):
                    self.recv(cond, (key, o), k, sh, 2)
                    if o == 0:
                        self.send(p.has_up, (key, 1), k, sh, 2, p.up)
                        self.send(p.has_down, (key, -1), k, sh, 2, p.down)
                    self.send(cond, ("d" + key, o), k, sh, half, to)
                    self.send(cond, ("c" + key, o), k, sh, 2, p.nc)
        if 2 <= s <= L + 1:
            for o in self.offs(s - 2):
                cond, zz = self.col(o)
                sd = p.dev(zz, 1 - p.y, 1 - p.x, p.c)
                self.recv(cond, ("dx", o), k, sd, 0)
                self.recv(cond, ("dy", o), k, sd, 1)
                self.send(cond, ("cd", o), k, sd, 2, p.nc)
        if s == L + 2:
            for t in range(L):
                for o in self.offs(t):
                    cond, zz = self.col(o)
                    for key, yy, xx in (("c", p.y, p.x), ("cx", p.y, 1 - p.x), ("cy", 1 - p.y, p.x), ("cd", 1 - p.y, 1 - p.x)):
                        self.recv(cond, (key, o), k, p.dev(zz, yy, xx, 1 - p.c), 2)
    def stages(self):
        return self.p.Z + 3
    def finish(self):
        for cond, f in self.pend:
            when(cond, f)

def sems_needed(dims, K):
    Z = dims[0]
    return K * (2 * (Z - 1) + 12 * (2 * Z - 1))


F32, BF16 = jnp.float32, jnp.bfloat16
TILE = 256
O_GAIN, O_SHIFT, O_OMEGA, O_AFF, O_REL = 0, 2 * D, 4 * D, 5 * D, 5 * D + 4 * Z
O_VB = O_REL + STRETCH
O_MXB = O_VB + VALUE_WIDTH
MXW = 2 * D + Z + VALUE_WIDTH
O_HB = O_MXB + MXW
O_UPB = O_HB + D
O_DNB = O_UPB + FF
O_EMA = O_DNB + D
C_LAT, C_RES, C_HX = D, D + Z, D + Z + VALUE_WIDTH


def sigmoid(v):
    return 0.5 * jnp.tanh(0.5 * v) + 0.5


def silu_slope(v, s):
    return s * (1.0 + v * (1.0 - s))


def col_sum(v):
    return jnp.sum(v, axis=0, keepdims=True)


def dot(a, b, ca=1, cb=0):
    return lax.dot_general(a, b, (((ca,), (cb,)), ((), ())), preferred_element_type=F32)


def tiles(lo, hi, step, f):
    @pl.loop(0, (hi - lo) // step)
    def _(i):
        f(pl.multiple_of(lo + i * step, 128))


def lane_block(l):
    return pl.ds(pl.multiple_of(l * 128, 128), 128)


def center(xf):
    c = xf - jnp.mean(xf, axis=-1, keepdims=True)
    r = lax.rsqrt(jnp.mean(c * c, axis=-1, keepdims=True) + epsilon)
    return c * r, r


def ema_rates(ema):
    gate, a = sigmoid(ema[0]), sigmoid(ema[1])
    retain = 1.0 - gate * a
    weight = gate * ema[2] * ema[3] * (1.0 / math.sqrt(H))
    return gate, a, retain, weight


def rel_table(rel_row):
    wide = jnp.broadcast_to(rel_row, (STRETCH, STRETCH))
    return pltpu.roll(wide, 0, 1, stride=1, stride_axis=0).T


def causal():
    i = lax.broadcasted_iota(jnp.int32, (STRETCH, STRETCH), 0)
    j = lax.broadcasted_iota(jnp.int32, (STRETCH, STRETCH), 1)
    return j <= i


class Forward:
    def __init__(self, x, valid, prow, ema, w, s):
        self.x, self.valid, self.prow, self.ema, self.w, self.s = x, valid, prow, ema, w, s
        self.m = x.shape[0]
        self.seqs = self.m // STRETCH

    def p(self, lo, n):
        return self.prow[:, lo : lo + n]

    def pd(self, lo, col, n):
        return self.prow[:, pl.ds(pl.multiple_of(lo + col, 128), n)]

    def norm_one(self):
        s = self.s
        g, b = self.p(O_GAIN, D), self.p(O_SHIFT, D)
        for q in range(self.seqs):
            s.mpad[q, 0:8, :] = jnp.zeros((8, D), F32)

            @pl.loop(0, STRETCH // 32)
            def _(i):
                r = pl.ds(q * STRETCH + i * 32, 32)
                xhat, _ = center(self.x[r, :].astype(F32))
                n = xhat * g + b
                s.normed[r, :] = n.astype(BF16)
                s.mpad[q, pl.ds(8 + i * 32, 32), :] = n * self.valid[r, 0:1]

    def ema_kernel(self):
        _, _, retain, weight = ema_rates(self.ema)

        def step(j, p):
            self.s.kern[pl.ds(j, 1), :] = col_sum(p)
            return p * retain

        lax.fori_loop(0, STRETCH, step, weight)

    def smooth(self, q):
        s = self.s
        for q in (q,):

            @pl.loop(0, D // 128)
            def _(l):
                lb = lane_block(l)
                om = self.prow[:, pl.ds(pl.multiple_of(O_OMEGA + l * 128, 128), 128)]
                nb = STRETCH // 8
                acc = [om * s.mpad[q, 8 + 8 * i : 16 + 8 * i, lb] for i in range(nb)]
                for b in range(8):
                    sh = [s.mpad[q, 8 - b + 8 * i : 16 - b + 8 * i, lb] for i in range(nb)]
                    for a in range(nb):
                        kb = jnp.broadcast_to(s.kern[8 * a + b : 8 * a + b + 1, lb], (8, 128))
                        for i in range(a, nb):
                            acc[i] = acc[i] + kb * sh[i - a]
                for i in range(nb):
                    r = slice(q * STRETCH + 8 * i, q * STRETCH + 8 * i + 8)
                    s.e[r, lb] = acc[i]

    def mix(self):
        s = self.s

        @pl.loop(0, self.m // 32)
        def _(i):
            r = pl.ds(i * 32, 32)
            e = s.e[r, :]
            s.mixed[r, :] = (e * sigmoid(e)).astype(BF16)

    def values(self):
        s = self.s

        def one(col):
            cols = pl.ds(col, TILE)
            v = dot(s.normed[...], self.w.v[:, cols]) + self.pd(O_VB, col, TILE)
            sv = sigmoid(v)
            s.vslope[:, cols] = silu_slope(v, sv).astype(BF16)
            s.val[:, cols] = (v * sv).astype(BF16)

        tiles(0, VALUE_WIDTH, TILE, one)

    def base(self):
        s = self.s

        def one(width):
            def f(col):
                cols = pl.ds(col, width)
                s.base[:, cols] = dot(s.mixed[...], self.w.mx[:, cols]) + self.pd(O_MXB, col, width)

            return f

        tiles(0, D, TILE, one(TILE))
        tiles(C_LAT, C_RES, Z, one(Z))
        tiles(C_RES, MXW, TILE, one(TILE))

    def attend(self):
        s = self.s
        table, mask = rel_table(self.p(O_REL, STRETCH)), causal()
        for q in range(self.seqs):
            r = slice(q * STRETCH, (q + 1) * STRETCH)
            b = s.base[r, C_LAT:C_RES]
            s.lat[r, :] = b
            lat = b * sigmoid(b)
            query = (lat * (1.0 + self.p(O_AFF, Z)) + self.p(O_AFF + 2 * Z, Z)).astype(BF16)
            keys = (lat * (1.0 + self.p(O_AFF + Z, Z)) + self.p(O_AFF + 3 * Z, Z)).astype(BF16)
            sc = jnp.where(mask, dot(query, keys, 1, 1) * (1.0 / math.sqrt(Z)) + table, -1e30)
            ex = jnp.exp(sc - jnp.max(sc, axis=-1, keepdims=True))
            pr = ex / jnp.sum(ex, axis=-1, keepdims=True)
            s.probs[r, :] = pr
            s.query[r, :] = query
            s.keys[r, :] = keys
            low = pr.astype(BF16)

            def one(col):
                cols = pl.ds(col, TILE)
                at = dot(low, s.val[r, cols])
                bb = s.base[r, pl.ds(pl.multiple_of(C_RES + col, 128), TILE)]
                sb = sigmoid(bb)
                res = bb * sb
                s.res[r, cols] = res.astype(BF16)
                s.ars[r, cols] = (at * silu_slope(bb, sb)).astype(BF16)
                s.gated[r, cols] = (at * res).astype(BF16)

            tiles(0, VALUE_WIDTH, TILE, one)

    def hidden(self):
        s = self.s

        def one(col):
            cols = pl.ds(col, TILE)
            h = dot(s.gated[...], self.w.h[:, cols]) + self.pd(O_HB, col, TILE)
            h = h + s.base[:, pl.ds(pl.multiple_of(C_HX + col, 128), TILE)]
            s.hpre[:, cols] = h
            xf = self.x[:, cols].astype(F32)
            u = sigmoid(s.base[:, cols])
            s.upd[:, cols] = u
            s.first[:, cols] = xf + self.valid[:, 0:1] * u * (h * sigmoid(h) - xf)

        tiles(0, D, TILE, one)

    def norm_two(self):
        s = self.s
        g, b = self.p(O_GAIN + D, D), self.p(O_SHIFT + D, D)

        @pl.loop(0, self.m // 32)
        def _(i):
            r = pl.ds(i * 32, 32)
            xhat, _ = center(s.first[r, :])
            s.second[r, :] = (xhat * g + b).astype(BF16)

    def up(self):
        s = self.s

        def one(col):
            cols = pl.ds(col, TILE)
            u = dot(s.second[...], self.w.up[:, cols]) + self.pd(O_UPB, col, TILE)
            su = sigmoid(u)
            s.uslope[:, cols] = silu_slope(u, su).astype(BF16)
            s.inner[:, cols] = (u * su).astype(BF16)

        tiles(0, FF, TILE, one)

    def down(self, out):
        s = self.s

        def one(col):
            cols = pl.ds(col, TILE)
            d = dot(s.inner[...], self.w.down[:, cols]) + self.pd(O_DNB, col, TILE)
            out[:, cols] = (s.first[:, cols] + self.valid[:, 0:1] * d).astype(BF16)

        tiles(0, D, TILE, one)


class Backward:
    def __init__(self, x, g, valid, prow, ema, w, s, t, grow, gema):
        self.x, self.g, self.valid, self.prow, self.ema = x, g, valid, prow, ema
        self.w, self.s, self.t, self.grow, self.gema = w, s, t, grow, gema
        self.m = x.shape[0]
        self.seqs = self.m // STRETCH

    p, pd = Forward.p, Forward.pd

    def put(self, lo, col, n, v):
        self.grow[:, pl.ds(pl.multiple_of(lo + col, 128), n)] = v

    def cot(self):
        def one(col):
            cols = pl.ds(col, TILE)
            d = self.valid[:, 0:1] * self.g[:, cols].astype(F32)
            self.put(O_DNB, col, TILE, col_sum(d))
            self.t.dd[:, cols] = d.astype(BF16)

        tiles(0, D, TILE, one)

    def d_up(self):
        s, t = self.s, self.t

        def one(col):
            cols = pl.ds(col, TILE)
            di = dot(t.dd[...], self.w.down[cols, :], 1, 1)
            du = di * s.uslope[:, cols].astype(F32)
            self.put(O_UPB, col, TILE, col_sum(du))
            t.dup[:, cols] = du.astype(BF16)

        tiles(0, FF, TILE, one)

    def d_second(self):
        t = self.t

        def one(col):
            cols = pl.ds(col, TILE)
            t.dsec[:, cols] = dot(t.dup[...], self.w.up[cols, :], 1, 1)

        tiles(0, D, TILE, one)

    def norm_two(self):
        s, t = self.s, self.t
        g = self.p(O_GAIN + D, D)
        t.acc[...] = jnp.zeros(t.acc.shape, F32)

        def add(k, v):
            t.acc[k] += jnp.sum(v.reshape(v.shape[0] // 8, 8, D), axis=0)

        @pl.loop(0, self.m // 32)
        def _(i):
            r = pl.ds(i * 32, 32)
            xhat, rstd = center(s.first[r, :])
            ds = t.dsec[r, :]
            add(0, ds * xhat)
            add(1, ds)
            dh = ds * g
            dn = rstd * (dh - jnp.mean(dh, axis=-1, keepdims=True) - xhat * jnp.mean(dh * xhat, axis=-1, keepdims=True))
            df = self.g[r, :].astype(F32) + dn
            v = self.valid[r, 0:1]
            u = s.upd[r, :]
            hp = s.hpre[r, :]
            sh = sigmoid(hp)
            xf = self.x[r, :].astype(F32)
            vu = v * u
            t.dx[r, :] = df - df * vu
            db = df * v * (hp * sh - xf) * u * (1.0 - u)
            add(2, db)
            t.dbase[r, 0:D] = db.astype(BF16)
            dhp = df * vu * silu_slope(hp, sh)
            add(3, dhp)
            t.dbase[r, C_HX:MXW] = dhp.astype(BF16)

        for k, lo in enumerate((O_GAIN + D, O_SHIFT + D, O_MXB, O_HB)):
            self.grow[:, lo : lo + D] = col_sum(t.acc[k])
        self.grow[:, O_MXB + C_HX : O_MXB + MXW] = col_sum(t.acc[3])

    def d_gated(self):
        s, t = self.s, self.t

        def one(col):
            cols = pl.ds(col, TILE)
            bcols = pl.ds(pl.multiple_of(C_RES + col, 128), TILE)
            dg = dot(t.dbase[:, C_HX:MXW], self.w.h[cols, :], 1, 1)
            t.datt[:, cols] = (dg * s.res[:, cols].astype(F32)).astype(BF16)
            db = dg * s.ars[:, cols].astype(F32)
            self.put(O_MXB + C_RES, col, TILE, col_sum(db))
            t.dbase[:, bcols] = db.astype(BF16)

        tiles(0, VALUE_WIDTH, TILE, one)

    def attend(self):
        s, t = self.s, self.t
        mask = causal()
        lows, drel = [], None
        aff = [0.0, 0.0, 0.0, 0.0]
        lat_bias = 0.0
        for q in range(self.seqs):
            r = slice(q * STRETCH, (q + 1) * STRETCH)
            pr = s.probs[r, :]
            lows.append(pr.astype(BF16))
            dp = dot(t.datt[r, :], s.val[r, :], 1, 1)
            ds = pr * (dp - jnp.sum(pr * dp, axis=-1, keepdims=True))
            ds = jnp.where(mask, ds, 0.0)
            drel = ds if drel is None else drel + ds
            raw = (ds * (1.0 / math.sqrt(Z))).astype(BF16)
            dq = dot(raw, s.keys[r, :])
            dk = dot(raw, s.query[r, :], 0, 0)
            b = s.lat[r, :]
            sb = sigmoid(b)
            lat = b * sb
            for k, v in enumerate((dq * lat, dk * lat, dq, dk)):
                aff[k] = aff[k] + col_sum(v)
            dl = dq * (1.0 + self.p(O_AFF, Z)) + dk * (1.0 + self.p(O_AFF + Z, Z))
            db = dl * silu_slope(b, sb)
            lat_bias = lat_bias + col_sum(db)
            t.dbase[r, C_LAT:C_RES] = db.astype(BF16)
        for k in range(4):
            self.grow[:, O_AFF + k * Z : O_AFF + (k + 1) * Z] = aff[k]
        self.grow[:, O_MXB + C_LAT : O_MXB + C_RES] = lat_bias
        drel = drel.T
        eight = 0.0
        for i in range(0, STRETCH, 8):
            eight = eight + pltpu.roll(drel[i : i + 8, :], (STRETCH - i) % STRETCH, 1)
        back = 0.0
        for i in range(8):
            back = back + pltpu.roll(eight[i : i + 1, :], (STRETCH - i) % STRETCH, 1)
        self.grow[:, O_REL : O_REL + STRETCH] = back

        def one(col):
            cols = pl.ds(col, TILE)
            bias = 0.0
            for q in range(self.seqs):
                r = slice(q * STRETCH, (q + 1) * STRETCH)
                dv = dot(lows[q], t.datt[r, cols], 0, 0)
                dv = dv * s.vslope[r, cols].astype(F32)
                bias = bias + col_sum(dv)
                t.dv[r, cols] = dv.astype(BF16)
            self.put(O_VB, col, TILE, bias)

        tiles(0, VALUE_WIDTH, TILE, one)

    def d_mixed(self):
        s, t = self.s, self.t
        for q in range(self.seqs):
            t.dpad[q, STRETCH : STRETCH + 8, :] = jnp.zeros((8, D), F32)

        def one(col):
            cols = pl.ds(col, TILE)
            dm = dot(t.dbase[...], self.w.mx[cols, :], 1, 1)
            e = s.e[:, cols]
            de = dm * silu_slope(e, sigmoid(e))
            om = 0.0
            for q in range(self.seqs):
                d = de[q * STRETCH : (q + 1) * STRETCH, :]
                t.dpad[q, 0:STRETCH, cols] = d
                om = om + col_sum(d * s.mpad[q, 8 : 8 + STRETCH, cols])
            self.put(O_OMEGA, col, TILE, om)

        tiles(0, D, TILE, one)

    def d_normed(self):
        t = self.t

        def one(col):
            cols = pl.ds(col, TILE)
            t.dn[:, cols] = dot(t.dv[...], self.w.v[cols, :], 1, 1)

        tiles(0, D, TILE, one)

    def smooth_signal(self, seq):
        s, t = self.s, self.t
        nb = STRETCH // 8

        @pl.loop(0, D // 128)
        def _(l):
            lb = lane_block(l)
            om = self.prow[:, pl.ds(pl.multiple_of(O_OMEGA + l * 128, 128), 128)]
            for q in (seq,):
                acc = [om * t.dpad[q, 8 * i : 8 * i + 8, lb] for i in range(nb)]
                for b in range(8):
                    sh = [t.dpad[q, 8 * i + b : 8 * i + b + 8, lb] for i in range(nb)]
                    for a in range(nb):
                        kb = jnp.broadcast_to(s.kern[8 * a + b : 8 * a + b + 1, lb], (8, 128))
                        for i in range(nb - a):
                            acc[i] = acc[i] + kb * sh[i + a]
                for i in range(nb):
                    r = slice(q * STRETCH + 8 * i, q * STRETCH + 8 * i + 8)
                    t.dn[r, lb] = t.dn[r, lb] + self.valid[r, :] * acc[i]

    def smooth_filter(self):
        s, t = self.s, self.t
        nb = STRETCH // 8

        @pl.loop(0, D // 128)
        def _(l):
            lb = lane_block(l)
            for b in range(8):
                sums = [None] * nb
                for q in range(self.seqs):
                    de = [t.dpad[q, 8 * i : 8 * i + 8, lb] for i in range(nb)]
                    sh = [s.mpad[q, 8 - b + 8 * i : 16 - b + 8 * i, lb] for i in range(nb)]
                    for a in range(nb):
                        for i in range(a, nb):
                            v = de[i] * sh[i - a]
                            sums[a] = v if sums[a] is None else sums[a] + v
                for a in range(nb):
                    t.dkern[8 * a + b : 8 * a + b + 1, lb] = col_sum(sums[a])

    def norm_one(self, out):
        t = self.t
        g = self.p(O_GAIN, D)
        t.acc[...] = jnp.zeros(t.acc.shape, F32)

        def add(k, v):
            t.acc[k] += jnp.sum(v.reshape(v.shape[0] // 8, 8, D), axis=0)

        @pl.loop(0, self.m // 32)
        def _(i):
            r = pl.ds(i * 32, 32)
            xhat, rstd = center(self.x[r, :].astype(F32))
            dn = t.dn[r, :]
            add(0, dn * xhat)
            add(1, dn)
            dh = dn * g
            d = rstd * (dh - jnp.mean(dh, axis=-1, keepdims=True) - xhat * jnp.mean(dh * xhat, axis=-1, keepdims=True))
            out[r, :] = (t.dx[r, :] + d).astype(BF16)

        for k, lo in enumerate((O_GAIN, O_SHIFT)):
            self.grow[:, lo : lo + D] = col_sum(t.acc[k])


    def ema_grads(self):
        t = self.t
        gate, a, retain, weight = ema_rates(self.ema)
        zero = retain - retain

        def step(j, carry):
            power, before, dw, dr = carry
            row = t.dkern[pl.ds(j, 1), :]
            dw = dw + row * power
            dr = dr + (row * j.astype(F32)) * before
            return power * retain, power, dw, dr

        _, _, dw, dr = lax.fori_loop(0, STRETCH, step, (zero + 1.0, zero, zero, zero))
        drate = -dr * weight
        scale = 1.0 / math.sqrt(H)
        dgate = drate * a + dw * self.ema[2] * self.ema[3] * scale
        self.gema[0] = dgate * gate * (1.0 - gate)
        self.gema[1] = drate * gate * a * (1.0 - a)
        self.gema[2] = dw * gate * self.ema[3] * scale
        self.gema[3] = dw * gate * self.ema[2] * scale


class Scatter:
    def __init__(self, place, grads, bufs, outs, send_sem, recv_sem, local_sem):
        self.p, self.grads, self.bufs, self.outs = place, grads, bufs, outs
        self.ss, self.rs, self.ls = send_sem, recv_sem, local_sem
        self.ids, self.pend = {}, []

    def copy(self, key, k, src, dst, to):
        i = self.ids.setdefault((key, k), len(self.ids))
        return pltpu.make_async_remote_copy(src_ref=src, dst_ref=dst, send_sem=self.ss.at[i], recv_sem=self.rs.at[i], device_id=(to,), device_id_type=MESH)

    def send(self, cond, key, k, src, dst, to):
        when(cond, lambda: self.copy(key, k, src, dst, to).start())
        self.pend.append((cond, lambda: self.copy(key, k, src, dst, to).wait_send()))

    def recv(self, cond, key, k, dst):
        when(cond, lambda: self.copy(key, k, dst, dst, self.p.me).wait_recv())

    def own(self, k, z):
        p, b = self.p, self.bufs[k]
        layer = p.Y * p.X
        i = k * p.Z + z
        return pltpu.make_async_copy(self.grads[k].at[pl.ds(z * layer, layer), p.c], b.mine.at[pl.ds((z % 2) * layer, layer)], self.ls.at[i])

    def add(self, dst, a, b, r0=0, rows=None):
        n = rows

        @pl.loop(0, n // 16)
        def _(i):
            def at(v, r):
                ref, q, off = v
                return ref.at[q, pl.ds(pl.multiple_of(off + r, 16), 16)]

            r = i * 16
            at(dst, r)[...] = at(a, r)[...] + at(b, r)[...]

    def stage(self, k, s):
        p, b = self.p, self.bufs[k]
        layer = p.Y * p.X
        r = b.sum.shape[1]
        half = r // 2
        chip = lambda z, y, x: (z * p.Y + y) * p.X + x
        col = lambda z: (chip(z, p.y, p.x), chip(z, p.y, 1 - p.x), chip(z, 1 - p.y, p.x), chip(z, 1 - p.y, 1 - p.x))
        L = p.Z
        planes = range(L)
        off = lambda z, d: p.z == z + d
        far = lambda z: jnp.logical_and(p.z != z - 1, p.z != z + 1)
        apart = lambda z: jnp.logical_and(far(z), p.z != z)
        S, H0, H1 = b.sum, 0, half
        if s == 0:
            for z in planes:
                self.send(None, ("c", z), k, self.grads[k].at[pl.ds(z * layer, layer), 1 - p.c], S.at[pl.ds(z * layer, layer)], p.nc)
                if z < 2:
                    self.own(k, z).start()
        if s == 1:
            for z in planes:
                self.recv(None, ("c", z), k, S.at[pl.ds(z * layer, layer)])
                self.own(k, z).wait()
                me, nx, ny, nd = col(z)
                back = (z - z % 2) * layer
                self.add((S, nd, 0), (S, nd, 0), (b.mine, nd - back, 0), rows=r)
                self.send(None, ("dy", z), k, S.at[nd, pl.ds(0, half)], b.dy.at[z], p.ny)
                self.send(None, ("dx", z), k, S.at[nd, pl.ds(half, half)], b.dx.at[z], p.nx)
                for q in (nx, ny, me):
                    self.add((S, q, 0), (S, q, 0), (b.mine, q - back, 0), rows=r)
                if z + 2 < L:
                    self.own(k, z + 2).start()
        if s == 2:
            for z in planes:
                me, nx, ny, nd = col(z)
                for key, q, h, buf, to, out in (("dy", nx, H0, b.dy, p.nx, b.rx), ("dx", ny, H1, b.dx, p.ny, b.ry)):
                    self.recv(None, (key, z), k, buf.at[z])
                    self.add((S, q, h), (S, q, h), (buf, z, 0), rows=half)
                    tag = "x" if key == "dy" else "y"
                    side = 0 if key == "dy" else 1
                    self.send(apart(z), (tag, z), k, S.at[q], out.at[z], to)
                    if z > 0:
                        self.send(off(z, -1), ("z" + tag, 0), k, S.at[q], b.rz.at[side], p.up)
                    if z < L - 1:
                        self.send(off(z, 1), ("z" + tag, 1), k, S.at[q], b.rz.at[2 + side], p.down)
        if s == 3:
            me, nx, ny, nd = col(p.z)
            for tag, q, side, to, out in (("x", nx, 0, p.nx, b.rx), ("y", ny, 1, p.ny, b.ry)):
                for cond, way in ((p.has_down, 0), (p.has_up, 1)):

                    def take(q=q, side=side, way=way, tag=tag):
                        self.copy(("z" + tag, way), k, b.rz.at[2 * way + side], b.rz.at[2 * way + side], p.me).wait_recv()
                        self.add((S, q, 0), (S, q, 0), (b.rz, 2 * way + side, 0), rows=r)

                    pl.when(cond)(take)
                for z in planes:
                    self.send(p.z == z, (tag, z), k, S.at[q], out.at[z], to)
        if s == 4:
            for z in planes:
                me = col(z)[0]
                for tag, buf in (("y", b.ry), ("x", b.rx)):

                    def take(me=me, tag=tag, buf=buf, z=z):
                        self.copy((tag, z), k, buf.at[z], buf.at[z], p.me).wait_recv()
                        self.add((S, me, 0), (S, me, 0), (buf, z, 0), rows=r)

                    pl.when(far(z))(take)
        if 4 <= s < 4 + L - 1:
            hop = s - 4
            for up in (True, False):
                zz = hop if up else L - 1 - hop
                buf, key, to = (b.ru, "u", p.up) if up else (b.rd, "d", p.down)
                here = p.z == zz
                for t in range(L - 1, zz, -1) if up else range(0, zz):
                    q = chip(t, p.y, p.x)

                    def relay(q=q, t=t, buf=buf, key=key):
                        self.copy((key, t), k, buf.at[t], buf.at[t], p.me).wait_recv()
                        self.add((S, q, 0), (S, q, 0), (buf, t, 0), rows=r)

                    if hop > 0:
                        pl.when(here)(relay)
                    self.send(here, (key, t), k, S.at[q], buf.at[t], to)
        if s == 4 + L - 1:
            me = chip(p.z, p.y, p.x)
            out = self.outs[k]

            @pl.loop(0, r // 16)
            def _(i):
                rr = pl.ds(pl.multiple_of(i * 16, 16), 16)
                out[rr, :] = S[me, rr, :].astype(F32)

            for buf, key in ((b.ru, "u"), (b.rd, "d")):
                for t in range(1, L) if key == "u" else range(0, L - 1):

                    def last(buf=buf, key=key, t=t):
                        self.copy((key, t), k, buf.at[t], buf.at[t], p.me).wait_recv()

                        @pl.loop(0, r // 16)
                        def _(i):
                            rr = pl.ds(pl.multiple_of(i * 16, 16), 16)
                            out[rr, :] += buf[t, rr, :].astype(F32)

                    pl.when(p.z == t)(last)

    def stages(self):
        return 4 + self.p.Z

    def finish(self):
        for cond, f in self.pend:
            when(cond, f)


class Names:
    def __init__(self, **kw):
        self.__dict__.update(kw)


SCATTER_BUFS = ("mine", "sum", "dx", "dy", "rx", "ry", "ru", "rd", "rz")


def scatter_scratch(dims, r, w):
    Z, Y, X = dims
    chips = Z * Y * X
    shapes = ((2 * Y * X, r, w), (chips, r, w), (Z, r // 2, w), (Z, r // 2, w), (Z, r, w), (Z, r, w), (Z, r, w), (Z, r, w), (4, r, w))
    return [pltpu.VMEM(s, BF16) for s in shapes]


def scatter_sems(dims, K):
    Z = dims[0]
    return K * (7 * Z + 4)


def rs_kernel(dims, K, *refs):
    grads, outs = refs[:K], refs[K : 2 * K]
    nb = len(SCATTER_BUFS)
    bufs = [Names(**dict(zip(SCATTER_BUFS, refs[2 * K + nb * k : 2 * K + nb * (k + 1)]))) for k in range(K)]
    ss, rs, ls = refs[2 * K + nb * K :]
    p = Place(dims)
    p.barrier()
    sc = Scatter(p, grads, bufs, outs, ss, rs, ls)
    S = sc.stages()
    for t in range(K + S - 1):
        for k in range(K):
            if 0 <= t - k < S:
                sc.stage(k, t - k)
    sc.finish()


def scatter(dims, grads, cid):
    K = len(grads)
    n = 2 * dims[0] * dims[1] * dims[2]
    shaped = [g.reshape(n // 2, 2, g.shape[0] // n, g.shape[1]) for g in grads]
    scratch = []
    for g in shaped:
        scratch += scatter_scratch(dims, g.shape[2], g.shape[3])
    ns = scatter_sems(dims, K)
    return pl.pallas_call(
        functools.partial(rs_kernel, dims, K),
        out_shape=[jax.ShapeDtypeStruct(g.shape[2:], F32) for g in shaped],
        in_specs=[pl.BlockSpec(memory_space=pl.ANY)] * K,
        out_specs=[pl.BlockSpec(memory_space=pltpu.VMEM)] * K,
        scratch_shapes=scratch + [pltpu.SemaphoreType.DMA((ns,)), pltpu.SemaphoreType.DMA((ns,)), pltpu.SemaphoreType.DMA((K * dims[0],))],
        compiler_params=pltpu.CompilerParams(collective_id=cid, has_side_effects=True, vmem_limit_bytes=64 * 1024 * 1024),
    )(*shaped)


KEPT_OLD = ("normed", "mpad", "e", "mixed", "kern", "vslope", "val", "base", "probs", "query", "keys", "att", "gated", "hpre", "first", "second", "uslope", "inner")


def kept_shapes(m):
    seqs = m // STRETCH
    f, b = (lambda *s: (s, F32)), (lambda *s: (s, BF16))
    return dict(
        normed=b(m, D), mpad=f(seqs, STRETCH + 8, D), e=f(m, D), mixed=b(m, D), kern=f(STRETCH, D),
        vslope=b(m, VALUE_WIDTH), val=b(m, VALUE_WIDTH), base=f(m, MXW), probs=f(m, STRETCH),
        query=b(m, Z), keys=b(m, Z), upd=f(m, D), lat=f(m, Z), res=b(m, VALUE_WIDTH), ars=b(m, VALUE_WIDTH), gated=b(m, VALUE_WIDTH), hpre=f(m, D),
        first=f(m, D), second=b(m, D), uslope=b(m, FF), inner=b(m, FF),
    )


VM = pltpu.VMEM
LIMIT = 64 * 1024 * 1024


def weight_grad(a, b, n, out, stage, sem, lo=0):
    flat = len(out.shape) == 2
    r = out.shape[-2]
    block = stage.shape[1]
    count = (out.shape[0] if flat else out.shape[0] * 2 * r) // block
    per = block // r

    def start(i, slot):
        if flat:
            pltpu.make_async_copy(stage.at[slot, :, 0:n], out.at[pl.ds(pl.multiple_of(i * block, block), block)], sem.at[slot]).start()
        for q in range(0 if flat else per):
            d = i * per + q
            pltpu.make_async_copy(stage.at[slot, pl.ds(q * r, r), 0:n], out.at[d // 2, d % 2], sem.at[slot]).start()

    def wait(slot):
        whole = stage.at[slot, :, 0:n]
        pltpu.make_async_copy(whole, whole, sem.at[slot]).wait()

    @pl.loop(0, count // 2)
    def _(j):
        for slot in range(2):
            i = j * 2 + slot

            @pl.when(j > 0)
            def _():
                wait(slot)

            rows = a[:, pl.ds(pl.multiple_of(i * block, block), block)]
            for c in range(0, n, 1024):
                wd = min(1024, n - c)
                stage[slot, :, c : c + wd] = dot(rows, b[:, lo + c : lo + c + wd], 0, 0).astype(BF16)
            start(i, slot)

    for slot in range(2):
        wait(slot)


def own_shapes(m):
    seqs = m // STRETCH
    return dict(
        dd=((m, D), BF16), acc=((4, 8, D), F32), dx=((m, D), F32),
        dbase=((m, MXW), BF16), datt=((m, VALUE_WIDTH), BF16), dv=((m, VALUE_WIDTH), BF16),
        dpad=((seqs, STRETCH + 8, D), F32), dn=((m, D), F32), dkern=((STRETCH, D), F32),
    )


SMALL_ROWS = 32
FRAME = 24


def frames(n, count):
    return [(count * d) // 128 for d in range(n)]


def spread(k):
    p = lax.broadcasted_iota(jnp.int32, (D, TILE), 0)
    c = lax.broadcasted_iota(jnp.int32, (D, TILE), 1) + k * TILE
    return (c == 8 * (p % 128) + p // 128).astype(BF16)


def unpack_params(n, count, packed, full, prow, ema):
    full[...] = jnp.zeros(full.shape, F32)
    for d, r in enumerate(frames(n, count)):
        full[r : r + FRAME, :] += packed[d * SMALL_ROWS : d * SMALL_ROWS + FRAME, :].astype(F32)
    for i in range(O_EMA // 128):
        prow[:, i * 128 : (i + 1) * 128] = full[i : i + 1, :]
    rows = []
    for j in range(4):
        lo = O_EMA // 128 + j * D * H // 128
        t = full[lo : lo + 128, :].T
        rows.append(jnp.concatenate([t[H * k : H * (k + 1), :] for k in range(8)], axis=1))
    stack = jnp.concatenate(rows, axis=0).astype(BF16)
    for k in range(D // TILE):
        e = dot(stack, spread(k))
        for j in range(4):
            ema[j, :, k * TILE : (k + 1) * TILE] = e[j * H : (j + 1) * H, :]


def pack_grads(n, count, grow, gema, full, out):
    for i in range(O_EMA // 128):
        full[i : i + 1, :] = grow[:, i * 128 : (i + 1) * 128]
    stack = jnp.concatenate([gema[j] for j in range(4)], axis=0).astype(BF16)
    back = 0.0
    for k in range(D // TILE):
        back = back + dot(stack[:, k * TILE : (k + 1) * TILE], spread(k), 1, 1)
    for j in range(4):
        e = back[j * H : (j + 1) * H, :]
        lo = O_EMA // 128 + j * D * H // 128
        full[lo : lo + 128, :] = jnp.concatenate([e[:, k * 128 : (k + 1) * 128] for k in range(8)], axis=0).T
    for d, r in enumerate(frames(n, count)):
        out[d // 2, d % 2, 0:FRAME, :] = full[r : r + FRAME, :].astype(BF16)
        out[d // 2, d % 2, FRAME:SMALL_ROWS, :] = jnp.zeros((SMALL_ROWS - FRAME, 128), BF16)


def size_table(n, count, m):
    rows = -(-(-(-(n * count) // 128) + FRAME) // 8) * 8
    table = {k: v for k, v in list(kept_shapes(m).items()) + list(own_shapes(m).items())}
    table.update(
        out=((m, D), BF16), dxo=((m, D), BF16), grow=((1, O_EMA), F32), prow=((1, O_EMA), F32), ema=((4, H, D), F32),
        gema=((4, H, D), F32), full=((rows, 128), F32), packed=((n * SMALL_ROWS, 128), BF16),
        gsmall=((n // 2, 2, SMALL_ROWS, 128), BF16), wr=((FF, D), BF16), wc=((D, MXW), BF16), wv=((D, VALUE_WIDTH), BF16),
        wup=((D, FF), BF16), stage=((2, TILE // 2, MXW), BF16),
    )
    return table


class Parts:
    def __init__(self, refs):
        self.refs = list(refs)

    def take(self, names):
        got, self.refs = self.refs[: len(names)], self.refs[len(names) :]
        return dict(zip(names, got))

    def rest(self, k):
        got, self.refs = self.refs[:k], self.refs[k:]
        return got


SAVED = dict(
    front=("inner", "uslope", "first", "hpre", "second", "dd", "upd", "lat", "res", "ars", "gated", "val", "vslope", "probs", "query", "keys", "mixed", "normed", "e", "mpad", "kern", "grow", "prow", "ema"),
    mid=("dbase", "dv", "dx", "grow"),
    back=(),
)
LOADED = dict(
    mid=("inner", "uslope", "first", "hpre", "second", "dd", "upd", "lat", "res", "ars", "gated", "val", "vslope", "probs", "query", "keys", "grow", "prow"),
    back=("dbase", "dv", "dx", "grow", "mixed", "normed", "e", "mpad", "kern", "prow", "ema"),
)
HELD = dict(
    front=SAVED["front"] + ("base", "full", "packed", "wr", "wc", "wv", "stage"),
    mid=LOADED["mid"] + ("dbase", "dn", "acc", "wr", "wup", "stage"),
    back=LOADED["back"] + ("dpad", "dn", "dkern", "acc", "gema", "full", "gsmall", "wc", "wv", "stage"),
)


class Store:
    def __init__(self, kind, r, ins, outs):
        held = r.take(HELD[kind])
        self.s = Names(**held)
        self.held = held
        self.ins, self.outs = ins, outs
        self.in_sem, self.out_sem = r.rest(2)
        self.names_in, self.names_out = list(ins), list(outs)
        self.seen, self.begun = set(), []

    def fetch(self):
        for k in self.names_in:
            self.copy_in(k).start()

    def copy_in(self, k):
        return pltpu.make_async_copy(self.ins[k], self.held[k], self.in_sem.at[self.names_in.index(k)])

    def need(self, *names):
        for k in names:
            if k not in self.seen:
                self.copy_in(k).wait()
                self.seen.add(k)

    def copy_out(self, k):
        return pltpu.make_async_copy(self.held[k], self.outs[k], self.out_sem.at[self.names_out.index(k)])

    def save(self, *names):
        for k in names:
            self.copy_out(k).start()
            self.begun.append(k)

    def close(self):
        self.need(*self.names_in)
        self.save(*[k for k in self.names_out if k not in self.begun])
        for k in self.begun:
            self.copy_out(k).wait()


def front_kernel(dims, n, count, *refs):
    r = Parts(refs)
    x, g, valid = r.rest(3)
    ins = r.rest(6)
    outs = r.take(SAVED["front"])
    gdown = r.rest(1)[0]
    whole = [None] + r.rest(5) if dims else ins
    st = Store("front", r, {}, outs)
    s = st.s
    lsem, ssem = r.rest(2)
    small = pltpu.make_async_copy(ins[0], s.packed, lsem.at[0])
    if dims:
        osem, gsend, grecv, send_sem, recv_sem = r.rest(5)
        p = Place(dims)
        p.barrier_all(n)
        mine = pl.ds(p.me * SMALL_ROWS, SMALL_ROWS)
        own = pltpu.make_async_copy(ins[0], s.packed.at[mine], lsem.at[0])
        own.start()

        def tell(i, dev, block):
            return pltpu.make_async_remote_copy(
                src_ref=ins[0], dst_ref=s.packed.at[pl.ds(block * SMALL_ROWS, SMALL_ROWS)], send_sem=gsend.at[i], recv_sem=grecv.at[i],
                device_id=(dev,), device_id_type=MESH,
            )

        @pl.loop(1, n)
        def _(i):
            tell(i, (p.me + i) % n, p.me).start()

        gat = Gather(p, ins[1:], whole[1:], send_sem, recv_sem)
        cps = [pltpu.make_async_copy(i, o.at[pl.ds(p.me * i.shape[0], i.shape[0])], osem.at[k]) for k, (i, o) in enumerate(zip(ins[1:], whole[1:]))]
        for cp in cps:
            cp.start()
        last = gat.stages() - 1

        def step(t):
            for k in range(5):
                if 0 <= t - k <= last:
                    gat.stage(k, t - k)
                    if t - k == last:
                        cps[k].wait()

        def small_here():
            own.wait()

            @pl.loop(1, n)
            def _(i):
                tell(i, p.me, (p.me - i + n) % n).wait()
    else:
        step = lambda t: None

        def small_here():
            small.start()
            small.wait()

    S = dims[0] + 2 if dims else 6
    w = Names(v=s.wv, mx=s.wc, h=s.wr.at[0:VALUE_WIDTH], up=s.wc.at[:, 0:FF])
    into = (None, s.wv, s.wc, s.wr.at[0:VALUE_WIDTH], s.wc.at[:, 0:FF])
    load = [None] + [pltpu.make_async_copy(whole[i], into[i], lsem.at[i]) for i in range(1, 5)]
    f = Forward(x, valid, s.prow, s.ema, w, s)
    b = Backward(x, g, valid, s.prow, s.ema, w, s, s, s.grow, None)
    b.grow[...] = jnp.zeros(b.grow.shape, F32)
    step(0)
    b.cot()
    step(1)
    small_here()
    unpack_params(n, count, s.packed, s.full, s.prow, s.ema)
    f.norm_one()
    step(2)
    f.ema_kernel()
    step(3)
    f.smooth(0)
    step(4)
    f.smooth(1)
    f.mix()
    st.save("normed", "mixed", "e", "mpad", "kern", "prow", "ema", "dd", "grow")
    for t in range(5, S):
        step(t)
    step(S)
    load[1].start()
    load[1].wait()
    f.values()
    st.save("val", "vslope")
    step(S + 1)
    load[2].start()
    load[2].wait()
    f.base()
    f.attend()
    st.save("lat", "res", "ars", "gated", "probs", "query", "keys")
    step(S + 2)
    load[3].start()
    load[3].wait()
    f.hidden()
    st.save("first", "hpre", "upd")
    f.norm_two()
    st.save("second")
    step(S + 3)
    load[4].start()
    load[4].wait()
    f.up()
    st.save("inner", "uslope")
    weight_grad(s.inner, s.dd, D, gdown, s.stage, ssem)
    step(S + 4)
    if dims:
        gat.finish()
    st.close()


def make_scatter(dims, parts, grads, outs):
    nb = len(SCATTER_BUFS)
    bufs = [Names(**dict(zip(SCATTER_BUFS, parts.rest(nb)))) for _ in grads]
    p = Place(dims)
    p.barrier()
    return Scatter(p, grads, bufs, outs, *parts.rest(3))


def columns(ref, w):
    pieces, lo = [], 0
    for q in w:
        pieces.append(ref.at[(slice(None),) * (len(ref.shape) - 1) + (pl.ds(lo, q),)])
        lo += q
    return pieces


def mid_kernel(dims, *refs):
    r = Parts(refs)
    x, g, valid, h, up, down = r.rest(6)
    gdown = r.rest(1)[0]
    ins = r.take(LOADED["mid"])
    out = r.rest(1)[0]
    outs = r.take(SAVED["mid"])
    gup, gh = r.rest(2)
    reduced = r.rest(2) if dims else []
    st = Store("mid", r, ins, outs)
    s = st.s
    s.datt, s.dv, s.dx, s.dup, s.dsec = s.gated, s.vslope, s.first, s.inner, s.dn
    st.held.update(dv=s.dv, dx=s.dx)
    lsem, ssem = r.rest(2)
    load_down = pltpu.make_async_copy(down, s.wr, lsem.at[0])
    load_up = pltpu.make_async_copy(up, s.wup, lsem.at[1])
    load_h = pltpu.make_async_copy(h, s.wr.at[0:VALUE_WIDTH], lsem.at[2])
    load_down.start()
    st.fetch()
    load_up.start()
    if dims:
        cut = ((D // 2, D // 2), (FF // 2, FF // 2))
        grads = columns(gdown, cut[0]) + columns(gup, cut[1])
        sc = make_scatter(dims, r, grads, columns(reduced[0], cut[0]) + columns(reduced[1], cut[1]))
        S = sc.stages()
        late = 3
        start = (0, 1, late, late + 1)

        def step(t):
            for k in range(4):
                if 0 <= t - start[k] < S:
                    sc.stage(k, t - start[k])
    else:
        S, late = 8, 3
        step = lambda t: None
    w = Names(h=s.wr.at[0:VALUE_WIDTH], up=s.wup, down=s.wr)
    f = Forward(x, valid, s.prow, None, w, s)
    b = Backward(x, g, valid, s.prow, None, w, s, s, s.grow, None)
    step(0)
    st.need("inner", "uslope", "first", "dd", "prow", "grow")
    load_down.wait()
    f.down(out)
    step(1)
    b.d_up()
    load_h.start()
    step(2)
    st.need("second")
    weight_grad(s.second, s.dup, FF, gup, s.stage, ssem)
    step(3)
    load_up.wait()
    b.d_second()
    step(4)
    st.need("hpre", "upd")
    b.norm_two()
    st.save("dx")
    step(5)
    st.need("gated")
    weight_grad(s.gated, s.dbase, D, gh, s.stage, ssem, lo=C_HX)
    step(6)
    load_h.wait()
    st.need("res", "ars")
    b.d_gated()
    step(7)
    st.need("lat", "val", "vslope", "probs", "query", "keys")
    b.attend()
    st.save("dbase", "dv", "grow")
    for t in range(8, late + 1 + S):
        step(t)
    if dims:
        sc.finish()
    st.close()


def back_kernel(dims, n, count, *refs):
    r = Parts(refs)
    x, valid, v, mx = r.rest(4)
    gh = r.rest(1)[0]
    ins = r.take(LOADED["back"])
    dxo = r.rest(1)[0]
    gmx, gv = r.rest(2)
    reduced = r.rest(4) if dims else r.rest(1)
    st = Store("back", r, ins, {})
    s = st.s
    lsem, ssem = r.rest(2)
    l_mx = pltpu.make_async_copy(mx, s.wc, lsem.at[0])
    l_v = pltpu.make_async_copy(v, s.wv, lsem.at[1])
    st.fetch()
    l_mx.start()
    l_v.start()
    start = (0, 2, 3, 2, 10)
    if dims:
        cut = (VALUE_WIDTH, MXW - VALUE_WIDTH)
        split = (n // 2, 2, D // n)
        gmx4, gv4 = gmx, gv
        grads = [gh] + columns(gmx4, cut) + [gv4, s.gsmall]
        sc = make_scatter(dims, r, grads, [reduced[0]] + columns(reduced[1], cut) + [reduced[2], reduced[3]])
        S = sc.stages()

        def step(t):
            for k in range(5):
                if 0 <= t - start[k] < S:
                    sc.stage(k, t - start[k])
    else:
        S = 8
        step = lambda t: None
    b = Backward(x, None, valid, s.prow, s.ema, Names(mx=s.wc, v=s.wv), s, s, s.grow, s.gema)
    step(0)
    st.need("dv", "normed", "prow", "grow")
    weight_grad(s.normed, s.dv, VALUE_WIDTH, gv, s.stage, ssem)
    step(1)
    st.need("dbase", "mixed")
    weight_grad(s.mixed, s.dbase, MXW, gmx, s.stage, ssem)
    step(2)
    l_mx.wait()
    st.need("e", "mpad")
    b.d_mixed()
    step(3)
    l_v.wait()
    b.d_normed()
    step(4)
    st.need("kern")
    b.smooth_signal(0)
    step(5)
    b.smooth_signal(1)
    step(6)
    b.smooth_filter()
    step(7)
    st.need("ema")
    b.ema_grads()
    step(8)
    st.need("dx")
    b.norm_one(dxo)
    step(9)
    pack_grads(n, count, s.grow, s.gema, s.full, s.gsmall)
    for t in range(10, start[4] + S):
        step(t)
    if dims:
        sc.finish()
    else:
        reduced[0][...] = s.gsmall[...]
    st.close()


def scatter_parts(dims, shapes):
    scratch = []
    for q in shapes:
        scratch += scatter_scratch(dims, q[0], q[1])
    ns = scatter_sems(dims, len(shapes))
    return scratch + [pltpu.SemaphoreType.DMA((ns,)), pltpu.SemaphoreType.DMA((ns,)), pltpu.SemaphoreType.DMA((len(shapes) * dims[0],))]


def run_kernel(body, ins, outs, scratch, cid):
    vm, hbm = pl.BlockSpec(memory_space=VM), pl.BlockSpec(memory_space=pl.ANY)
    params = dict(vmem_limit_bytes=LIMIT)
    if cid is not None:
        params.update(collective_id=cid, has_side_effects=True)
    return pl.pallas_call(
        body,
        out_shape=[jax.ShapeDtypeStruct(o[0], o[1]) for o in outs],
        in_specs=[vm if i[1] else hbm for i in ins],
        out_specs=[vm if o[2] else hbm for o in outs],
        scratch_shapes=scratch,
        compiler_params=pltpu.CompilerParams(**params),
    )(*[i[0] for i in ins])


def copy_kernel(k, *refs):
    ins, outs, bufs, sem = refs[:k], refs[k : 2 * k], refs[2 * k : 3 * k], refs[3 * k]
    get = [pltpu.make_async_copy(a, b, sem.at[i]) for i, (a, b) in enumerate(zip(ins, bufs))]
    put = [pltpu.make_async_copy(a, b, sem.at[k + i]) for i, (a, b) in enumerate(zip(bufs, outs))]
    for c in get:
        c.start()
    for c, d in zip(get, put):
        c.wait()
        d.start()
    for d in put:
        d.wait()


def settle(arrays):
    return run_kernel(
        functools.partial(copy_kernel, len(arrays)), [(a, False) for a in arrays], [(a.shape, a.dtype, False) for a in arrays],
        [VM(a.shape, a.dtype) for a in arrays] + [pltpu.SemaphoreType.DMA((2 * len(arrays),))], None,
    )


def layer(dims, n, count, x, g, valid, arrays):
    m = x.shape[0]
    table = size_table(n, count, m)
    dma = pltpu.SemaphoreType.DMA
    tmp = lambda names: [VM(*table[k]) for k in names]
    saved = lambda kind: [table[k] + (False,) for k in SAVED[kind]]
    whole = [(n * a.shape[0], a.shape[1]) if dims else a.shape for a in arrays]
    parts = [(q[0] // n, q[1]) for q in whole]
    split = lambda a: a.reshape(n // 2, 2, a.shape[0] // n, a.shape[1])
    four = lambda i: (n // 2, 2) + parts[i]
    held = lambda kind, k: tmp(HELD[kind]) + [dma((max(1, len(LOADED.get(kind, ()))),)), dma((max(1, len(SAVED[kind])),))] + [dma((k,)), dma((2,))]
    a = {}

    scratch = held("front", 6)
    o = saved("front") + [(whole[5], BF16, False)]
    if dims:
        ns = sems_needed(dims, 5)
        scratch += [dma((5,)), dma((n,)), dma((n,)), dma((ns,)), dma((ns,))]
        o += [(q, BF16, False) for q in whole[1:]]
    ins = [(x, True), (g, True), (valid, True)] + [(q, False) for q in arrays]
    res = run_kernel(functools.partial(front_kernel, dims, n, count), ins, o, scratch, 0 if dims else None)
    a.update(zip(SAVED["front"], res))
    res = res[len(SAVED["front"]) :]
    gdown = res[0]
    v, mx, h, up, down = res[1:] if dims else arrays[1:]

    ins = [(x, True), (g, True), (valid, True), (h, False), (up, False), (down, False), (split(gdown), False)]
    ins += [(a[k], False) for k in LOADED["mid"]]
    o = [((m, D), BF16, True)] + saved("mid") + [(four(4), BF16, False), (four(3), BF16, False)]
    scratch = held("mid", 3)
    if dims:
        o += [(parts[5], F32, True), (parts[4], F32, True)]
        scratch += scatter_parts(dims, ((parts[5][0], D // 2),) * 2 + ((parts[4][0], FF // 2),) * 2)
    res = run_kernel(functools.partial(mid_kernel, dims), ins, o, scratch, 1 if dims else None)
    out = res[0]
    a.update(zip(SAVED["mid"], res[1:]))
    gup, gh = res[5:7]
    if dims:
        gdown, gup = res[7:]

    ins = [(x, True), (valid, True), (v, False), (mx, False), (gh, False)] + [(a[k], False) for k in LOADED["back"]]
    o = [((m, D), BF16, True), (four(2), BF16, False), (four(1), BF16, False)]
    scratch = held("back", 2)
    if dims:
        o += [(parts[i], F32, True) for i in (3, 2, 1)] + [((SMALL_ROWS, 128), F32, True)]
        rows = parts[2][0]
        scratch += scatter_parts(dims, (parts[3], (rows, VALUE_WIDTH), (rows, MXW - VALUE_WIDTH), parts[1], (SMALL_ROWS, 128)))
    else:
        o += [table["gsmall"] + (True,)]
    res = run_kernel(functools.partial(back_kernel, dims, n, count), ins, o, scratch, 2 if dims else None)
    if dims:
        gh, gmx, gv, gs = res[3:]
    else:
        gmx, gv = res[1:3]
        gs = res[3]
        gv, gmx, gh, gup, gs = (q.reshape(-1, q.shape[-1]) for q in (gv, gmx, gh, gup, gs))
    return out, res[0], gv, gmx, gh, gup, gdown, gs


def frame_in(small, me):
    count = small.shape[0]
    line = lax.dynamic_update_slice(jnp.zeros((FRAME * 128,), small.dtype), small, ((me * count) % 128,))
    return jnp.pad(line.reshape(FRAME, 128), ((0, SMALL_ROWS - FRAME), (0, 0)))


def frame_out(block, me, count):
    return lax.dynamic_slice(block.reshape(-1), ((me * count) % 128,), (count,))


def grid_of(n):
    return (n // 8, 2, 2)


def per_device(n, inputs, lengths, cotangent, v_weight, mx_weight, h_weight, up_weight, down_weight, small_params):
    shape = inputs.shape
    m, count = shape[0] * shape[1] * shape[2], small_params.shape[0]
    me = lax.axis_index("fsdp")
    x, g = inputs.reshape(m, D), cotangent.reshape(m, D)
    mask = (jnp.arange(shape[2]) < lengths[:, :, None]).astype(F32).reshape(m, 1)
    valid = jnp.broadcast_to(mask, (m, 128))
    arrays = (frame_in(small_params, me), v_weight, mx_weight, h_weight, up_weight, down_weight)
    dims = grid_of(n) if n == 32 else None
    if not dims:
        arrays = [lax.all_gather(a, "fsdp", axis=0, tiled=True) for a in arrays]
    out, dx, gv, gmx, gh, gup, gdown, gs = layer(dims, n, count, x, g, valid, arrays)
    if dims:
        out, dx, gv, gmx, gh, gup, gdown = settle((out, dx, gv, gmx, gh, gup, gdown))
    else:
        gv, gmx, gh, gup, gdown, gs = (
            lax.psum_scatter(a.astype(F32), "fsdp", scatter_dimension=0, tiled=True) for a in (gv, gmx, gh, gup, gdown, gs)
        )
    return out.reshape(shape), dx.reshape(shape), gv, gmx, gh, gup, gdown, frame_out(gs, me, count)


def solution(mesh):
    rows, cols = P("fsdp", None), P(None, "fsdp", None, None)
    return jax.shard_map(
        functools.partial(per_device, mesh.shape["fsdp"]),
        mesh=mesh,
        in_specs=(cols, P(None, "fsdp"), cols, rows, rows, rows, rows, rows, P("fsdp")),
        out_specs=(cols, cols, rows, rows, rows, rows, rows, P("fsdp")),
        check_vma=False,
    )
```

```python
import functools
import math

import jax
import jax.numpy as jnp
from jax import lax
from jax.experimental import pallas as pl
from jax.experimental.pallas import tpu as pltpu
from jax.sharding import PartitionSpec as P

D = 1024
Z = 128
VALUE_WIDTH = 2048
H = 16
FF = 4096
STRETCH = 128


epsilon = 1e-05

MESH = pl.DeviceIdType.MESH

class Place:
    def __init__(self, dims):
        self.Z, self.Y, self.X = dims
        me = lax.axis_index("fsdp")
        self.me = me
        self.c = me % 2
        self.x = (me // 2) % self.X
        self.y = (me // (2 * self.X)) % self.Y
        self.z = me // (2 * self.X * self.Y)
        self.nx = self.dev(self.z, self.y, 1 - self.x, self.c)
        self.ny = self.dev(self.z, 1 - self.y, self.x, self.c)
        self.nc = self.dev(self.z, self.y, self.x, 1 - self.c)
        self.has_down = self.z > 0
        self.has_up = self.z < self.Z - 1
        self.down = self.dev(jnp.maximum(self.z - 1, 0), self.y, self.x, self.c)
        self.up = self.dev(jnp.minimum(self.z + 1, self.Z - 1), self.y, self.x, self.c)
    def dev(self, z, y, x, c):
        return ((z * self.Y + y) * self.X + x) * 2 + c
    def barrier(self):
        bar = pltpu.get_barrier_semaphore()
        def tell(d):
            pl.semaphore_signal(bar, inc=1, device_id=(d,), device_id_type=MESH)
        for d in (self.nx, self.ny, self.nc):
            tell(d)
        pl.when(self.has_down)(lambda: tell(self.down))
        pl.when(self.has_up)(lambda: tell(self.up))
        pl.semaphore_wait(bar, 3 + jnp.where(self.has_down, 1, 0) + jnp.where(self.has_up, 1, 0))

    def barrier_all(self, n):
        bar = pltpu.get_barrier_semaphore()

        @pl.loop(1, n)
        def _(i):
            pl.semaphore_signal(bar, inc=1, device_id=((self.me + i) % n,), device_id_type=MESH)

        pl.semaphore_wait(bar, n - 1)

def when(cond, f):
    if cond is None: f()
    else: pl.when(cond)(f)

class Gather:
    def __init__(self, place, ins, outs, send_sem, recv_sem):
        self.p, self.ins, self.outs = place, ins, outs
        self.ss, self.rs = send_sem, recv_sem
        self.ids, self.pend = {}, []
    def rows(self, k, h):
        n = self.ins[k].shape[0]
        return (0, n) if h == 2 else (h * (n // 2), n // 2)
    def copy(self, key, k, shard, h, to, own=False):
        i = self.ids.setdefault((key, k), len(self.ids))
        r, n = self.rows(k, h)
        full = self.ins[k].shape[0]
        dst = self.outs[k].at[pl.ds(shard * full + r, n)]
        src = self.ins[k].at[pl.ds(r, n)] if own else dst
        return pltpu.make_async_remote_copy(src_ref=src, dst_ref=dst, send_sem=self.ss.at[i], recv_sem=self.rs.at[i], device_id=(to,), device_id_type=MESH)
    def send(self, cond, *a):
        when(cond, lambda: self.copy(*a).start())
        self.pend.append((cond, lambda: self.copy(*a).wait_send()))
    def recv(self, cond, key, k, shard, h):
        when(cond, lambda: self.copy(key, k, shard, h, self.p.me).wait_recv())
    def col(self, o):
        p = self.p
        if o == 0: return None, p.z
        if o > 0: return p.z - o >= 0, jnp.maximum(p.z - o, 0)
        return p.z - o <= p.Z - 1, jnp.minimum(p.z - o, p.Z - 1)
    def offs(self, s):
        return (0,) if s == 0 else (s, -s)
    def stage(self, k, s):
        p = self.p
        L = p.Z
        if s < L:
            for o in self.offs(s):
                cond, zz = self.col(o)
                sh = p.dev(zz, p.y, p.x, p.c)
                own = o == 0
                if not own:
                    self.recv(cond, ("z", o), k, sh, 2)
                if s + 1 < L:
                    both = lambda c1: c1 if cond is None else jnp.logical_and(cond, c1)
                    if o >= 0: self.send(both(p.has_up), ("z", s + 1), k, sh, 2, p.up, own)
                    if o <= 0: self.send(both(p.has_down), ("z", -(s + 1)), k, sh, 2, p.down, own)
                if abs(o) != 1:
                    self.send(cond, ("x", o), k, sh, 2, p.nx, own)
                    self.send(cond, ("y", o), k, sh, 2, p.ny, own)
                self.send(cond, ("c", o), k, sh, 2, p.nc, own)
        if 1 <= s <= L:
            for o in self.offs(s - 1):
                cond, zz = self.col(o)
                sx, sy = p.dev(zz, p.y, 1 - p.x, p.c), p.dev(zz, 1 - p.y, p.x, p.c)
                for key, sh, half, to in (("x", sx, 0, p.ny), ("y", sy, 1, p.nx)):
                    self.recv(cond, (key, o), k, sh, 2)
                    if o == 0:
                        self.send(p.has_up, (key, 1), k, sh, 2, p.up)
                        self.send(p.has_down, (key, -1), k, sh, 2, p.down)
                    self.send(cond, ("d" + key, o), k, sh, half, to)
                    self.send(cond, ("c" + key, o), k, sh, 2, p.nc)
        if 2 <= s <= L + 1:
            for o in self.offs(s - 2):
                cond, zz = self.col(o)
                sd = p.dev(zz, 1 - p.y, 1 - p.x, p.c)
                self.recv(cond, ("dx", o), k, sd, 0)
                self.recv(cond, ("dy", o), k, sd, 1)
                self.send(cond, ("cd", o), k, sd, 2, p.nc)
        if s == L + 2:
            for t in range(L):
                for o in self.offs(t):
                    cond, zz = self.col(o)
                    for key, yy, xx in (("c", p.y, p.x), ("cx", p.y, 1 - p.x), ("cy", 1 - p.y, p.x), ("cd", 1 - p.y, 1 - p.x)):
                        self.recv(cond, (key, o), k, p.dev(zz, yy, xx, 1 - p.c), 2)
    def stages(self):
        return self.p.Z + 3
    def finish(self):
        for cond, f in self.pend:
            when(cond, f)

def sems_needed(dims, K):
    Z = dims[0]
    return K * (2 * (Z - 1) + 12 * (2 * Z - 1))


F32, BF16 = jnp.float32, jnp.bfloat16
TILE = 256
O_GAIN, O_SHIFT, O_OMEGA, O_AFF, O_REL = 0, 2 * D, 4 * D, 5 * D, 5 * D + 4 * Z
O_VB = O_REL + STRETCH
O_MXB = O_VB + VALUE_WIDTH
MXW = 2 * D + Z + VALUE_WIDTH
O_HB = O_MXB + MXW
O_UPB = O_HB + D
O_DNB = O_UPB + FF
O_EMA = O_DNB + D
C_LAT, C_RES, C_HX = D, D + Z, D + Z + VALUE_WIDTH


def sigmoid(v):
    return 0.5 * jnp.tanh(0.5 * v) + 0.5


def silu_slope(v, s):
    return s * (1.0 + v * (1.0 - s))


def col_sum(v):
    return jnp.sum(v, axis=0, keepdims=True)


def dot(a, b, ca=1, cb=0):
    return lax.dot_general(a, b, (((ca,), (cb,)), ((), ())), preferred_element_type=F32)


def tiles(lo, hi, step, f):
    @pl.loop(0, (hi - lo) // step)
    def _(i):
        f(pl.multiple_of(lo + i * step, 128))


def lane_block(l):
    return pl.ds(pl.multiple_of(l * 128, 128), 128)


def center(xf):
    c = xf - jnp.mean(xf, axis=-1, keepdims=True)
    r = lax.rsqrt(jnp.mean(c * c, axis=-1, keepdims=True) + epsilon)
    return c * r, r


def ema_rates(ema):
    gate, a = sigmoid(ema[0]), sigmoid(ema[1])
    retain = 1.0 - gate * a
    weight = gate * ema[2] * ema[3] * (1.0 / math.sqrt(H))
    return gate, a, retain, weight


def rel_table(rel_row):
    wide = jnp.broadcast_to(rel_row, (STRETCH, STRETCH))
    return pltpu.roll(wide, 0, 1, stride=1, stride_axis=0).T


def causal():
    i = lax.broadcasted_iota(jnp.int32, (STRETCH, STRETCH), 0)
    j = lax.broadcasted_iota(jnp.int32, (STRETCH, STRETCH), 1)
    return j <= i


class Forward:
    def __init__(self, x, valid, prow, ema, w, s):
        self.x, self.valid, self.prow, self.ema, self.w, self.s = x, valid, prow, ema, w, s
        self.m = x.shape[0]
        self.seqs = self.m // STRETCH

    def p(self, lo, n):
        return self.prow[:, lo : lo + n]

    def pd(self, lo, col, n):
        return self.prow[:, pl.ds(pl.multiple_of(lo + col, 128), n)]

    def norm_one(self):
        s = self.s
        g, b = self.p(O_GAIN, D), self.p(O_SHIFT, D)
        for q in range(self.seqs):
            s.mpad[q, 0:8, :] = jnp.zeros((8, D), F32)

            @pl.loop(0, STRETCH // 32)
            def _(i):
                r = pl.ds(q * STRETCH + i * 32, 32)
                xhat, _ = center(self.x[r, :].astype(F32))
                n = xhat * g + b
                s.normed[r, :] = n.astype(BF16)
                s.mpad[q, pl.ds(8 + i * 32, 32), :] = n * self.valid[r, 0:1]

    def ema_kernel(self):
        _, _, retain, weight = ema_rates(self.ema)

        def step(j, p):
            self.s.kern[pl.ds(j, 1), :] = col_sum(p)
            return p * retain

        lax.fori_loop(0, STRETCH, step, weight)

    def smooth(self, q):
        s = self.s
        for q in (q,):

            @pl.loop(0, D // 128)
            def _(l):
                lb = lane_block(l)
                om = self.prow[:, pl.ds(pl.multiple_of(O_OMEGA + l * 128, 128), 128)]
                nb = STRETCH // 8
                acc = [om * s.mpad[q, 8 + 8 * i : 16 + 8 * i, lb] for i in range(nb)]
                for b in range(8):
                    sh = [s.mpad[q, 8 - b + 8 * i : 16 - b + 8 * i, lb] for i in range(nb)]
                    for a in range(nb):
                        kb = jnp.broadcast_to(s.kern[8 * a + b : 8 * a + b + 1, lb], (8, 128))
                        for i in range(a, nb):
                            acc[i] = acc[i] + kb * sh[i - a]
                for i in range(nb):
                    r = slice(q * STRETCH + 8 * i, q * STRETCH + 8 * i + 8)
                    s.e[r, lb] = acc[i]

    def mix(self):
        s = self.s

        @pl.loop(0, self.m // 32)
        def _(i):
            r = pl.ds(i * 32, 32)
            e = s.e[r, :]
            s.mixed[r, :] = (e * sigmoid(e)).astype(BF16)

    def values(self):
        s = self.s

        def one(col):
            cols = pl.ds(col, TILE)
            v = dot(s.normed[...], self.w.v[:, cols]) + self.pd(O_VB, col, TILE)
            sv = sigmoid(v)
            s.vslope[:, cols] = silu_slope(v, sv).astype(BF16)
            s.val[:, cols] = (v * sv).astype(BF16)

        tiles(0, VALUE_WIDTH, TILE, one)

    def base(self):
        s = self.s

        def one(width):
            def f(col):
                cols = pl.ds(col, width)
                s.base[:, cols] = dot(s.mixed[...], self.w.mx[:, cols]) + self.pd(O_MXB, col, width)

            return f

        tiles(0, D, TILE, one(TILE))
        tiles(C_LAT, C_RES, Z, one(Z))
        tiles(C_RES, MXW, TILE, one(TILE))

    def attend(self):
        s = self.s
        table, mask = rel_table(self.p(O_REL, STRETCH)), causal()
        for q in range(self.seqs):
            r = slice(q * STRETCH, (q + 1) * STRETCH)
            b = s.base[r, C_LAT:C_RES]
            s.lat[r, :] = b
            lat = b * sigmoid(b)
            query = (lat * (1.0 + self.p(O_AFF, Z)) + self.p(O_AFF + 2 * Z, Z)).astype(BF16)
            keys = (lat * (1.0 + self.p(O_AFF + Z, Z)) + self.p(O_AFF + 3 * Z, Z)).astype(BF16)
            sc = jnp.where(mask, dot(query, keys, 1, 1) * (1.0 / math.sqrt(Z)) + table, -1e30)
            ex = jnp.exp(sc - jnp.max(sc, axis=-1, keepdims=True))
            pr = ex / jnp.sum(ex, axis=-1, keepdims=True)
            s.probs[r, :] = pr
            s.query[r, :] = query
            s.keys[r, :] = keys
            low = pr.astype(BF16)

            def one(col):
                cols = pl.ds(col, TILE)
                at = dot(low, s.val[r, cols])
                bb = s.base[r, pl.ds(pl.multiple_of(C_RES + col, 128), TILE)]
                sb = sigmoid(bb)
                res = bb * sb
                s.res[r, cols] = res.astype(BF16)
                s.ars[r, cols] = (at * silu_slope(bb, sb)).astype(BF16)
                s.gated[r, cols] = (at * res).astype(BF16)

            tiles(0, VALUE_WIDTH, TILE, one)

    def hidden(self):
        s = self.s

        def one(col):
            cols = pl.ds(col, TILE)
            h = dot(s.gated[...], self.w.h[:, cols]) + self.pd(O_HB, col, TILE)
            h = h + s.base[:, pl.ds(pl.multiple_of(C_HX + col, 128), TILE)]
            s.hpre[:, cols] = h
            xf = self.x[:, cols].astype(F32)
            u = sigmoid(s.base[:, cols])
            s.upd[:, cols] = u
            s.first[:, cols] = xf + self.valid[:, 0:1] * u * (h * sigmoid(h) - xf)

        tiles(0, D, TILE, one)

    def norm_two(self):
        s = self.s
        g, b = self.p(O_GAIN + D, D), self.p(O_SHIFT + D, D)

        @pl.loop(0, self.m // 32)
        def _(i):
            r = pl.ds(i * 32, 32)
            xhat, _ = center(s.first[r, :])
            s.second[r, :] = (xhat * g + b).astype(BF16)

    def up(self):
        s = self.s

        def one(col):
            cols = pl.ds(col, TILE)
            u = dot(s.second[...], self.w.up[:, cols]) + self.pd(O_UPB, col, TILE)
            su = sigmoid(u)
            s.uslope[:, cols] = silu_slope(u, su).astype(BF16)
            s.inner[:, cols] = (u * su).astype(BF16)

        tiles(0, FF, TILE, one)


class Backward:
    def __init__(self, x, g, valid, prow, ema, w, s, t, grow, gema):
        self.x, self.g, self.valid, self.prow, self.ema = x, g, valid, prow, ema
        self.w, self.s, self.t, self.grow, self.gema = w, s, t, grow, gema
        self.m = x.shape[0]
        self.seqs = self.m // STRETCH

    p, pd = Forward.p, Forward.pd

    def put(self, lo, col, n, v):
        self.grow[:, pl.ds(pl.multiple_of(lo + col, 128), n)] = v

    def cot(self):
        def one(col):
            cols = pl.ds(col, TILE)
            d = self.valid[:, 0:1] * self.g[:, cols].astype(F32)
            self.put(O_DNB, col, TILE, col_sum(d))
            self.t.dd[:, cols] = d.astype(BF16)

        tiles(0, D, TILE, one)

    def down_tile(self, col, w):
        s, t = self.s, self.t
        cols = pl.ds(col, TILE)
        t.dn[...] += dot(s.inner[:, cols], w[...])
        di = dot(t.dd[...], w[...], 1, 1)
        du = di * s.uslope[:, cols].astype(F32)
        self.put(O_UPB, col, TILE, col_sum(du))
        t.dup[:, cols] = du.astype(BF16)

    def output(self, out):
        s, t = self.s, self.t

        def one(col):
            cols = pl.ds(col, TILE)
            d = t.dn[:, cols] + self.pd(O_DNB, col, TILE)
            out[:, cols] = (s.first[:, cols] + self.valid[:, 0:1] * d).astype(BF16)

        tiles(0, D, TILE, one)

    def second_tile(self, col, w):
        self.t.dsec[:, pl.ds(col, TILE)] = dot(self.t.dup[...], w[...], 1, 1)

    def norm_two(self):
        s, t = self.s, self.t
        g = self.p(O_GAIN + D, D)
        t.acc[...] = jnp.zeros(t.acc.shape, F32)

        def add(k, v):
            t.acc[k] += jnp.sum(v.reshape(v.shape[0] // 8, 8, D), axis=0)

        @pl.loop(0, self.m // 32)
        def _(i):
            r = pl.ds(i * 32, 32)
            xhat, rstd = center(s.first[r, :])
            ds = t.dsec[r, :]
            add(0, ds * xhat)
            add(1, ds)
            dh = ds * g
            dn = rstd * (dh - jnp.mean(dh, axis=-1, keepdims=True) - xhat * jnp.mean(dh * xhat, axis=-1, keepdims=True))
            df = self.g[r, :].astype(F32) + dn
            v = self.valid[r, 0:1]
            u = s.upd[r, :]
            hp = s.hpre[r, :]
            sh = sigmoid(hp)
            xf = self.x[r, :].astype(F32)
            vu = v * u
            t.dx[r, :] = df - df * vu
            db = df * v * (hp * sh - xf) * u * (1.0 - u)
            add(2, db)
            t.dbase[r, 0:D] = db.astype(BF16)
            dhp = df * vu * silu_slope(hp, sh)
            add(3, dhp)
            t.dbase[r, C_HX:MXW] = dhp.astype(BF16)

        for k, lo in enumerate((O_GAIN + D, O_SHIFT + D, O_MXB, O_HB)):
            self.grow[:, lo : lo + D] = col_sum(t.acc[k])
        self.grow[:, O_MXB + C_HX : O_MXB + MXW] = col_sum(t.acc[3])

    def gated_tile(self, col, w):
        s, t = self.s, self.t
        cols = pl.ds(col, TILE)
        bcols = pl.ds(pl.multiple_of(C_RES + col, 128), TILE)
        dg = dot(t.dbase[:, C_HX:MXW], w[...], 1, 1)
        t.datt[:, cols] = (dg * s.res[:, cols].astype(F32)).astype(BF16)
        db = dg * s.ars[:, cols].astype(F32)
        self.put(O_MXB + C_RES, col, TILE, col_sum(db))
        t.dbase[:, bcols] = db.astype(BF16)

    def attend(self):
        s, t = self.s, self.t
        mask = causal()
        lows, drel = [], None
        aff = [0.0, 0.0, 0.0, 0.0]
        lat_bias = 0.0
        for q in range(self.seqs):
            r = slice(q * STRETCH, (q + 1) * STRETCH)
            pr = s.probs[r, :]
            lows.append(pr.astype(BF16))
            dp = dot(t.datt[r, :], s.val[r, :], 1, 1)
            ds = pr * (dp - jnp.sum(pr * dp, axis=-1, keepdims=True))
            ds = jnp.where(mask, ds, 0.0)
            drel = ds if drel is None else drel + ds
            raw = (ds * (1.0 / math.sqrt(Z))).astype(BF16)
            dq = dot(raw, s.keys[r, :])
            dk = dot(raw, s.query[r, :], 0, 0)
            b = s.lat[r, :]
            sb = sigmoid(b)
            lat = b * sb
            for k, v in enumerate((dq * lat, dk * lat, dq, dk)):
                aff[k] = aff[k] + col_sum(v)
            dl = dq * (1.0 + self.p(O_AFF, Z)) + dk * (1.0 + self.p(O_AFF + Z, Z))
            db = dl * silu_slope(b, sb)
            lat_bias = lat_bias + col_sum(db)
            t.dbase[r, C_LAT:C_RES] = db.astype(BF16)
        for k in range(4):
            self.grow[:, O_AFF + k * Z : O_AFF + (k + 1) * Z] = aff[k]
        self.grow[:, O_MXB + C_LAT : O_MXB + C_RES] = lat_bias
        drel = drel.T
        eight = 0.0
        for i in range(0, STRETCH, 8):
            eight = eight + pltpu.roll(drel[i : i + 8, :], (STRETCH - i) % STRETCH, 1)
        back = 0.0
        for i in range(8):
            back = back + pltpu.roll(eight[i : i + 1, :], (STRETCH - i) % STRETCH, 1)
        self.grow[:, O_REL : O_REL + STRETCH] = back

        def one(col):
            cols = pl.ds(col, TILE)
            bias = 0.0
            for q in range(self.seqs):
                r = slice(q * STRETCH, (q + 1) * STRETCH)
                dv = dot(lows[q], t.datt[r, cols], 0, 0)
                dv = dv * s.vslope[r, cols].astype(F32)
                bias = bias + col_sum(dv)
                t.dv[r, cols] = dv.astype(BF16)
            self.put(O_VB, col, TILE, bias)

        tiles(0, VALUE_WIDTH, TILE, one)

    def pad_tail(self):
        for q in range(self.seqs):
            self.t.dpad[q, STRETCH : STRETCH + 8, :] = jnp.zeros((8, D), F32)

    def mixed_tile(self, col, w):
        s, t = self.s, self.t
        cols = pl.ds(col, TILE)
        dm = dot(t.dbase[...], w[...], 1, 1)
        e = s.e[:, cols]
        de = dm * silu_slope(e, sigmoid(e))
        om = 0.0
        for q in range(self.seqs):
            d = de[q * STRETCH : (q + 1) * STRETCH, :]
            t.dpad[q, 0:STRETCH, cols] = d
            om = om + col_sum(d * s.mpad[q, 8 : 8 + STRETCH, cols])
        self.put(O_OMEGA, col, TILE, om)

    def normed_tile(self, col, w):
        self.t.dn[:, pl.ds(col, TILE)] = dot(self.t.dv[...], w[...], 1, 1)

    def smooth_signal(self, seq):
        s, t = self.s, self.t
        nb = STRETCH // 8

        @pl.loop(0, D // 128)
        def _(l):
            lb = lane_block(l)
            om = self.prow[:, pl.ds(pl.multiple_of(O_OMEGA + l * 128, 128), 128)]
            for q in (seq,):
                acc = [om * t.dpad[q, 8 * i : 8 * i + 8, lb] for i in range(nb)]
                for b in range(8):
                    sh = [t.dpad[q, 8 * i + b : 8 * i + b + 8, lb] for i in range(nb)]
                    for a in range(nb):
                        kb = jnp.broadcast_to(s.kern[8 * a + b : 8 * a + b + 1, lb], (8, 128))
                        for i in range(nb - a):
                            acc[i] = acc[i] + kb * sh[i + a]
                for i in range(nb):
                    r = slice(q * STRETCH + 8 * i, q * STRETCH + 8 * i + 8)
                    t.dn[r, lb] = t.dn[r, lb] + self.valid[r, :] * acc[i]

    def smooth_filter(self):
        s, t = self.s, self.t
        nb = STRETCH // 8

        @pl.loop(0, D // 128)
        def _(l):
            lb = lane_block(l)
            for b in range(8):
                sums = [None] * nb
                for q in range(self.seqs):
                    de = [t.dpad[q, 8 * i : 8 * i + 8, lb] for i in range(nb)]
                    sh = [s.mpad[q, 8 - b + 8 * i : 16 - b + 8 * i, lb] for i in range(nb)]
                    for a in range(nb):
                        for i in range(a, nb):
                            v = de[i] * sh[i - a]
                            sums[a] = v if sums[a] is None else sums[a] + v
                for a in range(nb):
                    t.dkern[8 * a + b : 8 * a + b + 1, lb] = col_sum(sums[a])

    def norm_one(self, out):
        t = self.t
        g = self.p(O_GAIN, D)
        t.acc[...] = jnp.zeros(t.acc.shape, F32)

        def add(k, v):
            t.acc[k] += jnp.sum(v.reshape(v.shape[0] // 8, 8, D), axis=0)

        @pl.loop(0, self.m // 32)
        def _(i):
            r = pl.ds(i * 32, 32)
            xhat, rstd = center(self.x[r, :].astype(F32))
            dn = t.dn[r, :]
            add(0, dn * xhat)
            add(1, dn)
            dh = dn * g
            d = rstd * (dh - jnp.mean(dh, axis=-1, keepdims=True) - xhat * jnp.mean(dh * xhat, axis=-1, keepdims=True))
            out[r, :] = (t.dx[r, :] + d).astype(BF16)

        for k, lo in enumerate((O_GAIN, O_SHIFT)):
            self.grow[:, lo : lo + D] = col_sum(t.acc[k])


    def ema_grads(self):
        t = self.t
        gate, a, retain, weight = ema_rates(self.ema)
        zero = retain - retain

        def step(j, carry):
            power, before, dw, dr = carry
            row = t.dkern[pl.ds(j, 1), :]
            dw = dw + row * power
            dr = dr + (row * j.astype(F32)) * before
            return power * retain, power, dw, dr

        _, _, dw, dr = lax.fori_loop(0, STRETCH, step, (zero + 1.0, zero, zero, zero))
        drate = -dr * weight
        scale = 1.0 / math.sqrt(H)
        dgate = drate * a + dw * self.ema[2] * self.ema[3] * scale
        self.gema[0] = dgate * gate * (1.0 - gate)
        self.gema[1] = drate * gate * a * (1.0 - a)
        self.gema[2] = dw * gate * self.ema[3] * scale
        self.gema[3] = dw * gate * self.ema[2] * scale


class Scatter:
    def __init__(self, place, grads, rings, depth, outs, send_sem, recv_sem, local_sem, credit):
        self.p, self.grads, self.outs, self.depth, self.credit = place, grads, outs, depth, credit
        self.bufs = []
        for k, g in enumerate(grads):
            e, w = k % depth, pl.ds(0, g.shape[-1])
            self.bufs.append(Names(**{name: ref.at[e, :, :, w] for name, ref in rings.items()}))
        self.ss, self.rs, self.ls = send_sem, recv_sem, local_sem
        self.ids, self.pend = {}, [[] for _ in grads]

    def around(self):
        p = self.p
        return ((None, p.nc), (None, p.nx), (None, p.ny), (p.has_up, p.up), (p.has_down, p.down))

    def release(self, k):
        self.finish(k)
        if k + self.depth < len(self.grads):
            for i, (cond, to) in enumerate(self.around()):
                slot = (0, 1, 2, 4, 3)[i]
                when(cond, lambda slot=slot, to=to: pl.semaphore_signal(self.credit.at[k, slot], inc=1, device_id=(to,), device_id_type=MESH))

    def admit(self, k):
        if k >= self.depth:
            for i, (cond, to) in enumerate(self.around()):
                when(cond, lambda i=i: pl.semaphore_wait(self.credit.at[k - self.depth, i], 1))

    def copy(self, key, k, src, dst, to):
        i = self.ids.setdefault((key, k), len(self.ids))
        return pltpu.make_async_remote_copy(src_ref=src, dst_ref=dst, send_sem=self.ss.at[i], recv_sem=self.rs.at[i], device_id=(to,), device_id_type=MESH)

    def send(self, cond, key, k, src, dst, to):
        when(cond, lambda: self.copy(key, k, src, dst, to).start())
        self.pend[k].append((cond, lambda: self.copy(key, k, src, dst, to).wait_send()))

    def recv(self, cond, key, k, dst):
        when(cond, lambda: self.copy(key, k, dst, dst, self.p.me).wait_recv())

    def own(self, k, z):
        p, b = self.p, self.bufs[k]
        layer = p.Y * p.X
        i = k * p.Z + z
        return pltpu.make_async_copy(self.grads[k].at[pl.ds(z * layer, layer), p.c], b.mine.at[pl.ds((z % 2) * layer, layer)], self.ls.at[i])

    def add(self, dst, a, b, r0=0, rows=None):
        n = rows

        @pl.loop(0, n // 16)
        def _(i):
            def at(v, r):
                ref, q, off = v
                return ref.at[q, pl.ds(pl.multiple_of(off + r, 16), 16)]

            r = i * 16
            at(dst, r)[...] = at(a, r)[...] + at(b, r)[...]

    def stage(self, k, s):
        p, b = self.p, self.bufs[k]
        layer = p.Y * p.X
        r = b.sum.shape[1]
        half = r // 2
        chip = lambda z, y, x: (z * p.Y + y) * p.X + x
        col = lambda z: (chip(z, p.y, p.x), chip(z, p.y, 1 - p.x), chip(z, 1 - p.y, p.x), chip(z, 1 - p.y, 1 - p.x))
        L = p.Z
        planes = range(L)
        off = lambda z, d: p.z == z + d
        far = lambda z: jnp.logical_and(p.z != z - 1, p.z != z + 1)
        apart = lambda z: jnp.logical_and(far(z), p.z != z)
        S, H0, H1 = b.sum, 0, half
        if s == 0:
            self.admit(k)
            for z in planes:
                self.send(None, ("c", z), k, self.grads[k].at[pl.ds(z * layer, layer), 1 - p.c], S.at[pl.ds(z * layer, layer)], p.nc)
                if z < 2:
                    self.own(k, z).start()
        if s == 1:
            for z in planes:
                self.recv(None, ("c", z), k, S.at[pl.ds(z * layer, layer)])
                self.own(k, z).wait()
                me, nx, ny, nd = col(z)
                back = (z - z % 2) * layer
                self.add((S, nd, 0), (S, nd, 0), (b.mine, nd - back, 0), rows=r)
                self.send(None, ("dy", z), k, S.at[nd, pl.ds(0, half)], b.dy.at[z], p.ny)
                self.send(None, ("dx", z), k, S.at[nd, pl.ds(half, half)], b.dx.at[z], p.nx)
                for q in (nx, ny, me):
                    self.add((S, q, 0), (S, q, 0), (b.mine, q - back, 0), rows=r)
                if z + 2 < L:
                    self.own(k, z + 2).start()
        if s == 2:
            for z in planes:
                me, nx, ny, nd = col(z)
                for key, q, h, buf, to, out in (("dy", nx, H0, b.dy, p.nx, b.rx), ("dx", ny, H1, b.dx, p.ny, b.ry)):
                    self.recv(None, (key, z), k, buf.at[z])
                    self.add((S, q, h), (S, q, h), (buf, z, 0), rows=half)
                    tag = "x" if key == "dy" else "y"
                    side = 0 if key == "dy" else 1
                    self.send(apart(z), (tag, z), k, S.at[q], out.at[z], to)
                    if z > 0:
                        self.send(off(z, -1), ("z" + tag, 0), k, S.at[q], b.rz.at[side], p.up)
                    if z < L - 1:
                        self.send(off(z, 1), ("z" + tag, 1), k, S.at[q], b.rz.at[2 + side], p.down)
        if s == 3:
            me, nx, ny, nd = col(p.z)
            for tag, q, side, to, out in (("x", nx, 0, p.nx, b.rx), ("y", ny, 1, p.ny, b.ry)):
                for cond, way in ((p.has_down, 0), (p.has_up, 1)):

                    def take(q=q, side=side, way=way, tag=tag):
                        self.copy(("z" + tag, way), k, b.rz.at[2 * way + side], b.rz.at[2 * way + side], p.me).wait_recv()
                        self.add((S, q, 0), (S, q, 0), (b.rz, 2 * way + side, 0), rows=r)

                    pl.when(cond)(take)
                for z in planes:
                    self.send(p.z == z, (tag, z), k, S.at[q], out.at[z], to)
        if s == 4:
            for z in planes:
                me = col(z)[0]
                for tag, buf in (("y", b.ry), ("x", b.rx)):

                    def take(me=me, tag=tag, buf=buf, z=z):
                        self.copy((tag, z), k, buf.at[z], buf.at[z], p.me).wait_recv()
                        self.add((S, me, 0), (S, me, 0), (buf, z, 0), rows=r)

                    pl.when(far(z))(take)
        if 4 <= s < 4 + L - 1:
            hop = s - 4
            for up in (True, False):
                zz = hop if up else L - 1 - hop
                buf, key, to = (b.ru, "u", p.up) if up else (b.rd, "d", p.down)
                here = p.z == zz
                for t in range(L - 1, zz, -1) if up else range(0, zz):
                    q = chip(t, p.y, p.x)

                    def relay(q=q, t=t, buf=buf, key=key):
                        self.copy((key, t), k, buf.at[t], buf.at[t], p.me).wait_recv()
                        self.add((S, q, 0), (S, q, 0), (buf, t, 0), rows=r)

                    if hop > 0:
                        pl.when(here)(relay)
                    self.send(here, (key, t), k, S.at[q], buf.at[t], to)
        if s == 4 + L - 1:
            me = chip(p.z, p.y, p.x)
            for key, buf, ts in (("", None, (0,)), ("u", b.ru, range(1, L)), ("d", b.rd, range(0, L - 1))):
                for t in ts:

                    def last(key=key, buf=buf, t=t):
                        if buf is not None:
                            self.copy((key, t), k, buf.at[t], buf.at[t], p.me).wait_recv()

                        @pl.loop(0, r // 16)
                        def _(i):
                            rr = pl.ds(pl.multiple_of(i * 16, 16), 16)
                            v = (S[me, rr, :] if buf is None else buf[t, rr, :]).astype(F32)
                            for out, row, col, lo, w in self.outs[k]:
                                o = out.at[pl.ds(pl.multiple_of(row + i * 16, 16), 16), col : col + w]
                                if buf is None:
                                    o[...] = v[:, lo : lo + w]
                                else:
                                    o[...] += v[:, lo : lo + w]

                    when(None if buf is None else p.z == t, last)
            self.release(k)

    def stages(self):
        return 4 + self.p.Z

    def finish(self, k):
        for cond, f in self.pend[k]:
            when(cond, f)
        self.pend[k] = []


class Names:
    def __init__(self, **kw):
        self.__dict__.update(kw)


SCATTER_BUFS = ("mine", "sum", "dx", "dy", "rx", "ry", "ru", "rd", "rz")


def scatter_scratch(dims, r, w, depth, K):
    Z, Y, X = dims
    sizes = dict(mine=(2 * Y * X, r), sum=(Z * Y * X, r), dx=(Z, r // 2), dy=(Z, r // 2), rx=(Z, r), ry=(Z, r), ru=(Z, r), rd=(Z, r), rz=(4, r))
    ns = K * (7 * Z + 4)
    dma = pltpu.SemaphoreType.DMA
    scratch = [pltpu.VMEM((depth,) + sizes[k] + (w,), BF16) for k in SCATTER_BUFS]
    return scratch + [dma((ns,)), dma((ns,)), dma((K * Z,)), pltpu.SemaphoreType.REGULAR((K, 5))]


KEPT_OLD = ("normed", "mpad", "e", "mixed", "kern", "vslope", "val", "base", "probs", "query", "keys", "att", "gated", "hpre", "first", "second", "uslope", "inner")


def kept_shapes(m):
    seqs = m // STRETCH
    f, b = (lambda *s: (s, F32)), (lambda *s: (s, BF16))
    return dict(
        normed=b(m, D), mpad=f(seqs, STRETCH + 8, D), e=f(m, D), mixed=b(m, D), kern=f(STRETCH, D),
        vslope=b(m, VALUE_WIDTH), val=b(m, VALUE_WIDTH), base=f(m, MXW), probs=f(m, STRETCH),
        query=b(m, Z), keys=b(m, Z), upd=f(m, D), lat=f(m, Z), res=b(m, VALUE_WIDTH), ars=b(m, VALUE_WIDTH), gated=b(m, VALUE_WIDTH), hpre=f(m, D),
        first=f(m, D), second=b(m, D), uslope=b(m, FF), inner=b(m, FF),
    )


VM = pltpu.VMEM
LIMIT = 64 * 1024 * 1024


def weight_grad(a, b, out, turned, stage, sem, lo=0, start=0, stop=None, place=None):
    stop = stop or b.shape[1] - lo

    def begin(slot, i, col, w):
        if place is None:
            cols = pl.ds(pl.multiple_of(col, 128), w)
            pltpu.make_async_copy(stage.at[slot, :, 0:w], out.at[pl.ds(i * D, D), cols], sem.at[slot]).start()
            return
        chips, pieces = place
        src = stage.at[slot, :, 0:w].reshape(chips, 2, pieces, D // (2 * chips * pieces), w)
        for q in range(pieces):
            cols = pl.ds(pl.multiple_of((q % 2) * D + col, 128), w)
            pltpu.make_async_copy(src.at[:, :, q], out.at[q // 2, pl.ds(i * chips, chips), :, :, cols], sem.at[slot]).start()

    def wait(slot, w):
        whole = stage.at[slot, :, 0:w]
        pltpu.make_async_copy(whole, whole, sem.at[slot]).wait()

    def block(slot, i, col, w):
        stage[slot, :, 0:w] = dot(turned[...], b[:, pl.ds(pl.multiple_of(lo + col, 128), w)]).astype(BF16)
        begin(slot, i, col, w)

    pairs = (stop - start) // (2 * TILE)
    for i in range(a.shape[1] // D):
        turned[...] = a[:, i * D : (i + 1) * D].T

        @pl.loop(0, pairs)
        def _(j):
            for slot in range(2):

                @pl.when(jnp.logical_or(j > 0, i > 0))
                def _():
                    wait(slot, TILE)

                block(slot, i, start + (j * 2 + slot) * TILE, TILE)

    rest = stop - start - pairs * 2 * TILE
    wait(0, TILE)
    if rest:
        block(0, 0, stop - rest, rest)
    wait(1, TILE)
    if rest:
        wait(0, rest)


class Stream:
    def __init__(self, w, ring, sem):
        self.w, self.ring, self.sem = w, ring, sem
        self.width = w.shape[1]

    def copy(self, i, slot):
        rows = pl.ds(pl.multiple_of(i * TILE, TILE), TILE)
        return pltpu.make_async_copy(self.w.at[rows], self.ring.at[slot, :, 0 : self.width], self.sem.at[slot])

    def prefetch(self):
        self.copy(0, 0).start()
        self.copy(1, 1).start()

    def run(self, body, lo=0, hi=None):
        count = self.w.shape[0] // TILE
        hi = hi or count

        @pl.loop(lo // 2, hi // 2)
        def _(j):
            for slot in range(2):
                i = j * 2 + slot
                self.copy(i, slot).wait()
                body(pl.multiple_of(i * TILE, TILE), self.ring.at[slot, :, 0 : self.width])

                @pl.when(i + 2 < count)
                def _():
                    self.copy(i + 2, slot).start()


def own_shapes(m):
    seqs = m // STRETCH
    return dict(
        dd=((m, D), BF16), acc=((4, 8, D), F32), dx=((m, D), F32),
        dbase=((m, MXW), BF16), datt=((m, VALUE_WIDTH), BF16), dv=((m, VALUE_WIDTH), BF16),
        dpad=((seqs, STRETCH + 8, D), F32), dn=((m, D), F32), dkern=((STRETCH, D), F32),
    )


SMALL_ROWS = 32
FRAME = 24


def frames(n, count):
    return [(count * d) // 128 for d in range(n)]


def spread(k):
    p = lax.broadcasted_iota(jnp.int32, (D, TILE), 0)
    c = lax.broadcasted_iota(jnp.int32, (D, TILE), 1) + k * TILE
    return (c == 8 * (p % 128) + p // 128).astype(BF16)


def unpack_params(n, count, packed, full, prow, ema):
    full[...] = jnp.zeros(full.shape, F32)
    for d, r in enumerate(frames(n, count)):
        full[r : r + FRAME, :] += packed[d * SMALL_ROWS : d * SMALL_ROWS + FRAME, :].astype(F32)
    for i in range(O_EMA // 128):
        prow[:, i * 128 : (i + 1) * 128] = full[i : i + 1, :]
    rows = []
    for j in range(4):
        lo = O_EMA // 128 + j * D * H // 128
        t = full[lo : lo + 128, :].T
        rows.append(jnp.concatenate([t[H * k : H * (k + 1), :] for k in range(8)], axis=1))
    stack = jnp.concatenate(rows, axis=0).astype(BF16)
    for k in range(D // TILE):
        e = dot(stack, spread(k))
        for j in range(4):
            ema[j, :, k * TILE : (k + 1) * TILE] = e[j * H : (j + 1) * H, :]


def pack_grads(n, count, grow, gema, full, out):
    for i in range(O_EMA // 128):
        full[i : i + 1, :] = grow[:, i * 128 : (i + 1) * 128]
    stack = jnp.concatenate([gema[j] for j in range(4)], axis=0).astype(BF16)
    back = 0.0
    for k in range(D // TILE):
        back = back + dot(stack[:, k * TILE : (k + 1) * TILE], spread(k), 1, 1)
    for j in range(4):
        e = back[j * H : (j + 1) * H, :]
        lo = O_EMA // 128 + j * D * H // 128
        full[lo : lo + 128, :] = jnp.concatenate([e[:, k * 128 : (k + 1) * 128] for k in range(8)], axis=0).T
    for d, r in enumerate(frames(n, count)):
        out[d // 2, d % 2, 0:FRAME, :] = full[r : r + FRAME, :].astype(BF16)
        out[d // 2, d % 2, FRAME:SMALL_ROWS, :] = jnp.zeros((SMALL_ROWS - FRAME, 128), BF16)


def size_table(n, count, m):
    rows = -(-(-(-(n * count) // 128) + FRAME) // 8) * 8
    table = {k: v for k, v in list(kept_shapes(m).items()) + list(own_shapes(m).items())}
    table.update(
        out=((m, D), BF16), dxo=((m, D), BF16), grow=((1, O_EMA), F32), prow=((1, O_EMA), F32), ema=((4, H, D), F32),
        gema=((4, H, D), F32), full=((rows, 128), F32), packed=((n * SMALL_ROWS, 128), BF16),
        gsmall=((n // 2, 2, SMALL_ROWS, 128), BF16), wr=((FF, D), BF16), wc=((D, MXW), BF16), wv=((D, VALUE_WIDTH), BF16),
        wup=((D, FF), BF16), ring=((2, TILE, MXW), BF16), stage=((2, D, TILE), BF16), turned=((D, m), BF16), wh=((VALUE_WIDTH, D), BF16),
    )
    return table


class Parts:
    def __init__(self, refs):
        self.refs = list(refs)

    def take(self, names):
        got, self.refs = self.refs[: len(names)], self.refs[len(names) :]
        return dict(zip(names, got))

    def rest(self, k):
        got, self.refs = self.refs[:k], self.refs[k:]
        return got


GATHER_STARTS = (0, 1, 2, 3, 4)
LAG = GATHER_STARTS[-1]

SAVED = dict(
    front=("inner", "uslope", "first", "hpre", "second", "dd", "upd", "lat", "res", "ars", "gated", "val", "vslope", "probs", "query", "keys", "mixed", "normed", "e", "mpad", "kern", "grow", "prow", "ema"),
    back=(),
)
LOADED = dict(back=SAVED["front"])
HELD = dict(
    front=SAVED["front"] + ("base", "full", "packed", "wh", "wup", "wc", "wv", "stage", "turned"),
    back=SAVED["front"] + ("dbase", "dn", "acc", "dpad", "dkern", "gema", "full", "gsmall", "ring", "stage", "turned"),
)
DEPTH = 4
UNIT = 2 * D
WIDE = MXW - UNIT


class Store:
    def __init__(self, kind, r, ins, outs):
        held = r.take(HELD[kind])
        self.s = Names(**held)
        self.held = held
        self.ins, self.outs = ins, outs
        self.in_sem, self.out_sem = r.rest(2)
        self.names_in, self.names_out = list(ins), list(outs)
        self.seen, self.begun = set(), []

    def fetch(self):
        for k in self.names_in:
            self.copy_in(k).start()

    def copy_in(self, k):
        return pltpu.make_async_copy(self.ins[k], self.held[k], self.in_sem.at[self.names_in.index(k)])

    def need(self, *names):
        for k in names:
            if k not in self.seen:
                self.copy_in(k).wait()
                self.seen.add(k)

    def copy_out(self, k):
        return pltpu.make_async_copy(self.held[k], self.outs[k], self.out_sem.at[self.names_out.index(k)])

    def save(self, *names):
        for k in names:
            self.copy_out(k).start()
            self.begun.append(k)

    def close(self):
        self.need(*self.names_in)
        self.save(*[k for k in self.names_out if k not in self.begun])
        for k in self.begun:
            self.copy_out(k).wait()


def front_kernel(dims, n, count, *refs):
    r = Parts(refs)
    x, g, valid = r.rest(3)
    ins = r.rest(6)
    outs = r.take(SAVED["front"])
    gdown = r.rest(1)[0]
    whole = [None] + r.rest(5) if dims else ins
    st = Store("front", r, {}, outs)
    s = st.s
    lsem, ssem = r.rest(2)

    if dims:
        osem, gsend, grecv, send_sem, recv_sem = r.rest(5)
        p = Place(dims)
        p.barrier_all(n)
        mine = pl.ds(p.me * SMALL_ROWS, SMALL_ROWS)
        own = pltpu.make_async_copy(ins[0], s.packed.at[mine], lsem.at[0])
        own.start()

        def tell(i, dev, block):
            return pltpu.make_async_remote_copy(
                src_ref=ins[0], dst_ref=s.packed.at[pl.ds(block * SMALL_ROWS, SMALL_ROWS)], send_sem=gsend.at[i], recv_sem=grecv.at[i],
                device_id=(dev,), device_id_type=MESH,
            )

        @pl.loop(1, n)
        def _(i):
            tell(i, (p.me + i) % n, p.me).start()

        gat = Gather(p, ins[1:], whole[1:], send_sem, recv_sem)
        cps = [pltpu.make_async_copy(i, o.at[pl.ds(p.me * i.shape[0], i.shape[0])], osem.at[k]) for k, (i, o) in enumerate(zip(ins[1:], whole[1:]))]
        for cp in cps:
            cp.start()
        last = gat.stages() - 1

        def step(t):
            for k, q in enumerate(GATHER_STARTS):
                if 0 <= t - q <= last:
                    gat.stage(k, t - q)
                    if t - q == last:
                        cps[k].wait()

        def small_here():
            own.wait()

            @pl.loop(1, n)
            def _(i):
                tell(i, p.me, (p.me - i + n) % n).wait()
    else:
        step = lambda t: None

        def small_here():
            small = pltpu.make_async_copy(ins[0], s.packed, lsem.at[0])
            small.start()
            small.wait()

    S = dims[0] + 2 if dims else 6
    w = Names(v=s.wv, mx=s.wc, h=s.wh, up=s.wup)
    into = (None, s.wv, s.wc, s.wh, s.wup)
    load = [None] + [pltpu.make_async_copy(whole[i], into[i], lsem.at[i]) for i in range(1, 5)]
    f = Forward(x, valid, s.prow, s.ema, w, s)
    b = Backward(x, g, valid, s.prow, s.ema, w, s, s, s.grow, None)
    b.grow[...] = jnp.zeros(b.grow.shape, F32)
    step(0)
    b.cot()
    step(1)
    small_here()
    unpack_params(n, count, s.packed, s.full, s.prow, s.ema)
    f.norm_one()
    step(2)
    f.ema_kernel()
    step(3)
    f.smooth(0)
    step(4)
    f.smooth(1)
    f.mix()
    st.save("normed", "mixed", "e", "mpad", "kern", "prow", "ema", "dd", "grow")
    for t in range(5, S + 1):
        step(t)
    load[1].start()
    step(S + 1)
    load[2].start()
    load[1].wait()
    f.values()
    st.save("val", "vslope")
    step(S + 2)
    load[3].start()
    load[2].wait()
    f.base()
    f.attend()
    st.save("lat", "res", "ars", "gated", "probs", "query", "keys")
    step(S + 3)
    load[4].start()
    load[3].wait()
    f.hidden()
    st.save("first", "hpre", "upd")
    f.norm_two()
    st.save("second")
    for t in range(S + 4, S + LAG):
        step(t)
    load[4].wait()
    f.up()
    st.save("inner", "uslope")
    weight_grad(s.inner, s.dd, gdown, s.turned, s.stage, ssem, place=unit_place(n, FF) if dims else None)
    step(S + LAG)
    if dims:
        gat.finish()
    st.close()


def unit_place(n, rows):
    return D * n // (2 * rows), rows // (32 * n)


def blocks_of(ref, n):
    return ref.reshape(n // 2, 2, ref.shape[0] // n, ref.shape[1])


def back_kernel(dims, n, count, *refs):
    r = Parts(refs)
    x, g, valid, v, mx, h, up, down, gdown = r.rest(9)
    ins = r.take(LOADED["back"])
    out, dxo = r.rest(2)
    gup, gh, gmx, gv = r.rest(4)
    reduced = r.rest(6) if dims else r.rest(1)
    st = Store("back", r, ins, {})
    s = st.s
    s.datt, s.dv, s.dx, s.dup, s.dsec = s.gated, s.vslope, s.first, s.inner, s.dn
    wsem, ssem = r.rest(2)
    ws = {k: Stream(w, s.ring, wsem) for k, w in (("down", down), ("up", up), ("h", h), ("mx", mx), ("v", v))}
    if dims:
        arrive, gsend, grecv = r.rest(3)
        rings = dict(zip(SCATTER_BUFS, r.rest(len(SCATTER_BUFS))))
        p = Place(dims)
        p.barrier_all(n)
        cols = lambda ref, lo, w: ref.at[:, :, :, pl.ds(lo, w)]
        up4, mx4 = blocks_of(gup, n), blocks_of(gmx, n)
        rv, rmx, rh, rup, rdown, rsmall = reduced
        halves = lambda o, row: [(o, row, 0, 0, D), (o, row + 32, 0, D, D)]
        units = [
            (gdown.at[0], halves(rdown, 0)),
            (gdown.at[1], halves(rdown, 64)),
            (cols(up4, 0, UNIT), [(rup, 0, 0, 0, UNIT)]),
            (cols(up4, UNIT, UNIT), [(rup, 0, UNIT, 0, UNIT)]),
            (gh.at[0], halves(rh, 0)),
            (blocks_of(gv, n), [(rv, 0, 0, 0, UNIT)]),
            (cols(mx4, 0, UNIT), [(rmx, 0, 0, 0, UNIT)]),
            (cols(mx4, UNIT, WIDE), [(rmx, 0, UNIT, 0, WIDE)]),
        ]
        sc = Scatter(p, [u[0] for u in units], rings, DEPTH, [u[1] for u in units], *r.rest(4))
        S = sc.stages()

        def step(t):
            for k, q in enumerate(UNIT_STARTS):
                if 0 <= t - q < S:
                    sc.stage(k, t - q)

        def give(i, dev, slot):
            return pltpu.make_async_remote_copy(
                src_ref=s.gsmall.at[dev // 2, dev % 2], dst_ref=arrive.at[slot], send_sem=gsend.at[i], recv_sem=grecv.at[i],
                device_id=(dev,), device_id_type=MESH,
            )
    else:
        S = 8
        step = lambda t: None
    st.fetch()
    ws["down"].prefetch()
    b = Backward(x, g, valid, s.prow, s.ema, None, s, s, s.grow, s.gema)
    grad = lambda *q, **kw: weight_grad(*q[:3], s.turned, s.stage, ssem, **kw)
    step(0)
    s.dn[...] = jnp.zeros(s.dn.shape, F32)
    b.pad_tail()
    st.need("inner", "uslope", "first", "dd", "prow", "grow")
    step(1)
    ws["down"].run(b.down_tile)
    ws["up"].prefetch()
    step(2)
    st.need("second")
    grad(s.second, s.dup, gup, start=0, stop=UNIT)
    step(3)
    grad(s.second, s.dup, gup, start=UNIT, stop=FF)
    step(4)
    b.output(out)
    ws["up"].run(b.second_tile)
    ws["h"].prefetch()
    step(5)
    st.need("hpre", "upd")
    b.norm_two()
    step(6)
    st.need("gated")
    grad(s.gated, s.dbase, gh, lo=C_HX, place=unit_place(n, VALUE_WIDTH) if dims else None)
    step(7)
    st.need("res", "ars")
    ws["h"].run(b.gated_tile)
    ws["mx"].prefetch()
    step(8)
    st.need("lat", "val", "vslope", "probs", "query", "keys")
    b.attend()
    st.need("normed")
    grad(s.normed, s.dv, gv)
    step(9)
    st.need("mixed")
    grad(s.mixed, s.dbase, gmx, start=0, stop=UNIT)
    step(10)
    grad(s.mixed, s.dbase, gmx, start=UNIT)
    step(11)
    st.need("e", "mpad")
    ws["mx"].run(b.mixed_tile)
    ws["v"].prefetch()
    step(12)
    ws["v"].run(b.normed_tile)
    st.need("kern")
    b.smooth_signal(0)
    step(13)
    b.smooth_signal(1)
    step(14)
    b.smooth_filter()
    step(15)
    st.need("ema")
    b.ema_grads()
    b.norm_one(dxo)
    step(16)
    pack_grads(n, count, s.grow, s.gema, s.full, s.gsmall)
    if dims:
        me = p.me

        @pl.loop(1, n)
        def _(i):
            give(i, (me + i) % n, i).start()

        for t in range(17, UNIT_STARTS[-1] + S):
            step(t)
        rsmall[...] = s.gsmall[me // 2, me % 2].astype(F32)

        @pl.loop(1, n)
        def _(i):
            give(i, me, i).wait()
            rsmall[...] += arrive[i].astype(F32)
    else:
        reduced[0][...] = s.gsmall[...]
    st.close()


UNIT_STARTS = (0, 1, 3, 4, 8, 9, 11, 12)


def run_kernel(body, ins, outs, scratch, cid):
    vm, hbm = pl.BlockSpec(memory_space=VM), pl.BlockSpec(memory_space=pl.ANY)
    params = dict(vmem_limit_bytes=LIMIT)
    if cid is not None:
        params.update(collective_id=cid, has_side_effects=True)
    return pl.pallas_call(
        body,
        out_shape=[jax.ShapeDtypeStruct(o[0], o[1]) for o in outs],
        in_specs=[vm if i[1] else hbm for i in ins],
        out_specs=[vm if o[2] else hbm for o in outs],
        scratch_shapes=scratch,
        compiler_params=pltpu.CompilerParams(**params),
    )(*[i[0] for i in ins])


def copy_kernel(k, *refs):
    ins, outs, bufs, sem = refs[:k], refs[k : 2 * k], refs[2 * k : 3 * k], refs[3 * k]
    get = [pltpu.make_async_copy(a, b, sem.at[i]) for i, (a, b) in enumerate(zip(ins, bufs))]
    put = [pltpu.make_async_copy(a, b, sem.at[k + i]) for i, (a, b) in enumerate(zip(bufs, outs))]
    for c in get:
        c.start()
    for c, d in zip(get, put):
        c.wait()
        d.start()
    for d in put:
        d.wait()


def settle(arrays):
    return run_kernel(
        functools.partial(copy_kernel, len(arrays)), [(a, False) for a in arrays], [(a.shape, a.dtype, False) for a in arrays],
        [VM(a.shape, a.dtype) for a in arrays] + [pltpu.SemaphoreType.DMA((2 * len(arrays),))], None,
    )


def layer(dims, n, count, x, g, valid, arrays):
    m = x.shape[0]
    table = size_table(n, count, m)
    dma = pltpu.SemaphoreType.DMA
    tmp = lambda names: [VM(*table[k]) for k in names]
    saved = lambda kind: [table[k] + (False,) for k in SAVED[kind]]
    whole = [(n * a.shape[0], a.shape[1]) if dims else a.shape for a in arrays]
    parts = [(q[0] // n, q[1]) for q in whole]
    split = lambda a: a.reshape(n // 2, 2, a.shape[0] // n, a.shape[1])
    held = lambda kind, k: tmp(HELD[kind]) + [dma((max(1, len(LOADED.get(kind, ()))),)), dma((max(1, len(SAVED[kind])),))] + [dma((k,)), dma((2,))]
    a = {}
    unit = lambda k: (k, n // 2, 2, 32, UNIT)

    scratch = held("front", 6)
    o = saved("front") + [(unit(2) if dims else whole[5], BF16, False)]
    if dims:
        ns = sems_needed(dims, 5)
        scratch += [dma((5,)), dma((n,)), dma((n,)), dma((ns,)), dma((ns,))]
        o += [(q, BF16, False) for q in whole[1:]]
    ins = [(x, True), (g, True), (valid, True)] + [(q, False) for q in arrays]
    res = run_kernel(functools.partial(front_kernel, dims, n, count), ins, o, scratch, 0 if dims else None)
    a.update(zip(SAVED["front"], res))
    res = res[len(SAVED["front"]) :]
    gdown = res[0]
    v, mx, h, up, down = res[1:] if dims else arrays[1:]

    ins = [(x, True), (g, True), (valid, True)] + [(q, False) for q in (v, mx, h, up, down, gdown)] + [(a[k], False) for k in LOADED["back"]]
    o = [((m, D), BF16, True)] * 2 + [(whole[4], BF16, False), (unit(1) if dims else whole[3], BF16, False), (whole[2], BF16, False), (whole[1], BF16, False)]
    scratch = held("back", 2)
    if dims:
        o += [(parts[i], F32, True) for i in (1, 2, 3, 4, 5)] + [((SMALL_ROWS, 128), F32, True)]
        scratch += [VM((n, SMALL_ROWS, 128), BF16), dma((n,)), dma((n,))]
        scratch += scatter_scratch(dims, 32, WIDE, DEPTH, len(UNIT_STARTS))
    else:
        o += [table["gsmall"] + (True,)]
    res = run_kernel(functools.partial(back_kernel, dims, n, count), ins, o, scratch, 1 if dims else None)
    out, dx = res[:2]
    if dims:
        gv, gmx, gh, gup, gdown, gs = res[6:]
    else:
        gup, gh, gmx, gv = res[2:6]
        gs = res[6].reshape(n * SMALL_ROWS, 128)
    return out, dx, gv, gmx, gh, gup, gdown, gs


def frame_in(small, me):
    count = small.shape[0]
    line = lax.dynamic_update_slice(jnp.zeros((FRAME * 128,), small.dtype), small, ((me * count) % 128,))
    return jnp.pad(line.reshape(FRAME, 128), ((0, SMALL_ROWS - FRAME), (0, 0)))


def frame_out(block, me, count):
    return lax.dynamic_slice(block.reshape(-1), ((me * count) % 128,), (count,))


def grid_of(n):
    return (n // 8, 2, 2)


def per_device(n, inputs, lengths, cotangent, v_weight, mx_weight, h_weight, up_weight, down_weight, small_params):
    shape = inputs.shape
    m, count = shape[0] * shape[1] * shape[2], small_params.shape[0]
    me = lax.axis_index("fsdp")
    x, g = inputs.reshape(m, D), cotangent.reshape(m, D)
    mask = (jnp.arange(shape[2]) < lengths[:, :, None]).astype(F32).reshape(m, 1)
    valid = jnp.broadcast_to(mask, (m, 128))
    arrays = (frame_in(small_params, me), v_weight, mx_weight, h_weight, up_weight, down_weight)
    dims = grid_of(n) if n == 32 else None
    if not dims:
        arrays = [lax.all_gather(a, "fsdp", axis=0, tiled=True) for a in arrays]
    out, dx, gv, gmx, gh, gup, gdown, gs = layer(dims, n, count, x, g, valid, arrays)
    if dims:
        out, dx, gv, gmx, gh, gup, gdown = settle((out, dx, gv, gmx, gh, gup, gdown))
    else:
        gv, gmx, gh, gup, gdown, gs = (
            lax.psum_scatter(a.astype(F32), "fsdp", scatter_dimension=0, tiled=True) for a in (gv, gmx, gh, gup, gdown, gs)
        )
    return out.reshape(shape), dx.reshape(shape), gv, gmx, gh, gup, gdown, frame_out(gs, me, count)


def solution(mesh):
    rows, cols = P("fsdp", None), P(None, "fsdp", None, None)
    return jax.shard_map(
        functools.partial(per_device, mesh.shape["fsdp"]),
        mesh=mesh,
        in_specs=(cols, P(None, "fsdp"), cols, rows, rows, rows, rows, rows, P("fsdp")),
        out_specs=(cols, cols, rows, rows, rows, rows, rows, P("fsdp")),
        check_vma=False,
    )
```

```python
import functools
import math

import jax
import jax.numpy as jnp
from jax import lax
from jax.experimental import pallas as pl
from jax.experimental.pallas import tpu as pltpu
from jax.sharding import PartitionSpec as P

D = 1024
Z = 128
VALUE_WIDTH = 2048
H = 16
FF = 4096
STRETCH = 128


epsilon = 1e-05

MESH = pl.DeviceIdType.MESH

class Place:
    def __init__(self, dims):
        self.Z, self.Y, self.X = dims
        me = lax.axis_index("fsdp")
        self.me = me
        self.c = me % 2
        self.x = (me // 2) % self.X
        self.y = (me // (2 * self.X)) % self.Y
        self.z = me // (2 * self.X * self.Y)
        self.nx = self.dev(self.z, self.y, 1 - self.x, self.c)
        self.ny = self.dev(self.z, 1 - self.y, self.x, self.c)
        self.nc = self.dev(self.z, self.y, self.x, 1 - self.c)
        self.has_down = self.z > 0
        self.has_up = self.z < self.Z - 1
        self.down = self.dev(jnp.maximum(self.z - 1, 0), self.y, self.x, self.c)
        self.up = self.dev(jnp.minimum(self.z + 1, self.Z - 1), self.y, self.x, self.c)
    def dev(self, z, y, x, c):
        return ((z * self.Y + y) * self.X + x) * 2 + c
    def barrier(self):
        bar = pltpu.get_barrier_semaphore()
        def tell(d):
            pl.semaphore_signal(bar, inc=1, device_id=(d,), device_id_type=MESH)
        for d in (self.nx, self.ny, self.nc):
            tell(d)
        pl.when(self.has_down)(lambda: tell(self.down))
        pl.when(self.has_up)(lambda: tell(self.up))
        pl.semaphore_wait(bar, 3 + jnp.where(self.has_down, 1, 0) + jnp.where(self.has_up, 1, 0))

    def barrier_all(self, n):
        bar = pltpu.get_barrier_semaphore()

        @pl.loop(1, n)
        def _(i):
            pl.semaphore_signal(bar, inc=1, device_id=((self.me + i) % n,), device_id_type=MESH)

        pl.semaphore_wait(bar, n - 1)

def when(cond, f):
    if cond is None: f()
    else: pl.when(cond)(f)

class Gather:
    def __init__(self, place, ins, outs, send_sem, recv_sem):
        self.p, self.ins, self.outs = place, ins, outs
        self.ss, self.rs = send_sem, recv_sem
        self.ids, self.pend = {}, []
    def rows(self, k, h):
        n = self.ins[k].shape[0]
        return (0, n) if h == 2 else (h * (n // 2), n // 2)
    def copy(self, key, k, shard, h, to, own=False):
        i = self.ids.setdefault((key, k), len(self.ids))
        r, n = self.rows(k, h)
        full = self.ins[k].shape[0]
        dst = self.outs[k].at[pl.ds(shard * full + r, n)]
        src = self.ins[k].at[pl.ds(r, n)] if own else dst
        return pltpu.make_async_remote_copy(src_ref=src, dst_ref=dst, send_sem=self.ss.at[i], recv_sem=self.rs.at[i], device_id=(to,), device_id_type=MESH)
    def send(self, cond, *a):
        when(cond, lambda: self.copy(*a).start())
        self.pend.append((cond, lambda: self.copy(*a).wait_send()))
    def recv(self, cond, key, k, shard, h):
        when(cond, lambda: self.copy(key, k, shard, h, self.p.me).wait_recv())
    def col(self, o):
        p = self.p
        if o == 0: return None, p.z
        if o > 0: return p.z - o >= 0, jnp.maximum(p.z - o, 0)
        return p.z - o <= p.Z - 1, jnp.minimum(p.z - o, p.Z - 1)
    def offs(self, s):
        return (0,) if s == 0 else (s, -s)
    def stage(self, k, s):
        p = self.p
        L = p.Z
        if s < L:
            for o in self.offs(s):
                cond, zz = self.col(o)
                sh = p.dev(zz, p.y, p.x, p.c)
                own = o == 0
                if not own:
                    self.recv(cond, ("z", o), k, sh, 2)
                if s + 1 < L:
                    both = lambda c1: c1 if cond is None else jnp.logical_and(cond, c1)
                    if o >= 0: self.send(both(p.has_up), ("z", s + 1), k, sh, 2, p.up, own)
                    if o <= 0: self.send(both(p.has_down), ("z", -(s + 1)), k, sh, 2, p.down, own)
                if abs(o) != 1:
                    self.send(cond, ("x", o), k, sh, 2, p.nx, own)
                    self.send(cond, ("y", o), k, sh, 2, p.ny, own)
                self.send(cond, ("c", o), k, sh, 2, p.nc, own)
        if 1 <= s <= L:
            for o in self.offs(s - 1):
                cond, zz = self.col(o)
                sx, sy = p.dev(zz, p.y, 1 - p.x, p.c), p.dev(zz, 1 - p.y, p.x, p.c)
                for key, sh, half, to in (("x", sx, 0, p.ny), ("y", sy, 1, p.nx)):
                    self.recv(cond, (key, o), k, sh, 2)
                    if o == 0:
                        self.send(p.has_up, (key, 1), k, sh, 2, p.up)
                        self.send(p.has_down, (key, -1), k, sh, 2, p.down)
                    self.send(cond, ("d" + key, o), k, sh, half, to)
                    self.send(cond, ("c" + key, o), k, sh, 2, p.nc)
        if 2 <= s <= L + 1:
            for o in self.offs(s - 2):
                cond, zz = self.col(o)
                sd = p.dev(zz, 1 - p.y, 1 - p.x, p.c)
                self.recv(cond, ("dx", o), k, sd, 0)
                self.recv(cond, ("dy", o), k, sd, 1)
                self.send(cond, ("cd", o), k, sd, 2, p.nc)
        if s == L + 2:
            for t in range(L):
                for o in self.offs(t):
                    cond, zz = self.col(o)
                    for key, yy, xx in (("c", p.y, p.x), ("cx", p.y, 1 - p.x), ("cy", 1 - p.y, p.x), ("cd", 1 - p.y, 1 - p.x)):
                        self.recv(cond, (key, o), k, p.dev(zz, yy, xx, 1 - p.c), 2)
    def stages(self):
        return self.p.Z + 3
    def finish(self):
        for cond, f in self.pend:
            when(cond, f)

def sems_needed(dims, K):
    Z = dims[0]
    return K * (2 * (Z - 1) + 8 * (2 * Z - 1) + 4)


F32, BF16 = jnp.float32, jnp.bfloat16
TILE = 256
O_GAIN, O_SHIFT, O_OMEGA, O_AFF, O_REL = 0, 2 * D, 4 * D, 5 * D, 5 * D + 4 * Z
O_VB = O_REL + STRETCH
O_MXB = O_VB + VALUE_WIDTH
MXW = 2 * D + Z + VALUE_WIDTH
O_HB = O_MXB + MXW
O_UPB = O_HB + D
O_DNB = O_UPB + FF
O_EMA = O_DNB + D
C_LAT, C_RES, C_HX = D, D + Z, D + Z + VALUE_WIDTH


def sigmoid(v):
    return 0.5 * jnp.tanh(0.5 * v) + 0.5


def silu_slope(v, s):
    return s * (1.0 + v * (1.0 - s))


def col_sum(v):
    return jnp.sum(v, axis=0, keepdims=True)


def dot(a, b, ca=1, cb=0):
    return lax.dot_general(a, b, (((ca,), (cb,)), ((), ())), preferred_element_type=F32)


def tiles(lo, hi, step, f):
    @pl.loop(0, (hi - lo) // step)
    def _(i):
        f(pl.multiple_of(lo + i * step, 128))


def lane_block(l):
    return pl.ds(pl.multiple_of(l * 128, 128), 128)


def center(xf):
    c = xf - jnp.mean(xf, axis=-1, keepdims=True)
    r = lax.rsqrt(jnp.mean(c * c, axis=-1, keepdims=True) + epsilon)
    return c * r, r


def ema_rates(ema):
    gate, a = sigmoid(ema[0]), sigmoid(ema[1])
    retain = 1.0 - gate * a
    weight = gate * ema[2] * ema[3] * (1.0 / math.sqrt(H))
    return gate, a, retain, weight


def rel_table(rel_row):
    wide = jnp.broadcast_to(rel_row, (STRETCH, STRETCH))
    return pltpu.roll(wide, 0, 1, stride=1, stride_axis=0).T


def causal():
    i = lax.broadcasted_iota(jnp.int32, (STRETCH, STRETCH), 0)
    j = lax.broadcasted_iota(jnp.int32, (STRETCH, STRETCH), 1)
    return j <= i


class Forward:
    def __init__(self, x, valid, prow, ema, w, s):
        self.x, self.valid, self.prow, self.ema, self.w, self.s = x, valid, prow, ema, w, s
        self.m = x.shape[0]
        self.seqs = self.m // STRETCH

    def p(self, lo, n):
        return self.prow[:, lo : lo + n]

    def pd(self, lo, col, n):
        return self.prow[:, pl.ds(pl.multiple_of(lo + col, 128), n)]

    def norm_one(self):
        s = self.s
        g, b = self.p(O_GAIN, D), self.p(O_SHIFT, D)
        for q in range(self.seqs):
            s.mpad[q, 0:8, :] = jnp.zeros((8, D), F32)

            @pl.loop(0, STRETCH // 32)
            def _(i):
                r = pl.ds(q * STRETCH + i * 32, 32)
                xhat, _ = center(self.x[r, :].astype(F32))
                n = xhat * g + b
                s.normed[r, :] = n.astype(BF16)
                s.mpad[q, pl.ds(8 + i * 32, 32), :] = n * self.valid[r, 0:1]

    def ema_kernel(self):
        _, _, retain, weight = ema_rates(self.ema)

        def step(j, p):
            self.s.kern[pl.ds(j, 1), :] = col_sum(p)
            return p * retain

        lax.fori_loop(0, STRETCH, step, weight)

    def smooth(self, q):
        s = self.s
        for q in (q,):

            @pl.loop(0, D // 128)
            def _(l):
                lb = lane_block(l)
                om = self.prow[:, pl.ds(pl.multiple_of(O_OMEGA + l * 128, 128), 128)]
                nb = STRETCH // 8
                acc = [om * s.mpad[q, 8 + 8 * i : 16 + 8 * i, lb] for i in range(nb)]
                for b in range(8):
                    sh = [s.mpad[q, 8 - b + 8 * i : 16 - b + 8 * i, lb] for i in range(nb)]
                    for a in range(nb):
                        kb = jnp.broadcast_to(s.kern[8 * a + b : 8 * a + b + 1, lb], (8, 128))
                        for i in range(a, nb):
                            acc[i] = acc[i] + kb * sh[i - a]
                for i in range(nb):
                    r = slice(q * STRETCH + 8 * i, q * STRETCH + 8 * i + 8)
                    s.e[r, lb] = acc[i]

    def mix(self):
        s = self.s

        @pl.loop(0, self.m // 32)
        def _(i):
            r = pl.ds(i * 32, 32)
            e = s.e[r, :]
            s.mixed[r, :] = (e * sigmoid(e)).astype(BF16)

    def values(self):
        s = self.s

        def one(col):
            cols = pl.ds(col, TILE)
            v = dot(s.normed[...], self.w.v[:, cols]) + self.pd(O_VB, col, TILE)
            sv = sigmoid(v)
            s.vslope[:, cols] = silu_slope(v, sv).astype(BF16)
            s.val[:, cols] = (v * sv).astype(BF16)

        tiles(0, VALUE_WIDTH, TILE, one)

    def base_one(self):
        s = self.s

        def f(dst, lo, width):
            def one(col):
                dst[:, pl.ds(pl.multiple_of(col - lo, 128), width)] = dot(s.mixed[...], self.w.mx1[:, pl.ds(col, width)]) + self.pd(O_MXB, col, width)

            return one

        def gate(col):
            cols = pl.ds(col, TILE)
            s.upd[:, cols] = sigmoid(dot(s.mixed[...], self.w.mx1[:, cols]) + self.pd(O_MXB, col, TILE))

        tiles(0, D, TILE, gate)
        s.lat[...] = dot(s.mixed[...], self.w.mx1[:, C_LAT:C_RES]) + self.p(O_MXB + C_LAT, Z)
        tiles(C_RES, C_RES + D, TILE, f(s.first, C_RES, TILE))

    def base_two(self):
        s = self.s

        def f(dst, lo):
            def one(col):
                here = pl.multiple_of(lo + col, 128)
                v = dot(s.mixed[...], self.w.mx2[:, pl.ds(here, TILE)]) + self.pd(O_MXB + C_RES + D, here, TILE)
                dst[:, pl.ds(col, TILE)] = v

            return one

        tiles(0, D, TILE, f(s.dn, 0))
        tiles(0, D, TILE, f(s.hpre, D))

    def attend(self):
        s = self.s
        table, mask = rel_table(self.p(O_REL, STRETCH)), causal()
        for q in range(self.seqs):
            r = slice(q * STRETCH, (q + 1) * STRETCH)
            b = s.lat[r, :]
            lat = b * sigmoid(b)
            query = (lat * (1.0 + self.p(O_AFF, Z)) + self.p(O_AFF + 2 * Z, Z)).astype(BF16)
            keys = (lat * (1.0 + self.p(O_AFF + Z, Z)) + self.p(O_AFF + 3 * Z, Z)).astype(BF16)
            sc = jnp.where(mask, dot(query, keys, 1, 1) * (1.0 / math.sqrt(Z)) + table, -1e30)
            ex = jnp.exp(sc - jnp.max(sc, axis=-1, keepdims=True))
            pr = ex / jnp.sum(ex, axis=-1, keepdims=True)
            s.probs[r, :] = pr
            s.query[r, :] = query
            s.keys[r, :] = keys
            low = pr.astype(BF16)

            def one(half, pre, col):
                cols = pl.ds(pl.multiple_of(half + col, 128), TILE)
                at = dot(low, s.val[r, cols])
                bb = pre[r, pl.ds(col, TILE)]
                sb = sigmoid(bb)
                res = bb * sb
                s.res[r, cols] = res.astype(BF16)
                s.ars[r, cols] = (at * silu_slope(bb, sb)).astype(BF16)
                s.gated[r, cols] = (at * res).astype(BF16)

            tiles(0, D, TILE, functools.partial(one, 0, s.first))
            tiles(0, D, TILE, functools.partial(one, D, s.dn))

    def hidden(self):
        s = self.s

        def one(col):
            cols = pl.ds(col, TILE)
            h = dot(s.gated[:, 0:D], self.w.h1[:, cols]) + dot(s.gated[:, D : 2 * D], self.w.h2[:, cols])
            h = s.hpre[:, cols] + h + self.pd(O_HB, col, TILE)
            s.hpre[:, cols] = h
            xf = self.x[:, cols].astype(F32)
            s.first[:, cols] = xf + self.valid[:, 0:1] * s.upd[:, cols] * (h * sigmoid(h) - xf)

        tiles(0, D, TILE, one)

    def norm_two(self):
        s = self.s
        g, b = self.p(O_GAIN + D, D), self.p(O_SHIFT + D, D)

        @pl.loop(0, self.m // 32)
        def _(i):
            r = pl.ds(i * 32, 32)
            xhat, _ = center(s.first[r, :])
            s.second[r, :] = (xhat * g + b).astype(BF16)

    def up(self, half):
        s = self.s
        w, lo = (self.w.up1, 0) if half == 0 else (self.w.up2, FF // 2)

        def one(col):
            cols = pl.ds(pl.multiple_of(lo + col, 128), TILE)
            u = dot(s.second[...], w[:, pl.ds(col, TILE)]) + self.pd(O_UPB + lo, col, TILE)
            su = sigmoid(u)
            s.uslope[:, cols] = silu_slope(u, su).astype(BF16)
            s.inner[:, cols] = (u * su).astype(BF16)

        tiles(0, FF // 2, TILE, one)


class Backward:
    def __init__(self, x, g, valid, prow, ema, w, s, t, grow, gema):
        self.x, self.g, self.valid, self.prow, self.ema = x, g, valid, prow, ema
        self.w, self.s, self.t, self.grow, self.gema = w, s, t, grow, gema
        self.m = x.shape[0]
        self.seqs = self.m // STRETCH

    p, pd = Forward.p, Forward.pd

    def put(self, lo, col, n, v):
        self.grow[:, pl.ds(pl.multiple_of(lo + col, 128), n)] = v

    def cot(self):
        def one(col):
            cols = pl.ds(col, TILE)
            d = self.valid[:, 0:1] * self.g[:, cols].astype(F32)
            self.put(O_DNB, col, TILE, col_sum(d))
            self.t.dd[:, cols] = d.astype(BF16)

        tiles(0, D, TILE, one)

    def down_tile(self, col, w):
        s, t = self.s, self.t
        cols = pl.ds(col, TILE)
        t.dn[...] += dot(s.inner[:, cols], w[...])
        di = dot(t.dd[...], w[...], 1, 1)
        du = di * s.uslope[:, cols].astype(F32)
        self.put(O_UPB, col, TILE, col_sum(du))
        t.dup[:, cols] = du.astype(BF16)

    def output(self, out):
        s, t = self.s, self.t

        def one(col):
            cols = pl.ds(col, TILE)
            d = t.dn[:, cols] + self.pd(O_DNB, col, TILE)
            out[:, cols] = (s.first[:, cols] + self.valid[:, 0:1] * d).astype(BF16)

        tiles(0, D, TILE, one)

    def second_tile(self, col, w):
        self.t.dsec[:, pl.ds(col, TILE)] = dot(self.t.dup[...], w[...], 1, 1)

    def norm_two(self):
        s, t = self.s, self.t
        g = self.p(O_GAIN + D, D)
        t.acc[...] = jnp.zeros(t.acc.shape, F32)

        def add(k, v):
            t.acc[k] += jnp.sum(v.reshape(v.shape[0] // 8, 8, D), axis=0)

        @pl.loop(0, self.m // 32)
        def _(i):
            r = pl.ds(i * 32, 32)
            xhat, rstd = center(s.first[r, :])
            ds = t.dsec[r, :]
            add(0, ds * xhat)
            add(1, ds)
            dh = ds * g
            dn = rstd * (dh - jnp.mean(dh, axis=-1, keepdims=True) - xhat * jnp.mean(dh * xhat, axis=-1, keepdims=True))
            df = self.g[r, :].astype(F32) + dn
            v = self.valid[r, 0:1]
            u = s.upd[r, :]
            hp = s.hpre[r, :]
            sh = sigmoid(hp)
            xf = self.x[r, :].astype(F32)
            vu = v * u
            t.dx[r, :] = df - df * vu
            db = df * v * (hp * sh - xf) * u * (1.0 - u)
            add(2, db)
            t.dbase[r, 0:D] = db.astype(BF16)
            dhp = df * vu * silu_slope(hp, sh)
            add(3, dhp)
            t.dbase[r, C_HX:MXW] = dhp.astype(BF16)

        for k, lo in enumerate((O_GAIN + D, O_SHIFT + D, O_MXB, O_HB)):
            self.grow[:, lo : lo + D] = col_sum(t.acc[k])
        self.grow[:, O_MXB + C_HX : O_MXB + MXW] = col_sum(t.acc[3])

    def gated_tile(self, col, w):
        s, t = self.s, self.t
        cols = pl.ds(col, TILE)
        bcols = pl.ds(pl.multiple_of(C_RES + col, 128), TILE)
        dg = dot(t.dbase[:, C_HX:MXW], w[...], 1, 1)
        t.datt[:, cols] = (dg * s.res[:, cols].astype(F32)).astype(BF16)
        db = dg * s.ars[:, cols].astype(F32)
        self.put(O_MXB + C_RES, col, TILE, col_sum(db))
        t.dbase[:, bcols] = db.astype(BF16)

    def attend(self):
        s, t = self.s, self.t
        mask = causal()
        lows, drel = [], None
        aff = [0.0, 0.0, 0.0, 0.0]
        lat_bias = 0.0
        for q in range(self.seqs):
            r = slice(q * STRETCH, (q + 1) * STRETCH)
            pr = s.probs[r, :]
            lows.append(pr.astype(BF16))
            dp = dot(t.datt[r, :], s.val[r, :], 1, 1)
            ds = pr * (dp - jnp.sum(pr * dp, axis=-1, keepdims=True))
            ds = jnp.where(mask, ds, 0.0)
            drel = ds if drel is None else drel + ds
            raw = (ds * (1.0 / math.sqrt(Z))).astype(BF16)
            dq = dot(raw, s.keys[r, :])
            dk = dot(raw, s.query[r, :], 0, 0)
            b = s.lat[r, :]
            sb = sigmoid(b)
            lat = b * sb
            for k, v in enumerate((dq * lat, dk * lat, dq, dk)):
                aff[k] = aff[k] + col_sum(v)
            dl = dq * (1.0 + self.p(O_AFF, Z)) + dk * (1.0 + self.p(O_AFF + Z, Z))
            db = dl * silu_slope(b, sb)
            lat_bias = lat_bias + col_sum(db)
            t.dbase[r, C_LAT:C_RES] = db.astype(BF16)
        for k in range(4):
            self.grow[:, O_AFF + k * Z : O_AFF + (k + 1) * Z] = aff[k]
        self.grow[:, O_MXB + C_LAT : O_MXB + C_RES] = lat_bias
        drel = drel.T
        eight = 0.0
        for i in range(0, STRETCH, 8):
            eight = eight + pltpu.roll(drel[i : i + 8, :], (STRETCH - i) % STRETCH, 1)
        back = 0.0
        for i in range(8):
            back = back + pltpu.roll(eight[i : i + 1, :], (STRETCH - i) % STRETCH, 1)
        self.grow[:, O_REL : O_REL + STRETCH] = back

        def one(col):
            cols = pl.ds(col, TILE)
            bias = 0.0
            for q in range(self.seqs):
                r = slice(q * STRETCH, (q + 1) * STRETCH)
                dv = dot(lows[q], t.datt[r, cols], 0, 0)
                dv = dv * s.vslope[r, cols].astype(F32)
                bias = bias + col_sum(dv)
                t.dv[r, cols] = dv.astype(BF16)
            self.put(O_VB, col, TILE, bias)

        tiles(0, VALUE_WIDTH, TILE, one)

    def pad_tail(self):
        for q in range(self.seqs):
            self.t.dpad[q, STRETCH : STRETCH + 8, :] = jnp.zeros((8, D), F32)

    def mixed_tile(self, col, w):
        s, t = self.s, self.t
        cols = pl.ds(col, TILE)
        dm = dot(t.dbase[...], w[...], 1, 1)
        e = s.e[:, cols]
        de = dm * silu_slope(e, sigmoid(e))
        om = 0.0
        for q in range(self.seqs):
            d = de[q * STRETCH : (q + 1) * STRETCH, :]
            t.dpad[q, 0:STRETCH, cols] = d
            om = om + col_sum(d * s.mpad[q, 8 : 8 + STRETCH, cols])
        self.put(O_OMEGA, col, TILE, om)

    def normed_tile(self, col, w):
        self.t.dn[:, pl.ds(col, TILE)] = dot(self.t.dv[...], w[...], 1, 1)

    def smooth_signal(self, seq):
        s, t = self.s, self.t
        nb = STRETCH // 8

        @pl.loop(0, D // 128)
        def _(l):
            lb = lane_block(l)
            om = self.prow[:, pl.ds(pl.multiple_of(O_OMEGA + l * 128, 128), 128)]
            for q in (seq,):
                acc = [om * t.dpad[q, 8 * i : 8 * i + 8, lb] for i in range(nb)]
                for b in range(8):
                    sh = [t.dpad[q, 8 * i + b : 8 * i + b + 8, lb] for i in range(nb)]
                    for a in range(nb):
                        kb = jnp.broadcast_to(s.kern[8 * a + b : 8 * a + b + 1, lb], (8, 128))
                        for i in range(nb - a):
                            acc[i] = acc[i] + kb * sh[i + a]
                for i in range(nb):
                    r = slice(q * STRETCH + 8 * i, q * STRETCH + 8 * i + 8)
                    t.dn[r, lb] = t.dn[r, lb] + self.valid[r, :] * acc[i]

    def smooth_filter(self):
        s, t = self.s, self.t
        nb = STRETCH // 8

        @pl.loop(0, D // 128)
        def _(l):
            lb = lane_block(l)
            for b in range(8):
                sums = [None] * nb
                for q in range(self.seqs):
                    de = [t.dpad[q, 8 * i : 8 * i + 8, lb] for i in range(nb)]
                    sh = [s.mpad[q, 8 - b + 8 * i : 16 - b + 8 * i, lb] for i in range(nb)]
                    for a in range(nb):
                        for i in range(a, nb):
                            v = de[i] * sh[i - a]
                            sums[a] = v if sums[a] is None else sums[a] + v
                for a in range(nb):
                    t.dkern[8 * a + b : 8 * a + b + 1, lb] = col_sum(sums[a])

    def norm_one(self, out):
        t = self.t
        g = self.p(O_GAIN, D)
        t.acc[...] = jnp.zeros(t.acc.shape, F32)

        def add(k, v):
            t.acc[k] += jnp.sum(v.reshape(v.shape[0] // 8, 8, D), axis=0)

        @pl.loop(0, self.m // 32)
        def _(i):
            r = pl.ds(i * 32, 32)
            xhat, rstd = center(self.x[r, :].astype(F32))
            dn = t.dn[r, :]
            add(0, dn * xhat)
            add(1, dn)
            dh = dn * g
            d = rstd * (dh - jnp.mean(dh, axis=-1, keepdims=True) - xhat * jnp.mean(dh * xhat, axis=-1, keepdims=True))
            out[r, :] = (t.dx[r, :] + d).astype(BF16)

        for k, lo in enumerate((O_GAIN, O_SHIFT)):
            self.grow[:, lo : lo + D] = col_sum(t.acc[k])


    def ema_grads(self):
        t = self.t
        scale = 1.0 / math.sqrt(H)

        @pl.loop(0, D // 128)
        def _(l):
            lb = lane_block(l)
            par = self.ema[:, :, lb]
            gate, a, retain, weight = ema_rates(par)
            zero = retain - retain

            def eight(k, carry):
                power, before, dw, dr = carry
                rows = t.dkern[pl.ds(pl.multiple_of(8 * k, 8), 8), lb]
                for i in range(8):
                    row = rows[i : i + 1, :]
                    dw = dw + row * power
                    dr = dr + (row * (8 * k + i).astype(F32)) * before
                    power, before = power * retain, power
                return power, before, dw, dr

            _, _, dw, dr = lax.fori_loop(0, STRETCH // 8, eight, (zero + 1.0, zero, zero, zero))
            drate = -dr * weight
            dgate = drate * a + dw * par[2] * par[3] * scale
            self.gema[0, :, lb] = dgate * gate * (1.0 - gate)
            self.gema[1, :, lb] = drate * gate * a * (1.0 - a)
            self.gema[2, :, lb] = dw * gate * par[3] * scale
            self.gema[3, :, lb] = dw * gate * par[2] * scale


class Scatter:
    def __init__(self, place, grads, pool, depth, outs, send_sem, recv_sem, local_sem, credit, first):
        self.ready = first
        self.p, self.grads, self.outs, self.depth, self.credit = place, grads, outs, depth, credit
        self.bufs = []
        for k, g in enumerate(grads):
            wide, w = pool.shape[1], pl.ds(0, g.shape[-1])
            lo = (k % depth) * (pool.shape[0] // depth)
            views = {}
            for name, (q, r) in unit_buffers((place.Z, place.Y, place.X), g.shape[-2]).items():
                views[name] = pool.at[pl.ds(lo, q * r)].reshape(q, r, wide).at[:, :, w]
                lo += q * r
            self.bufs.append(Names(**views))
        self.ss, self.rs, self.ls = send_sem, recv_sem, local_sem
        self.ids, self.pend = {}, [[] for _ in grads]

    def around(self):
        p = self.p
        return ((None, p.nc), (None, p.nx), (None, p.ny), (p.has_up, p.up), (p.has_down, p.down))

    def release(self, k):
        self.finish(k)
        if k + self.depth < len(self.grads):
            for i, (cond, to) in enumerate(self.around()):
                slot = (0, 1, 2, 4, 3)[i]
                when(cond, lambda slot=slot, to=to: pl.semaphore_signal(self.credit.at[k, slot], inc=1, device_id=(to,), device_id_type=MESH))

    def open(self):
        for i, (cond, to) in enumerate(self.around()):
            slot = (0, 1, 2, 4, 3)[i]
            when(cond, lambda slot=slot, to=to: pl.semaphore_signal(self.ready.at[slot], inc=1, device_id=(to,), device_id_type=MESH))

    def entered(self):
        for i, (cond, to) in enumerate(self.around()):
            when(cond, lambda i=i: pl.semaphore_wait(self.ready.at[i], 1))

    def admit(self, k):
        if k == 0:
            self.entered()
        if k >= self.depth:
            for i, (cond, to) in enumerate(self.around()):
                when(cond, lambda i=i: pl.semaphore_wait(self.credit.at[k - self.depth, i], 1))

    def copy(self, key, k, src, dst, to):
        i = self.ids.setdefault((key, k), len(self.ids))
        return pltpu.make_async_remote_copy(src_ref=src, dst_ref=dst, send_sem=self.ss.at[i], recv_sem=self.rs.at[i], device_id=(to,), device_id_type=MESH)

    def send(self, cond, key, k, src, dst, to):
        when(cond, lambda: self.copy(key, k, src, dst, to).start())
        self.pend[k].append((cond, lambda: self.copy(key, k, src, dst, to).wait_send()))

    def recv(self, cond, key, k, dst):
        when(cond, lambda: self.copy(key, k, dst, dst, self.p.me).wait_recv())

    def own(self, k, z):
        p, b = self.p, self.bufs[k]
        layer = p.Y * p.X
        i = k * p.Z + z
        return pltpu.make_async_copy(self.grads[k].at[pl.ds(z * layer, layer), p.c], b.mine.at[pl.ds((z % 2) * layer, layer)], self.ls.at[i])

    def add(self, dst, a, b, r0=0, rows=None):
        n = rows

        @pl.loop(0, n // 16)
        def _(i):
            def at(v, r):
                ref, q, off = v
                return ref.at[q, pl.ds(pl.multiple_of(off + r, 16), 16)]

            r = i * 16
            at(dst, r)[...] = at(a, r)[...] + at(b, r)[...]

    def stage(self, k, s):
        p, b = self.p, self.bufs[k]
        layer = p.Y * p.X
        r = b.sum.shape[1]
        half = r // 2
        chip = lambda z, y, x: (z * p.Y + y) * p.X + x
        col = lambda z: (chip(z, p.y, p.x), chip(z, p.y, 1 - p.x), chip(z, 1 - p.y, p.x), chip(z, 1 - p.y, 1 - p.x))
        L = p.Z
        planes = range(L)
        off = lambda z, d: p.z == z + d
        far = lambda z: jnp.logical_and(p.z != z - 1, p.z != z + 1)
        apart = lambda z: jnp.logical_and(far(z), p.z != z)
        S, H0, H1 = b.sum, 0, half
        if s == 0:
            self.admit(k)
            for z in planes:
                self.send(None, ("c", z), k, self.grads[k].at[pl.ds(z * layer, layer), 1 - p.c], S.at[pl.ds(z * layer, layer)], p.nc)
                if z < 2:
                    self.own(k, z).start()
        if s == 1:
            for z in planes:
                self.recv(None, ("c", z), k, S.at[pl.ds(z * layer, layer)])
                self.own(k, z).wait()
                me, nx, ny, nd = col(z)
                back = (z - z % 2) * layer
                self.add((S, nd, 0), (S, nd, 0), (b.mine, nd - back, 0), rows=r)
                self.send(None, ("dy", z), k, S.at[nd, pl.ds(0, half)], b.dy.at[z], p.ny)
                self.send(None, ("dx", z), k, S.at[nd, pl.ds(half, half)], b.dx.at[z], p.nx)
                for q in (nx, ny, me):
                    self.add((S, q, 0), (S, q, 0), (b.mine, q - back, 0), rows=r)
                if z + 2 < L:
                    self.own(k, z + 2).start()
        if s == 2:
            for z in planes:
                me, nx, ny, nd = col(z)
                for key, q, h, buf, to, out in (("dy", nx, H0, b.dy, p.nx, b.rx), ("dx", ny, H1, b.dx, p.ny, b.ry)):
                    self.recv(None, (key, z), k, buf.at[z])
                    self.add((S, q, h), (S, q, h), (buf, z, 0), rows=half)
                    tag = "x" if key == "dy" else "y"
                    side = 0 if key == "dy" else 1
                    self.send(apart(z), (tag, z), k, S.at[q], out.at[z], to)
                    if z > 0:
                        self.send(off(z, -1), ("z" + tag, 0), k, S.at[q], b.rz.at[side], p.up)
                    if z < L - 1:
                        self.send(off(z, 1), ("z" + tag, 1), k, S.at[q], b.rz.at[2 + side], p.down)
        if s == 3:
            me, nx, ny, nd = col(p.z)
            for tag, q, side, to, out in (("x", nx, 0, p.nx, b.rx), ("y", ny, 1, p.ny, b.ry)):
                for cond, way in ((p.has_down, 0), (p.has_up, 1)):

                    def take(q=q, side=side, way=way, tag=tag):
                        self.copy(("z" + tag, way), k, b.rz.at[2 * way + side], b.rz.at[2 * way + side], p.me).wait_recv()
                        self.add((S, q, 0), (S, q, 0), (b.rz, 2 * way + side, 0), rows=r)

                    pl.when(cond)(take)
                for z in planes:
                    self.send(p.z == z, (tag, z), k, S.at[q], out.at[z], to)
        if s == 4:
            for z in planes:
                me = col(z)[0]
                for tag, buf in (("y", b.ry), ("x", b.rx)):

                    def take(me=me, tag=tag, buf=buf, z=z):
                        self.copy((tag, z), k, buf.at[z], buf.at[z], p.me).wait_recv()
                        self.add((S, me, 0), (S, me, 0), (buf, z, 0), rows=r)

                    pl.when(far(z))(take)
        if 4 <= s < 4 + L - 1:
            hop = s - 4
            for up in (True, False):
                zz = hop if up else L - 1 - hop
                buf, key, to = (b.ru, "u", p.up) if up else (b.rd, "d", p.down)
                here = p.z == zz
                for t in range(L - 1, zz, -1) if up else range(0, zz):
                    q = chip(t, p.y, p.x)

                    def relay(q=q, t=t, buf=buf, key=key):
                        self.copy((key, t), k, buf.at[t], buf.at[t], p.me).wait_recv()
                        self.add((S, q, 0), (S, q, 0), (buf, t, 0), rows=r)

                    if hop > 0:
                        pl.when(here)(relay)
                    self.send(here, (key, t), k, S.at[q], buf.at[t], to)
        if s == 4 + L - 1:
            me = chip(p.z, p.y, p.x)
            for key, buf, ts in (("", None, (0,)), ("u", b.ru, range(1, L)), ("d", b.rd, range(0, L - 1))):
                for t in ts:

                    def last(key=key, buf=buf, t=t):
                        if buf is not None:
                            self.copy((key, t), k, buf.at[t], buf.at[t], p.me).wait_recv()

                        @pl.loop(0, r // 16)
                        def _(i):
                            rr = pl.ds(pl.multiple_of(i * 16, 16), 16)
                            v = (S[me, rr, :] if buf is None else buf[t, rr, :]).astype(F32)
                            for out, row, col, lo, w in self.outs[k]:
                                o = out.at[pl.ds(pl.multiple_of(row + i * 16, 16), 16), col : col + w]
                                if buf is None:
                                    o[...] = v[:, lo : lo + w]
                                else:
                                    o[...] += v[:, lo : lo + w]

                    when(None if buf is None else p.z == t, last)
            self.release(k)

    def stages(self):
        return 4 + self.p.Z

    def finish(self, k):
        for cond, f in self.pend[k]:
            when(cond, f)
        self.pend[k] = []


class Names:
    def __init__(self, **kw):
        self.__dict__.update(kw)


SCATTER_BUFS = ("mine", "sum", "dx", "dy", "rx", "ry", "ru", "rd", "rz")


def unit_buffers(dims, r):
    Z, Y, X = dims
    return dict(
        mine=(2 * Y * X, r), sum=(Z * Y * X, r), dx=(Z, r // 2), dy=(Z, r // 2), rx=(Z, r), ry=(Z, r), ru=(Z, r), rd=(Z, r), rz=(4, r)
    )


def scatter_sems(dims, K):
    ns = K * (7 * dims[0] + 4)
    dma, plain = pltpu.SemaphoreType.DMA, pltpu.SemaphoreType.REGULAR
    return [dma((ns,)), dma((ns,)), dma((K * dims[0],)), plain((K, 5)), plain((5,))]


KEPT_OLD = ("normed", "mpad", "e", "mixed", "kern", "vslope", "val", "base", "probs", "query", "keys", "att", "gated", "hpre", "first", "second", "uslope", "inner")


def kept_shapes(m):
    seqs = m // STRETCH
    f, b = (lambda *s: (s, F32)), (lambda *s: (s, BF16))
    return dict(
        normed=b(m, D), mpad=f(seqs, STRETCH + 8, D), e=f(m, D), mixed=b(m, D), kern=f(STRETCH, D),
        vslope=b(m, VALUE_WIDTH), val=b(m, VALUE_WIDTH), base=f(m, MXW), probs=f(m, STRETCH),
        query=b(m, Z), keys=b(m, Z), upd=f(m, D), lat=f(m, Z), res=b(m, VALUE_WIDTH), ars=b(m, VALUE_WIDTH), gated=b(m, VALUE_WIDTH), hpre=f(m, D),
        first=f(m, D), second=b(m, D), uslope=b(m, FF), inner=b(m, FF),
    )


VM = pltpu.VMEM
LIMIT = 64 * 1024 * 1024


def weight_grad(a, b, out, turned, stage, sem, lo=0, start=0, stop=None, place=None):
    stop = stop or b.shape[1] - lo

    def begin(slot, i, col, w):
        if place is None:
            cols = pl.ds(pl.multiple_of(col, 128), w)
            pltpu.make_async_copy(stage.at[slot, :, 0:w], out.at[pl.ds(i * D, D), cols], sem.at[slot]).start()
            return
        chips, pieces = place
        src = stage.at[slot, :, 0:w].reshape(chips, 2, pieces, D // (2 * chips * pieces), w)
        for q in range(pieces):
            cols = pl.ds(pl.multiple_of((q % 2) * D + col, 128), w)
            pltpu.make_async_copy(src.at[:, :, q], out.at[q // 2, pl.ds(i * chips, chips), :, :, cols], sem.at[slot]).start()

    def wait(slot, w):
        whole = stage.at[slot, :, 0:w]
        pltpu.make_async_copy(whole, whole, sem.at[slot]).wait()

    def block(slot, i, col, w):
        stage[slot, :, 0:w] = dot(turned[...], b[:, pl.ds(pl.multiple_of(lo + col, 128), w)]).astype(BF16)
        begin(slot, i, col, w)

    slots = stage.shape[0]
    rounds = (stop - start) // (slots * TILE)
    for i in range(a.shape[1] // D):
        turned[...] = a[:, i * D : (i + 1) * D].T

        @pl.loop(0, rounds)
        def _(j):
            for slot in range(slots):

                @pl.when(jnp.logical_or(j > 0, i > 0))
                def _():
                    wait(slot, TILE)

                block(slot, i, start + (j * slots + slot) * TILE, TILE)

    rest = stop - start - rounds * slots * TILE
    wait(0, TILE)
    if rest:
        block(0, 0, stop - rest, rest)
    for slot in range(1, slots):
        wait(slot, TILE)
    if rest:
        wait(0, rest)


class Stream:
    def __init__(self, w, ring, sem):
        self.w, self.ring, self.sem = w, ring, sem
        self.width = w.shape[1]

    def copy(self, i, slot):
        rows = pl.ds(pl.multiple_of(i * TILE, TILE), TILE)
        return pltpu.make_async_copy(self.w.at[rows], self.ring.at[slot, :, 0 : self.width], self.sem.at[slot])

    def prefetch(self):
        self.copy(0, 0).start()
        self.copy(1, 1).start()

    def run(self, body, lo=0, hi=None):
        count = self.w.shape[0] // TILE
        hi = hi or count

        @pl.loop(lo // 2, hi // 2)
        def _(j):
            for slot in range(2):
                i = j * 2 + slot
                self.copy(i, slot).wait()
                body(pl.multiple_of(i * TILE, TILE), self.ring.at[slot, :, 0 : self.width])

                @pl.when(i + 2 < count)
                def _():
                    self.copy(i + 2, slot).start()


def own_shapes(m):
    seqs = m // STRETCH
    return dict(
        dd=((m, D), BF16), acc=((4, 8, D), F32), dx=((m, D), F32),
        dbase=((m, MXW), BF16), datt=((m, VALUE_WIDTH), BF16), dv=((m, VALUE_WIDTH), BF16),
        dpad=((seqs, STRETCH + 8, D), F32), dn=((m, D), F32), dkern=((STRETCH, D), F32),
    )


def frame(count):
    return -(-(-(-count // 128) + 1) // 8) * 8


def slot_rows(count):
    return -(-frame(count) // 16) * 16


def frames(n, count):
    return [(count * d) // 128 for d in range(n)]


def spread(k):
    p = lax.broadcasted_iota(jnp.int32, (D, TILE), 0)
    c = lax.broadcasted_iota(jnp.int32, (D, TILE), 1) + k * TILE
    return (c == 8 * (p % 128) + p // 128).astype(BF16)


def unpack_params(n, count, packed, full, prow, ema):
    full[...] = jnp.zeros(full.shape, F32)
    for d, r in enumerate(frames(n, count)):
        full[r : r + frame(count), :] += packed[d * slot_rows(count) : d * slot_rows(count) + frame(count), :].astype(F32)
    for i in range(O_EMA // 128):
        prow[:, i * 128 : (i + 1) * 128] = full[i : i + 1, :]
    rows = []
    for j in range(4):
        lo = O_EMA // 128 + j * D * H // 128
        t = full[lo : lo + 128, :].T
        rows.append(jnp.concatenate([t[H * k : H * (k + 1), :] for k in range(8)], axis=1))
    stack = jnp.concatenate(rows, axis=0).astype(BF16)
    for k in range(D // TILE):
        e = dot(stack, spread(k))
        for j in range(4):
            ema[j, :, k * TILE : (k + 1) * TILE] = e[j * H : (j + 1) * H, :]


def pack_grads(n, count, grow, gema, full, out):
    for i in range(O_EMA // 128):
        full[i : i + 1, :] = grow[:, i * 128 : (i + 1) * 128]
    stack = jnp.concatenate([gema[j] for j in range(4)], axis=0).astype(BF16)
    back = 0.0
    for k in range(D // TILE):
        back = back + dot(stack[:, k * TILE : (k + 1) * TILE], spread(k), 1, 1)
    for j in range(4):
        e = back[j * H : (j + 1) * H, :]
        lo = O_EMA // 128 + j * D * H // 128
        full[lo : lo + 128, :] = jnp.concatenate([e[:, k * 128 : (k + 1) * 128] for k in range(8)], axis=0).T
    for d, r in enumerate(frames(n, count)):
        out[d // 2, d % 2, 0:frame(count), :] = full[r : r + frame(count), :].astype(BF16)
        out[d // 2, d % 2, frame(count):slot_rows(count), :] = jnp.zeros((slot_rows(count) - frame(count), 128), BF16)


def size_table(n, count, m):
    rows = -(-(-(-(n * count) // 128) + frame(count)) // 8) * 8
    table = {k: v for k, v in list(kept_shapes(m).items()) + list(own_shapes(m).items())}
    table.update(
        out=((m, D), BF16), dxo=((m, D), BF16), grow=((1, O_EMA), F32), prow=((1, O_EMA), F32), ema=((4, H, D), F32),
        gema=((4, H, D), F32), full=((rows, 128), F32), packed=((n * slot_rows(count), 128), BF16),
        gsmall=((n // 2, 2, slot_rows(count), 128), BF16), wr=((FF, D), BF16), wc=((D, MXW), BF16), wv=((D, VALUE_WIDTH), BF16),
        wup=((D, FF), BF16), ring=((2, TILE, MXW), BF16), pool=((6 * D, WIDE), BF16), stage=((4, D, TILE), BF16), turned=((D, m), BF16), wh=((VALUE_WIDTH, D), BF16),
    )
    return table


class Parts:
    def __init__(self, refs):
        self.refs = list(refs)

    def take(self, names):
        got, self.refs = self.refs[: len(names)], self.refs[len(names) :]
        return dict(zip(names, got))

    def rest(self, k):
        got, self.refs = self.refs[:k], self.refs[k:]
        return got


GATHER_STARTS = (0, 1, 2, 3, 4)
LAG = GATHER_STARTS[-1]

KEPT = ("inner", "uslope", "first", "hpre", "second", "dd", "upd", "lat", "res", "ars", "gated", "val", "vslope", "probs", "query", "keys", "mixed", "normed", "e", "mpad", "kern", "grow", "prow", "ema")
HELD = KEPT + ("packed", "dbase", "dn", "acc", "dpad", "dkern", "gema", "full", "gsmall", "ring", "stage", "turned", "pool")
DEPTH = 4
UNIT = 2 * D
WIDE = MXW - UNIT


def unit_place(n, rows):
    return D * n // (2 * rows), rows // (32 * n)


def blocks_of(ref, n):
    return ref.reshape(n // 2, 2, ref.shape[0] // n, ref.shape[1])


def layer_kernel(dims, n, count, *refs):
    r = Parts(refs)
    x, g, valid = r.rest(3)
    ins = r.rest(6)
    out, dxo = r.rest(2)
    gup, gh, gmx, gv, gdown = r.rest(5)
    reduced = r.rest(6) if dims else r.rest(1)
    whole = [None] + r.rest(5) if dims else ins
    s = Names(**r.take(HELD))
    s.datt, s.dv, s.dx, s.dup, s.dsec = s.gated, s.vslope, s.first, s.inner, s.dn
    lsem, wsem, ssem = r.rest(3)
    _, v, mx, h, up, down = whole
    ws = {k: Stream(w, s.ring, wsem) for k, w in (("down", down), ("up", up), ("h", h), ("mx", mx), ("v", v))}
    if dims:
        osem, gsend, grecv, hsend, hrecv, send_sem, recv_sem, arrive = r.rest(8)
        p = Place(dims)
        p.barrier_all(n)
        mine = pl.ds(p.me * slot_rows(count), slot_rows(count))
        own = pltpu.make_async_copy(ins[0], s.packed.at[mine], lsem.at[0])
        own.start()

        def tell(i, dev, block):
            return pltpu.make_async_remote_copy(
                src_ref=ins[0], dst_ref=s.packed.at[pl.ds(block * slot_rows(count), slot_rows(count))], send_sem=gsend.at[i], recv_sem=grecv.at[i],
                device_id=(dev,), device_id_type=MESH,
            )

        @pl.loop(1, n)
        def _(i):
            tell(i, (p.me + i) % n, p.me).start()

        gat = Gather(p, ins[1:], whole[1:], send_sem, recv_sem)
        cps = [pltpu.make_async_copy(i, o.at[pl.ds(p.me * i.shape[0], i.shape[0])], osem.at[k]) for k, (i, o) in enumerate(zip(ins[1:], whole[1:]))]
        for cp in cps:
            cp.start()
        last = gat.stages() - 1

        def get(t):
            for k, q in enumerate(GATHER_STARTS):
                if 0 <= t - q <= last:
                    gat.stage(k, t - q)
                    if t - q == last:
                        cps[k].wait()

        def small_here():
            own.wait()

            @pl.loop(1, n)
            def _(i):
                tell(i, p.me, (p.me - i + n) % n).wait()

        cols = lambda ref, lo, w: ref.at[:, :, :, pl.ds(lo, w)]
        up4, mx4 = blocks_of(gup, n), blocks_of(gmx, n)
        rv, rmx, rh, rup, rdown, rsmall = reduced
        halves = lambda o, row: [(o, row, 0, 0, D), (o, row + 32, 0, D, D)]
        units = [
            (gdown.at[0], halves(rdown, 0)),
            (gdown.at[1], halves(rdown, 64)),
            (cols(up4, 0, UNIT), [(rup, 0, 0, 0, UNIT)]),
            (cols(up4, UNIT, UNIT), [(rup, 0, UNIT, 0, UNIT)]),
            (gh.at[0], halves(rh, 0)),
            (blocks_of(gv, n), [(rv, 0, 0, 0, UNIT)]),
            (cols(mx4, 0, UNIT), [(rmx, 0, 0, 0, UNIT)]),
            (cols(mx4, UNIT, WIDE), [(rmx, 0, UNIT, 0, WIDE)]),
        ]
        sc = Scatter(p, [u[0] for u in units], s.pool, DEPTH, [u[1] for u in units], *r.rest(5))
        S = sc.stages()

        def put(t):
            for k, q in enumerate(UNIT_STARTS):
                if 0 <= t - q < S:
                    sc.stage(k, t - q)

        def give(i, dev, slot):
            return pltpu.make_async_remote_copy(
                src_ref=s.gsmall.at[dev // 2, dev % 2], dst_ref=arrive.at[slot], send_sem=hsend.at[i], recv_sem=hrecv.at[i],
                device_id=(dev,), device_id_type=MESH,
            )
    else:
        S = 8
        get = put = lambda t: None

        def small_here():
            small = pltpu.make_async_copy(ins[0], s.packed, lsem.at[0])
            small.start()
            small.wait()

    G = dims[0] + 2 if dims else 6
    q = lambda i, w=UNIT, lo=0: s.pool.at[i * D : (i + 1) * D, lo : lo + w]
    w = Names(v=q(0), mx1=q(1, WIDE), mx2=q(2), up1=q(3), up2=q(4), h1=q(5, D), h2=q(5, D, D))
    jobs = [
        [(v, w.v)],
        [(mx.at[:, 0:WIDE], w.mx1), (mx.at[:, WIDE:MXW], w.mx2)],
        [(h.at[0:D], w.h1), (h.at[D : 2 * D], w.h2)],
        [(up.at[:, 0:UNIT], w.up1), (up.at[:, UNIT:FF], w.up2)],
    ]
    load, i = [], 0
    for pairs in jobs:
        load.append([pltpu.make_async_copy(a, b, lsem.at[1 + i + e]) for e, (a, b) in enumerate(pairs)])
        i += len(pairs)

    def begin(k):
        for c in load[k]:
            c.start()

    f = Forward(x, valid, s.prow, s.ema, w, s)
    b = Backward(x, g, valid, s.prow, s.ema, None, s, s, s.grow, s.gema)
    grad = lambda *a, **kw: weight_grad(*a[:3], s.turned, s.stage, ssem, **kw)
    s.grow[...] = jnp.zeros(s.grow.shape, F32)
    get(0)
    b.cot()
    get(1)
    small_here()
    unpack_params(n, count, s.packed, s.full, s.prow, s.ema)
    f.norm_one()
    get(2)
    f.ema_kernel()
    get(3)
    f.smooth(0)
    get(4)
    f.smooth(1)
    f.mix()
    for t in range(5, G + 1):
        get(t)
    begin(0)
    get(G + 1)
    begin(1)
    load[0][0].wait()
    f.values()
    get(G + 2)
    begin(2)
    load[1][0].wait()
    f.base_one()
    load[1][1].wait()
    f.base_two()
    f.attend()
    get(G + 3)
    begin(3)
    for c in load[2]:
        c.wait()
    f.hidden()
    f.norm_two()
    get(G + 4)
    load[3][0].wait()
    f.up(0)
    for t in range(G + 5, G + LAG):
        get(t)
    load[3][1].wait()
    f.up(1)
    if dims:
        sc.open()
    grad(s.inner, s.dd, gdown, place=unit_place(n, FF) if dims else None)
    put(0)
    get(G + LAG)
    ws["down"].prefetch()
    s.dn[...] = jnp.zeros(s.dn.shape, F32)
    b.pad_tail()
    put(1)
    ws["down"].run(b.down_tile)
    ws["up"].prefetch()
    put(2)
    grad(s.second, s.dup, gup, start=0, stop=UNIT)
    put(3)
    grad(s.second, s.dup, gup, start=UNIT, stop=FF)
    put(4)
    b.output(out)
    ws["up"].run(b.second_tile)
    ws["h"].prefetch()
    put(5)
    b.norm_two()
    put(6)
    grad(s.gated, s.dbase, gh, lo=C_HX, place=unit_place(n, VALUE_WIDTH) if dims else None)
    put(7)
    ws["h"].run(b.gated_tile)
    ws["mx"].prefetch()
    put(8)
    b.attend()
    grad(s.normed, s.dv, gv)
    put(9)
    grad(s.mixed, s.dbase, gmx, start=0, stop=UNIT)
    put(10)
    grad(s.mixed, s.dbase, gmx, start=UNIT)
    put(11)
    ws["mx"].run(b.mixed_tile)
    ws["v"].prefetch()
    put(12)
    ws["v"].run(b.normed_tile)
    b.smooth_signal(0)
    put(13)
    b.smooth_signal(1)
    put(14)
    b.smooth_filter()
    put(15)
    b.ema_grads()
    b.norm_one(dxo)
    put(16)
    pack_grads(n, count, s.grow, s.gema, s.full, s.gsmall)
    if dims:
        me = p.me

        @pl.loop(1, n)
        def _(i):
            give(i, (me + i) % n, i).start()

        for t in range(17, UNIT_STARTS[-1] + S):
            put(t)
        rsmall[...] = s.gsmall[me // 2, me % 2].astype(F32)

        @pl.loop(1, n)
        def _(i):
            give(i, me, i).wait()
            rsmall[...] += arrive[i].astype(F32)

        gat.finish()
    else:
        keep = pltpu.make_async_copy(s.gsmall, reduced[0], lsem.at[0])
        keep.start()
        keep.wait()


UNIT_STARTS = (0, 1, 3, 4, 8, 9, 11, 12)
GATHER_STARTS = (0, 1, 2, 3, 6)
LAG = GATHER_STARTS[-1]


def run_kernel(body, ins, outs, scratch, cid):
    vm, hbm = pl.BlockSpec(memory_space=VM), pl.BlockSpec(memory_space=pl.ANY)
    params = dict(vmem_limit_bytes=LIMIT)
    if cid is not None:
        params.update(collective_id=cid, has_side_effects=True)
    return pl.pallas_call(
        body,
        out_shape=[jax.ShapeDtypeStruct(o[0], o[1]) for o in outs],
        in_specs=[vm if i[1] else hbm for i in ins],
        out_specs=[vm if o[2] else hbm for o in outs],
        scratch_shapes=scratch,
        compiler_params=pltpu.CompilerParams(**params),
    )(*[i[0] for i in ins])


def copy_kernel(k, *refs):
    ins, outs, bufs, sem = refs[:k], refs[k : 2 * k], refs[2 * k : 3 * k], refs[3 * k]
    get = [pltpu.make_async_copy(a, b, sem.at[i]) for i, (a, b) in enumerate(zip(ins, bufs))]
    put = [pltpu.make_async_copy(a, b, sem.at[k + i]) for i, (a, b) in enumerate(zip(bufs, outs))]
    for c in get:
        c.start()
    for c, d in zip(get, put):
        c.wait()
        d.start()
    for d in put:
        d.wait()


def settle(arrays):
    return run_kernel(
        functools.partial(copy_kernel, len(arrays)), [(a, False) for a in arrays], [(a.shape, a.dtype, False) for a in arrays],
        [VM(a.shape, a.dtype) for a in arrays] + [pltpu.SemaphoreType.DMA((2 * len(arrays),))], None,
    )


def layer(dims, n, count, x, g, valid, arrays):
    m = x.shape[0]
    table = size_table(n, count, m)
    dma = pltpu.SemaphoreType.DMA
    tmp = lambda names: [VM(*table[k]) for k in names]
    whole = [(n * a.shape[0], a.shape[1]) if dims else a.shape for a in arrays]
    parts = [(q[0] // n, q[1]) for q in whole]
    scratch = tmp(HELD) + [dma((8,)), dma((2,)), dma((4,))]
    unit = lambda k: (k, n // 2, 2, 32, UNIT)
    o = [((m, D), BF16, True)] * 2
    o += [(q, BF16, False) for q in (whole[4], unit(1) if dims else whole[3], whole[2], whole[1], unit(2) if dims else whole[5])]
    if dims:
        o += [(parts[i], F32, True) for i in (1, 2, 3, 4, 5)] + [((slot_rows(count), 128), F32, True)]
        o += [(q, BF16, False) for q in whole[1:]]
        ns = sems_needed(dims, 5)
        scratch += [dma((5,)), dma((n,)), dma((n,)), dma((n,)), dma((n,)), dma((ns,)), dma((ns,)), VM((n, slot_rows(count), 128), BF16)]
        scratch += scatter_sems(dims, len(UNIT_STARTS))
    else:
        o += [table["gsmall"] + (False,)]
    ins = [(x, True), (g, True), (valid, True)] + [(q, False) for q in arrays]
    res = run_kernel(functools.partial(layer_kernel, dims, n, count), ins, o, scratch, 0 if dims else None)
    out, dx = res[:2]
    if dims:
        gv, gmx, gh, gup, gdown, gs = res[7:13]
    else:
        gup, gh, gmx, gv, gdown = res[2:7]
        gs = res[7].reshape(n * slot_rows(count), 128)
    return out, dx, gv, gmx, gh, gup, gdown, gs


def frame_in(small, me):
    count = small.shape[0]
    line = lax.dynamic_update_slice(jnp.zeros((frame(count) * 128,), small.dtype), small, ((me * count) % 128,))
    return jnp.pad(line.reshape(frame(count), 128), ((0, slot_rows(count) - frame(count)), (0, 0)))


def frame_out(block, me, count):
    return lax.dynamic_slice(block.reshape(-1), ((me * count) % 128,), (count,))


def grid_of(n):
    return (n // 8, 2, 2)


def per_device(n, inputs, lengths, cotangent, v_weight, mx_weight, h_weight, up_weight, down_weight, small_params):
    shape = inputs.shape
    m, count = shape[0] * shape[1] * shape[2], small_params.shape[0]
    me = lax.axis_index("fsdp")
    x, g = inputs.reshape(m, D), cotangent.reshape(m, D)
    mask = (jnp.arange(shape[2]) < lengths[:, :, None]).astype(F32).reshape(m, 1)
    valid = jnp.broadcast_to(mask, (m, 128))
    arrays = (frame_in(small_params, me), v_weight, mx_weight, h_weight, up_weight, down_weight)
    dims = grid_of(n) if n == 32 else None
    if not dims:
        arrays = [lax.all_gather(a, "fsdp", axis=0, tiled=True) for a in arrays]
    out, dx, gv, gmx, gh, gup, gdown, gs = layer(dims, n, count, x, g, valid, arrays)
    if dims:
        out, dx, gv, gmx, gh, gup, gdown = settle((out, dx, gv, gmx, gh, gup, gdown))
    else:
        gv, gmx, gh, gup, gdown, gs = (
            lax.psum_scatter(a.astype(F32), "fsdp", scatter_dimension=0, tiled=True) for a in (gv, gmx, gh, gup, gdown, gs)
        )
    return out.reshape(shape), dx.reshape(shape), gv, gmx, gh, gup, gdown, frame_out(gs, me, count)


def solution(mesh):
    rows, cols = P("fsdp", None), P(None, "fsdp", None, None)
    return jax.shard_map(
        functools.partial(per_device, mesh.shape["fsdp"]),
        mesh=mesh,
        in_specs=(cols, P(None, "fsdp"), cols, rows, rows, rows, rows, rows, P("fsdp")),
        out_specs=(cols, cols, rows, rows, rows, rows, rows, P("fsdp")),
        check_vma=False,
    )
```

```python
import functools
import math

import jax
import jax.numpy as jnp
from jax import lax
from jax.experimental import pallas as pl
from jax.experimental.pallas import tpu as pltpu
from jax.sharding import PartitionSpec as P

D = 1024
Z = 128
VALUE_WIDTH = 2048
H = 16
FF = 4096
STRETCH = 128


epsilon = 1e-05

MESH = pl.DeviceIdType.MESH

class Place:
    def __init__(self, dims):
        self.Z, self.Y, self.X = dims
        me = lax.axis_index("fsdp")
        self.me = me
        self.c = me % 2
        self.x = (me // 2) % self.X
        self.y = (me // (2 * self.X)) % self.Y
        self.z = me // (2 * self.X * self.Y)
        self.nx = self.dev(self.z, self.y, 1 - self.x, self.c)
        self.ny = self.dev(self.z, 1 - self.y, self.x, self.c)
        self.nc = self.dev(self.z, self.y, self.x, 1 - self.c)
        self.has_down = self.z > 0
        self.has_up = self.z < self.Z - 1
        self.down = self.dev(jnp.maximum(self.z - 1, 0), self.y, self.x, self.c)
        self.up = self.dev(jnp.minimum(self.z + 1, self.Z - 1), self.y, self.x, self.c)
    def dev(self, z, y, x, c):
        return ((z * self.Y + y) * self.X + x) * 2 + c
    def barrier(self):
        bar = pltpu.get_barrier_semaphore()
        def tell(d):
            pl.semaphore_signal(bar, inc=1, device_id=(d,), device_id_type=MESH)
        for d in (self.nx, self.ny, self.nc):
            tell(d)
        pl.when(self.has_down)(lambda: tell(self.down))
        pl.when(self.has_up)(lambda: tell(self.up))
        pl.semaphore_wait(bar, 3 + jnp.where(self.has_down, 1, 0) + jnp.where(self.has_up, 1, 0))

    def barrier_all(self, n):
        bar = pltpu.get_barrier_semaphore()

        @pl.loop(1, n)
        def _(i):
            pl.semaphore_signal(bar, inc=1, device_id=((self.me + i) % n,), device_id_type=MESH)

        pl.semaphore_wait(bar, n - 1)

def when(cond, f):
    if cond is None: f()
    else: pl.when(cond)(f)

class Gather:
    def __init__(self, place, ins, outs, send_sem, recv_sem):
        self.p, self.ins, self.outs = place, ins, outs
        self.ss, self.rs = send_sem, recv_sem
        self.ids, self.pend = {}, []
    def rows(self, k, h):
        n = self.ins[k].shape[0]
        return (0, n) if h == 2 else (h * (n // 2), n // 2)
    def copy(self, key, k, shard, h, to, own=False):
        i = self.ids.setdefault((key, k), len(self.ids))
        r, n = self.rows(k, h)
        full = self.ins[k].shape[0]
        dst = self.outs[k].at[pl.ds(shard * full + r, n)]
        src = self.ins[k].at[pl.ds(r, n)] if own else dst
        return pltpu.make_async_remote_copy(src_ref=src, dst_ref=dst, send_sem=self.ss.at[i], recv_sem=self.rs.at[i], device_id=(to,), device_id_type=MESH)
    def send(self, cond, *a):
        when(cond, lambda: self.copy(*a).start())
        self.pend.append((cond, lambda: self.copy(*a).wait_send()))
    def recv(self, cond, key, k, shard, h):
        when(cond, lambda: self.copy(key, k, shard, h, self.p.me).wait_recv())
    def col(self, o):
        p = self.p
        if o == 0: return None, p.z
        if o > 0: return p.z - o >= 0, jnp.maximum(p.z - o, 0)
        return p.z - o <= p.Z - 1, jnp.minimum(p.z - o, p.Z - 1)
    def offs(self, s):
        return (0,) if s == 0 else (s, -s)
    def stage(self, k, s):
        p = self.p
        L = p.Z
        if s < L:
            for o in self.offs(s):
                cond, zz = self.col(o)
                sh = p.dev(zz, p.y, p.x, p.c)
                own = o == 0
                if not own:
                    self.recv(cond, ("z", o), k, sh, 2)
                if s + 1 < L:
                    both = lambda c1: c1 if cond is None else jnp.logical_and(cond, c1)
                    if o >= 0: self.send(both(p.has_up), ("z", s + 1), k, sh, 2, p.up, own)
                    if o <= 0: self.send(both(p.has_down), ("z", -(s + 1)), k, sh, 2, p.down, own)
                if abs(o) != 1:
                    self.send(cond, ("x", o), k, sh, 2, p.nx, own)
                    self.send(cond, ("y", o), k, sh, 2, p.ny, own)
                self.send(cond, ("c", o), k, sh, 2, p.nc, own)
        if 1 <= s <= L:
            for o in self.offs(s - 1):
                cond, zz = self.col(o)
                sx, sy = p.dev(zz, p.y, 1 - p.x, p.c), p.dev(zz, 1 - p.y, p.x, p.c)
                for key, sh, half, to in (("x", sx, 0, p.ny), ("y", sy, 1, p.nx)):
                    self.recv(cond, (key, o), k, sh, 2)
                    if o == 0:
                        self.send(p.has_up, (key, 1), k, sh, 2, p.up)
                        self.send(p.has_down, (key, -1), k, sh, 2, p.down)
                    self.send(cond, ("d" + key, o), k, sh, half, to)
                    self.send(cond, ("c" + key, o), k, sh, 2, p.nc)
        if 2 <= s <= L + 1:
            for o in self.offs(s - 2):
                cond, zz = self.col(o)
                sd = p.dev(zz, 1 - p.y, 1 - p.x, p.c)
                self.recv(cond, ("dx", o), k, sd, 0)
                self.recv(cond, ("dy", o), k, sd, 1)
                self.send(cond, ("cd", o), k, sd, 2, p.nc)
        if s == L + 2:
            for t in range(L):
                for o in self.offs(t):
                    cond, zz = self.col(o)
                    for key, yy, xx in (("c", p.y, p.x), ("cx", p.y, 1 - p.x), ("cy", 1 - p.y, p.x), ("cd", 1 - p.y, 1 - p.x)):
                        self.recv(cond, (key, o), k, p.dev(zz, yy, xx, 1 - p.c), 2)
    def stages(self):
        return self.p.Z + 3
    def finish(self):
        for cond, f in self.pend:
            when(cond, f)

def sems_needed(dims, K):
    Z = dims[0]
    return K * (2 * (Z - 1) + 8 * (2 * Z - 1) + 4)


F32, BF16 = jnp.float32, jnp.bfloat16
TILE = 256
O_GAIN, O_SHIFT, O_OMEGA, O_AFF, O_REL = 0, 2 * D, 4 * D, 5 * D, 5 * D + 4 * Z
O_VB = O_REL + STRETCH
O_MXB = O_VB + VALUE_WIDTH
MXW = 2 * D + Z + VALUE_WIDTH
O_HB = O_MXB + MXW
O_UPB = O_HB + D
O_DNB = O_UPB + FF
O_EMA = O_DNB + D
C_LAT, C_RES, C_HX = D, D + Z, D + Z + VALUE_WIDTH


def sigmoid(v):
    return 0.5 * jnp.tanh(0.5 * v) + 0.5


def silu_slope(v, s):
    return s * (1.0 + v * (1.0 - s))


def col_sum(v):
    return jnp.sum(v, axis=0, keepdims=True)


def dot(a, b, ca=1, cb=0):
    return lax.dot_general(a, b, (((ca,), (cb,)), ((), ())), preferred_element_type=F32)


def tiles(lo, hi, step, f):
    @pl.loop(0, (hi - lo) // step)
    def _(i):
        f(pl.multiple_of(lo + i * step, 128))


def lane_block(l):
    return pl.ds(pl.multiple_of(l * 128, 128), 128)


def center(xf):
    c = xf - jnp.mean(xf, axis=-1, keepdims=True)
    r = lax.rsqrt(jnp.mean(c * c, axis=-1, keepdims=True) + epsilon)
    return c * r, r


def ema_rates(ema):
    gate, a = sigmoid(ema[0]), sigmoid(ema[1])
    retain = 1.0 - gate * a
    weight = gate * ema[2] * ema[3] * (1.0 / math.sqrt(H))
    return gate, a, retain, weight


def rel_table(rel_row):
    wide = jnp.broadcast_to(rel_row, (STRETCH, STRETCH))
    return pltpu.roll(wide, 0, 1, stride=1, stride_axis=0).T


def causal():
    i = lax.broadcasted_iota(jnp.int32, (STRETCH, STRETCH), 0)
    j = lax.broadcasted_iota(jnp.int32, (STRETCH, STRETCH), 1)
    return j <= i


class Forward:
    def __init__(self, x, valid, prow, ema, w, s):
        self.x, self.valid, self.prow, self.ema, self.w, self.s = x, valid, prow, ema, w, s
        self.m = x.shape[0]
        self.seqs = self.m // STRETCH

    def p(self, lo, n):
        return self.prow[:, lo : lo + n]

    def pd(self, lo, col, n):
        return self.prow[:, pl.ds(pl.multiple_of(lo + col, 128), n)]

    def norm_one(self):
        s = self.s
        g, b = self.p(O_GAIN, D), self.p(O_SHIFT, D)
        for q in range(self.seqs):
            s.mpad[q, 0:8, :] = jnp.zeros((8, D), F32)

            @pl.loop(0, STRETCH // 32)
            def _(i):
                r = pl.ds(q * STRETCH + i * 32, 32)
                xhat, _ = center(self.x[r, :].astype(F32))
                n = xhat * g + b
                s.normed[r, :] = n.astype(BF16)
                s.mpad[q, pl.ds(8 + i * 32, 32), :] = n * self.valid[r, 0:1]

    def ema_kernel(self):
        _, _, retain, weight = ema_rates(self.ema)

        def step(j, p):
            self.s.kern[pl.ds(j, 1), :] = col_sum(p)
            return p * retain

        lax.fori_loop(0, STRETCH, step, weight)

    def smooth(self, q):
        s = self.s
        for q in (q,):

            @pl.loop(0, D // 128)
            def _(l):
                lb = lane_block(l)
                om = self.prow[:, pl.ds(pl.multiple_of(O_OMEGA + l * 128, 128), 128)]
                nb = STRETCH // 8
                acc = [om * s.mpad[q, 8 + 8 * i : 16 + 8 * i, lb] for i in range(nb)]
                for b in range(8):
                    sh = [s.mpad[q, 8 - b + 8 * i : 16 - b + 8 * i, lb] for i in range(nb)]
                    for a in range(nb):
                        kb = jnp.broadcast_to(s.kern[8 * a + b : 8 * a + b + 1, lb], (8, 128))
                        for i in range(a, nb):
                            acc[i] = acc[i] + kb * sh[i - a]
                for i in range(nb):
                    r = slice(q * STRETCH + 8 * i, q * STRETCH + 8 * i + 8)
                    s.e[r, lb] = acc[i]

    def mix(self):
        s = self.s

        @pl.loop(0, self.m // 32)
        def _(i):
            r = pl.ds(i * 32, 32)
            e = s.e[r, :]
            s.mixed[r, :] = (e * sigmoid(e)).astype(BF16)

    def values(self):
        s = self.s

        def one(col):
            cols = pl.ds(col, TILE)
            v = dot(s.normed[...], self.w.v[:, cols]) + self.pd(O_VB, col, TILE)
            sv = sigmoid(v)
            s.vslope[:, cols] = silu_slope(v, sv).astype(BF16)
            s.val[:, cols] = (v * sv).astype(BF16)

        tiles(0, VALUE_WIDTH, TILE, one)

    def base_one(self):
        s = self.s

        def f(dst, lo, width):
            def one(col):
                dst[:, pl.ds(pl.multiple_of(col - lo, 128), width)] = dot(s.mixed[...], self.w.mx1[:, pl.ds(col, width)]) + self.pd(O_MXB, col, width)

            return one

        def gate(col):
            cols = pl.ds(col, TILE)
            s.upd[:, cols] = sigmoid(dot(s.mixed[...], self.w.mx1[:, cols]) + self.pd(O_MXB, col, TILE))

        tiles(0, D, TILE, gate)
        s.lat[...] = dot(s.mixed[...], self.w.mx1[:, C_LAT:C_RES]) + self.p(O_MXB + C_LAT, Z)
        tiles(C_RES, C_RES + D, TILE, f(s.first, C_RES, TILE))

    def base_two(self):
        s = self.s

        def f(dst, lo):
            def one(col):
                here = pl.multiple_of(lo + col, 128)
                v = dot(s.mixed[...], self.w.mx2[:, pl.ds(here, TILE)]) + self.pd(O_MXB + C_RES + D, here, TILE)
                dst[:, pl.ds(col, TILE)] = v

            return one

        tiles(0, D, TILE, f(s.dn, 0))
        tiles(0, D, TILE, f(s.hpre, D))

    def attend(self):
        s = self.s
        table, mask = rel_table(self.p(O_REL, STRETCH)), causal()
        for q in range(self.seqs):
            r = slice(q * STRETCH, (q + 1) * STRETCH)
            b = s.lat[r, :]
            lat = b * sigmoid(b)
            query = (lat * (1.0 + self.p(O_AFF, Z)) + self.p(O_AFF + 2 * Z, Z)).astype(BF16)
            keys = (lat * (1.0 + self.p(O_AFF + Z, Z)) + self.p(O_AFF + 3 * Z, Z)).astype(BF16)
            sc = jnp.where(mask, dot(query, keys, 1, 1) * (1.0 / math.sqrt(Z)) + table, -1e30)
            ex = jnp.exp(sc - jnp.max(sc, axis=-1, keepdims=True))
            pr = ex / jnp.sum(ex, axis=-1, keepdims=True)
            s.probs[r, :] = pr
            s.query[r, :] = query
            s.keys[r, :] = keys
            low = pr.astype(BF16)

            def one(half, pre, col):
                cols = pl.ds(pl.multiple_of(half + col, 128), TILE)
                at = dot(low, s.val[r, cols])
                bb = pre[r, pl.ds(col, TILE)]
                sb = sigmoid(bb)
                res = bb * sb
                s.res[r, cols] = res.astype(BF16)
                s.ars[r, cols] = (at * silu_slope(bb, sb)).astype(BF16)
                s.gated[r, cols] = (at * res).astype(BF16)

            tiles(0, D, TILE, functools.partial(one, 0, s.first))
            tiles(0, D, TILE, functools.partial(one, D, s.dn))

    def hidden(self):
        s = self.s

        def one(col):
            cols = pl.ds(col, TILE)
            h = dot(s.gated[:, 0:D], self.w.h1[:, cols]) + dot(s.gated[:, D : 2 * D], self.w.h2[:, cols])
            h = s.hpre[:, cols] + h + self.pd(O_HB, col, TILE)
            s.hpre[:, cols] = h
            xf = self.x[:, cols].astype(F32)
            s.first[:, cols] = xf + self.valid[:, 0:1] * s.upd[:, cols] * (h * sigmoid(h) - xf)

        tiles(0, D, TILE, one)

    def norm_two(self):
        s = self.s
        g, b = self.p(O_GAIN + D, D), self.p(O_SHIFT + D, D)

        @pl.loop(0, self.m // 32)
        def _(i):
            r = pl.ds(i * 32, 32)
            xhat, _ = center(s.first[r, :])
            s.second[r, :] = (xhat * g + b).astype(BF16)

    def up(self, half):
        s = self.s
        w, lo = (self.w.up1, 0) if half == 0 else (self.w.up2, FF // 2)

        def one(col):
            cols = pl.ds(pl.multiple_of(lo + col, 128), TILE)
            u = dot(s.second[...], w[:, pl.ds(col, TILE)]) + self.pd(O_UPB + lo, col, TILE)
            su = sigmoid(u)
            s.uslope[:, cols] = silu_slope(u, su).astype(BF16)
            s.inner[:, cols] = (u * su).astype(BF16)

        tiles(0, FF // 2, TILE, one)


class Backward:
    def __init__(self, x, g, valid, prow, ema, w, s, t, grow, gema):
        self.x, self.g, self.valid, self.prow, self.ema = x, g, valid, prow, ema
        self.w, self.s, self.t, self.grow, self.gema = w, s, t, grow, gema
        self.m = x.shape[0]
        self.seqs = self.m // STRETCH

    p, pd = Forward.p, Forward.pd

    def put(self, lo, col, n, v):
        self.grow[:, pl.ds(pl.multiple_of(lo + col, 128), n)] = v

    def cot(self):
        def one(col):
            cols = pl.ds(col, TILE)
            d = self.valid[:, 0:1] * self.g[:, cols].astype(F32)
            self.put(O_DNB, col, TILE, col_sum(d))
            self.t.dd[:, cols] = d.astype(BF16)

        tiles(0, D, TILE, one)

    def down_tile(self, col, w):
        s, t = self.s, self.t
        cols = pl.ds(col, TILE)
        t.dn[...] += dot(s.inner[:, cols], w[...])
        di = dot(t.dd[...], w[...], 1, 1)
        du = di * s.uslope[:, cols].astype(F32)
        self.put(O_UPB, col, TILE, col_sum(du))
        t.dup[:, cols] = du.astype(BF16)

    def output(self, out):
        s, t = self.s, self.t

        def one(col):
            cols = pl.ds(col, TILE)
            d = t.dn[:, cols] + self.pd(O_DNB, col, TILE)
            out[:, cols] = (s.first[:, cols] + self.valid[:, 0:1] * d).astype(BF16)

        tiles(0, D, TILE, one)

    def second_tile(self, col, w):
        self.t.dsec[:, pl.ds(col, TILE)] = dot(self.t.dup[...], w[...], 1, 1)

    def norm_two(self):
        s, t = self.s, self.t
        g = self.p(O_GAIN + D, D)
        t.acc[...] = jnp.zeros(t.acc.shape, F32)

        def add(k, v):
            t.acc[k] += jnp.sum(v.reshape(v.shape[0] // 8, 8, D), axis=0)

        @pl.loop(0, self.m // 32)
        def _(i):
            r = pl.ds(i * 32, 32)
            xhat, rstd = center(s.first[r, :])
            ds = t.dsec[r, :]
            add(0, ds * xhat)
            add(1, ds)
            dh = ds * g
            dn = rstd * (dh - jnp.mean(dh, axis=-1, keepdims=True) - xhat * jnp.mean(dh * xhat, axis=-1, keepdims=True))
            df = self.g[r, :].astype(F32) + dn
            v = self.valid[r, 0:1]
            u = s.upd[r, :]
            hp = s.hpre[r, :]
            sh = sigmoid(hp)
            xf = self.x[r, :].astype(F32)
            vu = v * u
            t.dx[r, :] = df - df * vu
            db = df * v * (hp * sh - xf) * u * (1.0 - u)
            add(2, db)
            t.dbase[r, 0:D] = db.astype(BF16)
            dhp = df * vu * silu_slope(hp, sh)
            add(3, dhp)
            t.dbase[r, C_HX:MXW] = dhp.astype(BF16)

        for k, lo in enumerate((O_GAIN + D, O_SHIFT + D, O_MXB, O_HB)):
            self.grow[:, lo : lo + D] = col_sum(t.acc[k])
        self.grow[:, O_MXB + C_HX : O_MXB + MXW] = col_sum(t.acc[3])

    def gated_tile(self, col, w):
        s, t = self.s, self.t
        cols = pl.ds(col, TILE)
        bcols = pl.ds(pl.multiple_of(C_RES + col, 128), TILE)
        dg = dot(t.dbase[:, C_HX:MXW], w[...], 1, 1)
        t.datt[:, cols] = (dg * s.res[:, cols].astype(F32)).astype(BF16)
        db = dg * s.ars[:, cols].astype(F32)
        self.put(O_MXB + C_RES, col, TILE, col_sum(db))
        t.dbase[:, bcols] = db.astype(BF16)

    def attend(self):
        s, t = self.s, self.t
        mask = causal()
        lows, drel = [], None
        aff = [0.0, 0.0, 0.0, 0.0]
        lat_bias = 0.0
        for q in range(self.seqs):
            r = slice(q * STRETCH, (q + 1) * STRETCH)
            pr = s.probs[r, :]
            lows.append(pr.astype(BF16))
            dp = dot(t.datt[r, :], s.val[r, :], 1, 1)
            ds = pr * (dp - jnp.sum(pr * dp, axis=-1, keepdims=True))
            ds = jnp.where(mask, ds, 0.0)
            drel = ds if drel is None else drel + ds
            raw = (ds * (1.0 / math.sqrt(Z))).astype(BF16)
            dq = dot(raw, s.keys[r, :])
            dk = dot(raw, s.query[r, :], 0, 0)
            b = s.lat[r, :]
            sb = sigmoid(b)
            lat = b * sb
            for k, v in enumerate((dq * lat, dk * lat, dq, dk)):
                aff[k] = aff[k] + col_sum(v)
            dl = dq * (1.0 + self.p(O_AFF, Z)) + dk * (1.0 + self.p(O_AFF + Z, Z))
            db = dl * silu_slope(b, sb)
            lat_bias = lat_bias + col_sum(db)
            t.dbase[r, C_LAT:C_RES] = db.astype(BF16)
        for k in range(4):
            self.grow[:, O_AFF + k * Z : O_AFF + (k + 1) * Z] = aff[k]
        self.grow[:, O_MXB + C_LAT : O_MXB + C_RES] = lat_bias
        drel = drel.T
        eight = 0.0
        for i in range(0, STRETCH, 8):
            eight = eight + pltpu.roll(drel[i : i + 8, :], (STRETCH - i) % STRETCH, 1)
        back = 0.0
        for i in range(8):
            back = back + pltpu.roll(eight[i : i + 1, :], (STRETCH - i) % STRETCH, 1)
        self.grow[:, O_REL : O_REL + STRETCH] = back

        def one(col):
            cols = pl.ds(col, TILE)
            bias = 0.0
            for q in range(self.seqs):
                r = slice(q * STRETCH, (q + 1) * STRETCH)
                dv = dot(lows[q], t.datt[r, cols], 0, 0)
                dv = dv * s.vslope[r, cols].astype(F32)
                bias = bias + col_sum(dv)
                t.dv[r, cols] = dv.astype(BF16)
            self.put(O_VB, col, TILE, bias)

        tiles(0, VALUE_WIDTH, TILE, one)

    def pad_tail(self):
        for q in range(self.seqs):
            self.t.dpad[q, STRETCH : STRETCH + 8, :] = jnp.zeros((8, D), F32)

    def mixed_tile(self, col, w):
        s, t = self.s, self.t
        cols = pl.ds(col, TILE)
        dm = dot(t.dbase[...], w[...], 1, 1)
        e = s.e[:, cols]
        de = dm * silu_slope(e, sigmoid(e))
        om = 0.0
        for q in range(self.seqs):
            d = de[q * STRETCH : (q + 1) * STRETCH, :]
            t.dpad[q, 0:STRETCH, cols] = d
            om = om + col_sum(d * s.mpad[q, 8 : 8 + STRETCH, cols])
        self.put(O_OMEGA, col, TILE, om)

    def normed_tile(self, col, w):
        self.t.dn[:, pl.ds(col, TILE)] = dot(self.t.dv[...], w[...], 1, 1)

    def smooth_signal(self, seq):
        s, t = self.s, self.t
        nb = STRETCH // 8

        @pl.loop(0, D // 128)
        def _(l):
            lb = lane_block(l)
            om = self.prow[:, pl.ds(pl.multiple_of(O_OMEGA + l * 128, 128), 128)]
            for q in (seq,):
                acc = [om * t.dpad[q, 8 * i : 8 * i + 8, lb] for i in range(nb)]
                for b in range(8):
                    sh = [t.dpad[q, 8 * i + b : 8 * i + b + 8, lb] for i in range(nb)]
                    for a in range(nb):
                        kb = jnp.broadcast_to(s.kern[8 * a + b : 8 * a + b + 1, lb], (8, 128))
                        for i in range(nb - a):
                            acc[i] = acc[i] + kb * sh[i + a]
                for i in range(nb):
                    r = slice(q * STRETCH + 8 * i, q * STRETCH + 8 * i + 8)
                    t.dn[r, lb] = t.dn[r, lb] + self.valid[r, :] * acc[i]

    def smooth_filter(self):
        s, t = self.s, self.t
        nb = STRETCH // 8

        @pl.loop(0, D // 128)
        def _(l):
            lb = lane_block(l)
            for b in range(8):
                sums = [None] * nb
                for q in range(self.seqs):
                    de = [t.dpad[q, 8 * i : 8 * i + 8, lb] for i in range(nb)]
                    sh = [s.mpad[q, 8 - b + 8 * i : 16 - b + 8 * i, lb] for i in range(nb)]
                    for a in range(nb):
                        for i in range(a, nb):
                            v = de[i] * sh[i - a]
                            sums[a] = v if sums[a] is None else sums[a] + v
                for a in range(nb):
                    t.dkern[8 * a + b : 8 * a + b + 1, lb] = col_sum(sums[a])

    def norm_one(self, out):
        t = self.t
        g = self.p(O_GAIN, D)
        t.acc[...] = jnp.zeros(t.acc.shape, F32)

        def add(k, v):
            t.acc[k] += jnp.sum(v.reshape(v.shape[0] // 8, 8, D), axis=0)

        @pl.loop(0, self.m // 32)
        def _(i):
            r = pl.ds(i * 32, 32)
            xhat, rstd = center(self.x[r, :].astype(F32))
            dn = t.dn[r, :]
            add(0, dn * xhat)
            add(1, dn)
            dh = dn * g
            d = rstd * (dh - jnp.mean(dh, axis=-1, keepdims=True) - xhat * jnp.mean(dh * xhat, axis=-1, keepdims=True))
            out[r, :] = (t.dx[r, :] + d).astype(BF16)

        for k, lo in enumerate((O_GAIN, O_SHIFT)):
            self.grow[:, lo : lo + D] = col_sum(t.acc[k])


    def ema_grads(self):
        t = self.t
        scale = 1.0 / math.sqrt(H)

        @pl.loop(0, D // 128)
        def _(l):
            lb = lane_block(l)
            par = self.ema[:, :, lb]
            gate, a, retain, weight = ema_rates(par)
            zero = retain - retain

            def eight(k, carry):
                power, before, dw, dr = carry
                rows = t.dkern[pl.ds(pl.multiple_of(8 * k, 8), 8), lb]
                for i in range(8):
                    row = rows[i : i + 1, :]
                    dw = dw + row * power
                    dr = dr + (row * (8 * k + i).astype(F32)) * before
                    power, before = power * retain, power
                return power, before, dw, dr

            _, _, dw, dr = lax.fori_loop(0, STRETCH // 8, eight, (zero + 1.0, zero, zero, zero))
            drate = -dr * weight
            dgate = drate * a + dw * par[2] * par[3] * scale
            self.gema[0, :, lb] = dgate * gate * (1.0 - gate)
            self.gema[1, :, lb] = drate * gate * a * (1.0 - a)
            self.gema[2, :, lb] = dw * gate * par[3] * scale
            self.gema[3, :, lb] = dw * gate * par[2] * scale


class Scatter:
    def __init__(self, place, grads, pool, depth, outs, send_sem, recv_sem, local_sem, credit, first):
        self.ready = first
        self.p, self.grads, self.outs, self.depth, self.credit = place, grads, outs, depth, credit
        self.bufs = []
        for k, g in enumerate(grads):
            wide, w = pool.shape[1], pl.ds(0, g.shape[-1])
            lo = (k % depth) * (pool.shape[0] // depth)
            views = {}
            for name, (q, r) in unit_buffers((place.Z, place.Y, place.X), g.shape[-2]).items():
                views[name] = pool.at[pl.ds(lo, q * r)].reshape(q, r, wide).at[:, :, w]
                lo += q * r
            self.bufs.append(Names(**views))
        self.ss, self.rs, self.ls = send_sem, recv_sem, local_sem
        self.ids, self.pend = {}, [[] for _ in grads]

    def around(self):
        p = self.p
        return ((None, p.nc), (None, p.nx), (None, p.ny), (p.has_up, p.up), (p.has_down, p.down))

    def release(self, k):
        self.finish(k)
        if k + self.depth < len(self.grads):
            for i, (cond, to) in enumerate(self.around()):
                slot = (0, 1, 2, 4, 3)[i]
                when(cond, lambda slot=slot, to=to: pl.semaphore_signal(self.credit.at[k, slot], inc=1, device_id=(to,), device_id_type=MESH))

    def open(self):
        for i, (cond, to) in enumerate(self.around()):
            slot = (0, 1, 2, 4, 3)[i]
            when(cond, lambda slot=slot, to=to: pl.semaphore_signal(self.ready.at[slot], inc=1, device_id=(to,), device_id_type=MESH))

    def entered(self):
        for i, (cond, to) in enumerate(self.around()):
            when(cond, lambda i=i: pl.semaphore_wait(self.ready.at[i], 1))

    def admit(self, k):
        if k == 0:
            self.entered()
        if k >= self.depth:
            for i, (cond, to) in enumerate(self.around()):
                when(cond, lambda i=i: pl.semaphore_wait(self.credit.at[k - self.depth, i], 1))

    def copy(self, key, k, src, dst, to):
        i = self.ids.setdefault((key, k), len(self.ids))
        return pltpu.make_async_remote_copy(src_ref=src, dst_ref=dst, send_sem=self.ss.at[i], recv_sem=self.rs.at[i], device_id=(to,), device_id_type=MESH)

    def send(self, cond, key, k, src, dst, to):
        when(cond, lambda: self.copy(key, k, src, dst, to).start())
        self.pend[k].append((cond, lambda: self.copy(key, k, src, dst, to).wait_send()))

    def recv(self, cond, key, k, dst):
        when(cond, lambda: self.copy(key, k, dst, dst, self.p.me).wait_recv())

    def own(self, k, z):
        p, b = self.p, self.bufs[k]
        layer = p.Y * p.X
        i = k * p.Z + z
        return pltpu.make_async_copy(self.grads[k].at[pl.ds(z * layer, layer), p.c], b.mine.at[pl.ds((z % 2) * layer, layer)], self.ls.at[i])

    def add(self, dst, a, b, r0=0, rows=None):
        n = rows

        @pl.loop(0, n // 16)
        def _(i):
            def at(v, r):
                ref, q, off = v
                return ref.at[q, pl.ds(pl.multiple_of(off + r, 16), 16)]

            r = i * 16
            at(dst, r)[...] = at(a, r)[...] + at(b, r)[...]

    def stage(self, k, s):
        p, b = self.p, self.bufs[k]
        layer = p.Y * p.X
        r = b.sum.shape[1]
        half = r // 2
        chip = lambda z, y, x: (z * p.Y + y) * p.X + x
        col = lambda z: (chip(z, p.y, p.x), chip(z, p.y, 1 - p.x), chip(z, 1 - p.y, p.x), chip(z, 1 - p.y, 1 - p.x))
        L = p.Z
        planes = range(L)
        off = lambda z, d: p.z == z + d
        far = lambda z: jnp.logical_and(p.z != z - 1, p.z != z + 1)
        apart = lambda z: jnp.logical_and(far(z), p.z != z)
        S, H0, H1 = b.sum, 0, half
        if s == 0:
            self.admit(k)
            for z in planes:
                self.send(None, ("c", z), k, self.grads[k].at[pl.ds(z * layer, layer), 1 - p.c], S.at[pl.ds(z * layer, layer)], p.nc)
                if z < 2:
                    self.own(k, z).start()
        if s == 1:
            for z in planes:
                self.recv(None, ("c", z), k, S.at[pl.ds(z * layer, layer)])
                self.own(k, z).wait()
                me, nx, ny, nd = col(z)
                back = (z - z % 2) * layer
                self.add((S, nd, 0), (S, nd, 0), (b.mine, nd - back, 0), rows=r)
                self.send(None, ("dy", z), k, S.at[nd, pl.ds(0, half)], b.dy.at[z], p.ny)
                self.send(None, ("dx", z), k, S.at[nd, pl.ds(half, half)], b.dx.at[z], p.nx)
                for q in (nx, ny, me):
                    self.add((S, q, 0), (S, q, 0), (b.mine, q - back, 0), rows=r)
                if z + 2 < L:
                    self.own(k, z + 2).start()
        if s == 2:
            for z in planes:
                me, nx, ny, nd = col(z)
                for key, q, h, buf, to, out in (("dy", nx, H0, b.dy, p.nx, b.rx), ("dx", ny, H1, b.dx, p.ny, b.ry)):
                    self.recv(None, (key, z), k, buf.at[z])
                    self.add((S, q, h), (S, q, h), (buf, z, 0), rows=half)
                    tag = "x" if key == "dy" else "y"
                    side = 0 if key == "dy" else 1
                    self.send(apart(z), (tag, z), k, S.at[q], out.at[z], to)
                    if z > 0:
                        self.send(off(z, -1), ("z" + tag, 0), k, S.at[q], b.rz.at[side], p.up)
                    if z < L - 1:
                        self.send(off(z, 1), ("z" + tag, 1), k, S.at[q], b.rz.at[2 + side], p.down)
        if s == 3:
            me, nx, ny, nd = col(p.z)
            for tag, q, side, to, out in (("x", nx, 0, p.nx, b.rx), ("y", ny, 1, p.ny, b.ry)):
                for cond, way in ((p.has_down, 0), (p.has_up, 1)):

                    def take(q=q, side=side, way=way, tag=tag):
                        self.copy(("z" + tag, way), k, b.rz.at[2 * way + side], b.rz.at[2 * way + side], p.me).wait_recv()
                        self.add((S, q, 0), (S, q, 0), (b.rz, 2 * way + side, 0), rows=r)

                    pl.when(cond)(take)
                for z in planes:
                    self.send(p.z == z, (tag, z), k, S.at[q], out.at[z], to)
        if s == 4:
            for z in planes:
                me = col(z)[0]
                for tag, buf in (("y", b.ry), ("x", b.rx)):

                    def take(me=me, tag=tag, buf=buf, z=z):
                        self.copy((tag, z), k, buf.at[z], buf.at[z], p.me).wait_recv()
                        self.add((S, me, 0), (S, me, 0), (buf, z, 0), rows=r)

                    pl.when(far(z))(take)
        if 4 <= s < 4 + L - 1:
            hop = s - 4
            for up in (True, False):
                zz = hop if up else L - 1 - hop
                buf, key, to = (b.ru, "u", p.up) if up else (b.rd, "d", p.down)
                here = p.z == zz
                for t in range(L - 1, zz, -1) if up else range(0, zz):
                    q = chip(t, p.y, p.x)

                    def relay(q=q, t=t, buf=buf, key=key):
                        self.copy((key, t), k, buf.at[t], buf.at[t], p.me).wait_recv()
                        self.add((S, q, 0), (S, q, 0), (buf, t, 0), rows=r)

                    if hop > 0:
                        pl.when(here)(relay)
                    self.send(here, (key, t), k, S.at[q], buf.at[t], to)
        if s == 4 + L - 1:
            me = chip(p.z, p.y, p.x)
            for key, buf, ts in (("", None, (0,)), ("u", b.ru, range(1, L)), ("d", b.rd, range(0, L - 1))):
                for t in ts:

                    def last(key=key, buf=buf, t=t):
                        if buf is not None:
                            self.copy((key, t), k, buf.at[t], buf.at[t], p.me).wait_recv()

                        @pl.loop(0, r // 16)
                        def _(i):
                            rr = pl.ds(pl.multiple_of(i * 16, 16), 16)
                            v = (S[me, rr, :] if buf is None else buf[t, rr, :]).astype(F32)
                            for out, row, col, lo, w in self.outs[k]:
                                o = out.at[pl.ds(pl.multiple_of(row + i * 16, 16), 16), col : col + w]
                                if buf is None:
                                    o[...] = v[:, lo : lo + w]
                                else:
                                    o[...] += v[:, lo : lo + w]

                    when(None if buf is None else p.z == t, last)
            self.release(k)

    def stages(self):
        return 4 + self.p.Z

    def finish(self, k):
        for cond, f in self.pend[k]:
            when(cond, f)
        self.pend[k] = []


class Names:
    def __init__(self, **kw):
        self.__dict__.update(kw)


SCATTER_BUFS = ("mine", "sum", "dx", "dy", "rx", "ry", "ru", "rd", "rz")


def unit_buffers(dims, r):
    Z, Y, X = dims
    return dict(
        mine=(2 * Y * X, r), sum=(Z * Y * X, r), dx=(Z, r // 2), dy=(Z, r // 2), rx=(Z, r), ry=(Z, r), ru=(Z, r), rd=(Z, r), rz=(4, r)
    )


def scatter_sems(dims, K):
    ns = K * (7 * dims[0] + 4)
    dma, plain = pltpu.SemaphoreType.DMA, pltpu.SemaphoreType.REGULAR
    return [dma((ns,)), dma((ns,)), dma((K * dims[0],)), plain((K, 5)), plain((5,))]


KEPT_OLD = ("normed", "mpad", "e", "mixed", "kern", "vslope", "val", "base", "probs", "query", "keys", "att", "gated", "hpre", "first", "second", "uslope", "inner")


def kept_shapes(m):
    seqs = m // STRETCH
    f, b = (lambda *s: (s, F32)), (lambda *s: (s, BF16))
    return dict(
        normed=b(m, D), mpad=f(seqs, STRETCH + 8, D), e=f(m, D), mixed=b(m, D), kern=f(STRETCH, D),
        vslope=b(m, VALUE_WIDTH), val=b(m, VALUE_WIDTH), base=f(m, MXW), probs=f(m, STRETCH),
        query=b(m, Z), keys=b(m, Z), upd=f(m, D), lat=f(m, Z), res=b(m, VALUE_WIDTH), ars=b(m, VALUE_WIDTH), gated=b(m, VALUE_WIDTH), hpre=f(m, D),
        first=f(m, D), second=b(m, D), uslope=b(m, FF), inner=b(m, FF),
    )


VM = pltpu.VMEM
LIMIT = 64 * 1024 * 1024


def weight_grad(a, b, out, turned, stage, sem, lo=0, start=0, stop=None, place=None):
    stop = stop or b.shape[1] - lo

    def begin(slot, i, col, w):
        if place is None:
            cols = pl.ds(pl.multiple_of(col, 128), w)
            pltpu.make_async_copy(stage.at[slot, :, 0:w], out.at[pl.ds(i * D, D), cols], sem.at[slot]).start()
            return
        chips, pieces = place
        src = stage.at[slot, :, 0:w].reshape(chips, 2, pieces, D // (2 * chips * pieces), w)
        for q in range(pieces):
            cols = pl.ds(pl.multiple_of((q % 2) * D + col, 128), w)
            pltpu.make_async_copy(src.at[:, :, q], out.at[q // 2, pl.ds(i * chips, chips), :, :, cols], sem.at[slot]).start()

    def wait(slot, w):
        whole = stage.at[slot, :, 0:w]
        pltpu.make_async_copy(whole, whole, sem.at[slot]).wait()

    def block(slot, i, col, w):
        stage[slot, :, 0:w] = dot(turned[...], b[:, pl.ds(pl.multiple_of(lo + col, 128), w)]).astype(BF16)
        begin(slot, i, col, w)

    slots = stage.shape[0]
    rounds = (stop - start) // (slots * TILE)
    for i in range(a.shape[1] // D):
        turned[...] = a[:, i * D : (i + 1) * D].T

        @pl.loop(0, rounds * slots)
        def _(j):
            slot = j % slots

            @pl.when(jnp.logical_or(j >= slots, i > 0))
            def _():
                wait(slot, TILE)

            block(slot, i, start + j * TILE, TILE)

    rest = stop - start - rounds * slots * TILE
    wait(0, TILE)
    if rest:
        block(0, 0, stop - rest, rest)
    for slot in range(1, slots):
        wait(slot, TILE)
    if rest:
        wait(0, rest)


class Stream:
    def __init__(self, w, ring, sem):
        self.w, self.ring, self.sem = w, ring, sem
        self.width = w.shape[1]

    def copy(self, i, slot):
        rows = pl.ds(pl.multiple_of(i * TILE, TILE), TILE)
        return pltpu.make_async_copy(self.w.at[rows], self.ring.at[slot, :, 0 : self.width], self.sem.at[slot])

    def prefetch(self):
        self.copy(0, 0).start()
        self.copy(1, 1).start()

    def run(self, body, lo=0, hi=None):
        count = self.w.shape[0] // TILE
        hi = hi or count

        @pl.loop(lo // 2, hi // 2)
        def _(j):
            for slot in range(2):
                i = j * 2 + slot
                self.copy(i, slot).wait()
                body(pl.multiple_of(i * TILE, TILE), self.ring.at[slot, :, 0 : self.width])

                @pl.when(i + 2 < count)
                def _():
                    self.copy(i + 2, slot).start()


def own_shapes(m):
    seqs = m // STRETCH
    return dict(
        dd=((m, D), BF16), acc=((4, 8, D), F32), dx=((m, D), F32),
        dbase=((m, MXW), BF16), datt=((m, VALUE_WIDTH), BF16), dv=((m, VALUE_WIDTH), BF16),
        dpad=((seqs, STRETCH + 8, D), F32), dn=((m, D), F32), dkern=((STRETCH, D), F32),
    )


def frame(count):
    return -(-(-(-count // 128) + 1) // 8) * 8


def slot_rows(count):
    return -(-frame(count) // 16) * 16


def frames(n, count):
    return [(count * d) // 128 for d in range(n)]


def spread(k):
    p = lax.broadcasted_iota(jnp.int32, (D, TILE), 0)
    c = lax.broadcasted_iota(jnp.int32, (D, TILE), 1) + k * TILE
    return (c == 8 * (p % 128) + p // 128).astype(BF16)


def unpack_params(n, count, packed, full, prow, ema):
    full[...] = jnp.zeros(full.shape, F32)
    for d, r in enumerate(frames(n, count)):
        full[r : r + frame(count), :] += packed[d * slot_rows(count) : d * slot_rows(count) + frame(count), :].astype(F32)
    for i in range(O_EMA // 128):
        prow[:, i * 128 : (i + 1) * 128] = full[i : i + 1, :]
    rows = []
    for j in range(4):
        lo = O_EMA // 128 + j * D * H // 128
        t = full[lo : lo + 128, :].T
        rows.append(jnp.concatenate([t[H * k : H * (k + 1), :] for k in range(8)], axis=1))
    stack = jnp.concatenate(rows, axis=0).astype(BF16)
    for k in range(D // TILE):
        e = dot(stack, spread(k))
        for j in range(4):
            ema[j, :, k * TILE : (k + 1) * TILE] = e[j * H : (j + 1) * H, :]


def pack_grads(n, count, grow, gema, full, out):
    for i in range(O_EMA // 128):
        full[i : i + 1, :] = grow[:, i * 128 : (i + 1) * 128]
    stack = jnp.concatenate([gema[j] for j in range(4)], axis=0).astype(BF16)
    back = 0.0
    for k in range(D // TILE):
        back = back + dot(stack[:, k * TILE : (k + 1) * TILE], spread(k), 1, 1)
    for j in range(4):
        e = back[j * H : (j + 1) * H, :]
        lo = O_EMA // 128 + j * D * H // 128
        full[lo : lo + 128, :] = jnp.concatenate([e[:, k * 128 : (k + 1) * 128] for k in range(8)], axis=0).T
    for d, r in enumerate(frames(n, count)):
        out[d // 2, d % 2, 0:frame(count), :] = full[r : r + frame(count), :].astype(BF16)
        out[d // 2, d % 2, frame(count):slot_rows(count), :] = jnp.zeros((slot_rows(count) - frame(count), 128), BF16)


def size_table(n, count, m):
    rows = -(-(-(-(n * count) // 128) + frame(count)) // 8) * 8
    table = {k: v for k, v in list(kept_shapes(m).items()) + list(own_shapes(m).items())}
    table.update(
        out=((m, D), BF16), dxo=((m, D), BF16), grow=((1, O_EMA), F32), prow=((1, O_EMA), F32), ema=((4, H, D), F32),
        gema=((4, H, D), F32), full=((rows, 128), F32), packed=((n * slot_rows(count), 128), BF16),
        gsmall=((n // 2, 2, slot_rows(count), 128), BF16), wr=((FF, D), BF16), wc=((D, MXW), BF16), wv=((D, VALUE_WIDTH), BF16),
        wup=((D, FF), BF16), ring=((2, TILE, MXW), BF16), pool=((6 * D, WIDE), BF16), stage=((4, D, TILE), BF16), turned=((D, m), BF16), wh=((VALUE_WIDTH, D), BF16),
    )
    return table


class Parts:
    def __init__(self, refs):
        self.refs = list(refs)

    def take(self, names):
        got, self.refs = self.refs[: len(names)], self.refs[len(names) :]
        return dict(zip(names, got))

    def rest(self, k):
        got, self.refs = self.refs[:k], self.refs[k:]
        return got


GATHER_STARTS = (0, 1, 2, 3, 4)
LAG = GATHER_STARTS[-1]

KEPT = ("inner", "uslope", "first", "hpre", "second", "dd", "upd", "lat", "res", "ars", "gated", "val", "vslope", "probs", "query", "keys", "mixed", "normed", "e", "mpad", "kern", "grow", "prow", "ema")
HELD = KEPT + ("packed", "dbase", "dn", "acc", "dpad", "dkern", "gema", "full", "gsmall", "ring", "stage", "turned", "pool")
DEPTH = 4
UNIT = 2 * D
WIDE = MXW - UNIT


def unit_place(n, rows):
    return D * n // (2 * rows), rows // (32 * n)


def blocks_of(ref, n):
    return ref.reshape(n // 2, 2, ref.shape[0] // n, ref.shape[1])


def layer_kernel(dims, n, count, *refs):
    r = Parts(refs)
    x, g, valid = r.rest(3)
    ins = r.rest(6)
    out, dxo = r.rest(2)
    gup, gh, gmx, gv, gdown = r.rest(5)
    reduced = r.rest(6) if dims else r.rest(1)
    whole = [None] + r.rest(5) if dims else ins
    s = Names(**r.take(HELD))
    s.datt, s.dv, s.dx, s.dup, s.dsec = s.gated, s.vslope, s.first, s.inner, s.dn
    lsem, wsem, ssem = r.rest(3)
    _, v, mx, h, up, down = whole
    ws = {k: Stream(w, s.ring, wsem) for k, w in (("down", down), ("up", up), ("h", h), ("mx", mx), ("v", v))}
    if dims:
        osem, gsend, grecv, hsend, hrecv, send_sem, recv_sem, arrive = r.rest(8)
        p = Place(dims)
        p.barrier_all(n)
        mine = pl.ds(p.me * slot_rows(count), slot_rows(count))
        own = pltpu.make_async_copy(ins[0], s.packed.at[mine], lsem.at[0])
        own.start()

        def tell(i, dev, block):
            return pltpu.make_async_remote_copy(
                src_ref=ins[0], dst_ref=s.packed.at[pl.ds(block * slot_rows(count), slot_rows(count))], send_sem=gsend.at[i], recv_sem=grecv.at[i],
                device_id=(dev,), device_id_type=MESH,
            )

        @pl.loop(1, n)
        def _(i):
            tell(i, (p.me + i) % n, p.me).start()

        gat = Gather(p, ins[1:], whole[1:], send_sem, recv_sem)
        cps = [pltpu.make_async_copy(i, o.at[pl.ds(p.me * i.shape[0], i.shape[0])], osem.at[k]) for k, (i, o) in enumerate(zip(ins[1:], whole[1:]))]
        for cp in cps:
            cp.start()
        last = gat.stages() - 1

        def get(t):
            for k, q in enumerate(GATHER_STARTS):
                if 0 <= t - q <= last:
                    gat.stage(k, t - q)
                    if t - q == last:
                        cps[k].wait()

        def small_here():
            own.wait()

            @pl.loop(1, n)
            def _(i):
                tell(i, p.me, (p.me - i + n) % n).wait()

        cols = lambda ref, lo, w: ref.at[:, :, :, pl.ds(lo, w)]
        up4, mx4 = blocks_of(gup, n), blocks_of(gmx, n)
        rv, rmx, rh, rup, rdown, rsmall = reduced
        halves = lambda o, row: [(o, row, 0, 0, D), (o, row + 32, 0, D, D)]
        units = [
            (gdown.at[0], halves(rdown, 0)),
            (gdown.at[1], halves(rdown, 64)),
            (cols(up4, 0, UNIT), [(rup, 0, 0, 0, UNIT)]),
            (cols(up4, UNIT, UNIT), [(rup, 0, UNIT, 0, UNIT)]),
            (gh.at[0], halves(rh, 0)),
            (blocks_of(gv, n), [(rv, 0, 0, 0, UNIT)]),
            (cols(mx4, 0, UNIT), [(rmx, 0, 0, 0, UNIT)]),
            (cols(mx4, UNIT, WIDE), [(rmx, 0, UNIT, 0, WIDE)]),
        ]
        sc = Scatter(p, [u[0] for u in units], s.pool, DEPTH, [u[1] for u in units], *r.rest(5))
        S = sc.stages()

        def put(t):
            for k, q in enumerate(UNIT_STARTS):
                if 0 <= t - q < S:
                    sc.stage(k, t - q)

        def give(i, dev, slot):
            return pltpu.make_async_remote_copy(
                src_ref=s.gsmall.at[dev // 2, dev % 2], dst_ref=arrive.at[slot], send_sem=hsend.at[i], recv_sem=hrecv.at[i],
                device_id=(dev,), device_id_type=MESH,
            )
    else:
        S = 8
        get = put = lambda t: None

        def small_here():
            small = pltpu.make_async_copy(ins[0], s.packed, lsem.at[0])
            small.start()
            small.wait()

    G = dims[0] + 2 if dims else 6
    q = lambda i, w=UNIT, lo=0: s.pool.at[i * D : (i + 1) * D, lo : lo + w]
    w = Names(v=q(0), mx1=q(1, WIDE), mx2=q(2), up1=q(3), up2=q(4), h1=q(5, D), h2=q(5, D, D))
    jobs = [
        [(v, w.v)],
        [(mx.at[:, 0:WIDE], w.mx1), (mx.at[:, WIDE:MXW], w.mx2)],
        [(h.at[0:D], w.h1), (h.at[D : 2 * D], w.h2)],
        [(up.at[:, 0:UNIT], w.up1), (up.at[:, UNIT:FF], w.up2)],
    ]
    load, i = [], 0
    for pairs in jobs:
        load.append([pltpu.make_async_copy(a, b, lsem.at[1 + i + e]) for e, (a, b) in enumerate(pairs)])
        i += len(pairs)

    def begin(k):
        for c in load[k]:
            c.start()

    f = Forward(x, valid, s.prow, s.ema, w, s)
    b = Backward(x, g, valid, s.prow, s.ema, None, s, s, s.grow, s.gema)
    grad = lambda *a, **kw: weight_grad(*a[:3], s.turned, s.stage, ssem, **kw)
    s.grow[...] = jnp.zeros(s.grow.shape, F32)
    get(0)
    b.cot()
    get(1)
    small_here()
    unpack_params(n, count, s.packed, s.full, s.prow, s.ema)
    f.norm_one()
    get(2)
    f.ema_kernel()
    get(3)
    f.smooth(0)
    get(4)
    f.smooth(1)
    f.mix()
    for t in range(5, G + 1):
        get(t)
    begin(0)
    get(G + 1)
    begin(1)
    load[0][0].wait()
    f.values()
    get(G + 2)
    begin(2)
    load[1][0].wait()
    f.base_one()
    load[1][1].wait()
    f.base_two()
    f.attend()
    get(G + 3)
    begin(3)
    for c in load[2]:
        c.wait()
    f.hidden()
    f.norm_two()
    get(G + 4)
    load[3][0].wait()
    f.up(0)
    for t in range(G + 5, G + LAG):
        get(t)
    load[3][1].wait()
    f.up(1)
    if dims:
        sc.open()
    grad(s.inner, s.dd, gdown, place=unit_place(n, FF) if dims else None)
    put(0)
    get(G + LAG)
    ws["down"].prefetch()
    s.dn[...] = jnp.zeros(s.dn.shape, F32)
    b.pad_tail()
    put(1)
    ws["down"].run(b.down_tile)
    ws["up"].prefetch()
    put(2)
    grad(s.second, s.dup, gup, start=0, stop=UNIT)
    put(3)
    grad(s.second, s.dup, gup, start=UNIT, stop=FF)
    put(4)
    b.output(out)
    ws["up"].run(b.second_tile)
    ws["h"].prefetch()
    put(5)
    b.norm_two()
    put(6)
    grad(s.gated, s.dbase, gh, lo=C_HX, place=unit_place(n, VALUE_WIDTH) if dims else None)
    put(7)
    ws["h"].run(b.gated_tile)
    ws["mx"].prefetch()
    put(8)
    b.attend()
    grad(s.normed, s.dv, gv)
    put(9)
    grad(s.mixed, s.dbase, gmx, start=0, stop=UNIT)
    put(10)
    grad(s.mixed, s.dbase, gmx, start=UNIT)
    put(11)
    ws["mx"].run(b.mixed_tile)
    ws["v"].prefetch()
    put(12)
    ws["v"].run(b.normed_tile)
    b.smooth_signal(0)
    put(13)
    b.smooth_signal(1)
    put(14)
    b.smooth_filter()
    put(15)
    b.ema_grads()
    b.norm_one(dxo)
    put(16)
    pack_grads(n, count, s.grow, s.gema, s.full, s.gsmall)
    if dims:
        me = p.me

        @pl.loop(1, n)
        def _(i):
            give(i, (me + i) % n, i).start()

        for t in range(17, UNIT_STARTS[-1] + S):
            put(t)
        rsmall[...] = s.gsmall[me // 2, me % 2].astype(F32)

        @pl.loop(1, n)
        def _(i):
            give(i, me, i).wait()
            rsmall[...] += arrive[i].astype(F32)

        gat.finish()
    else:
        keep = pltpu.make_async_copy(s.gsmall, reduced[0], lsem.at[0])
        keep.start()
        keep.wait()


UNIT_STARTS = (0, 1, 3, 4, 8, 9, 11, 12)
GATHER_STARTS = (0, 1, 2, 3, 6)
LAG = GATHER_STARTS[-1]


def run_kernel(body, ins, outs, scratch, cid):
    vm, hbm = pl.BlockSpec(memory_space=VM), pl.BlockSpec(memory_space=pl.ANY)
    params = dict(vmem_limit_bytes=LIMIT)
    if cid is not None:
        params.update(collective_id=cid, has_side_effects=True)
    return pl.pallas_call(
        body,
        out_shape=[jax.ShapeDtypeStruct(o[0], o[1]) for o in outs],
        in_specs=[vm if i[1] else hbm for i in ins],
        out_specs=[vm if o[2] else hbm for o in outs],
        scratch_shapes=scratch,
        compiler_params=pltpu.CompilerParams(**params),
    )(*[i[0] for i in ins])


def copy_kernel(k, *refs):
    ins, outs, bufs, sem = refs[:k], refs[k : 2 * k], refs[2 * k : 3 * k], refs[3 * k]
    get = [pltpu.make_async_copy(a, b, sem.at[i]) for i, (a, b) in enumerate(zip(ins, bufs))]
    put = [pltpu.make_async_copy(a, b, sem.at[k + i]) for i, (a, b) in enumerate(zip(bufs, outs))]
    for c in get:
        c.start()
    for c, d in zip(get, put):
        c.wait()
        d.start()
    for d in put:
        d.wait()


def settle(arrays):
    return run_kernel(
        functools.partial(copy_kernel, len(arrays)), [(a, False) for a in arrays], [(a.shape, a.dtype, False) for a in arrays],
        [VM(a.shape, a.dtype) for a in arrays] + [pltpu.SemaphoreType.DMA((2 * len(arrays),))], None,
    )


def layer(dims, n, count, x, g, valid, arrays):
    m = x.shape[0]
    table = size_table(n, count, m)
    dma = pltpu.SemaphoreType.DMA
    tmp = lambda names: [VM(*table[k]) for k in names]
    whole = [(n * a.shape[0], a.shape[1]) if dims else a.shape for a in arrays]
    parts = [(q[0] // n, q[1]) for q in whole]
    scratch = tmp(HELD) + [dma((8,)), dma((2,)), dma((4,))]
    unit = lambda k: (k, n // 2, 2, 32, UNIT)
    o = [((m, D), BF16, True)] * 2
    o += [(q, BF16, False) for q in (whole[4], unit(1) if dims else whole[3], whole[2], whole[1], unit(2) if dims else whole[5])]
    if dims:
        o += [(parts[i], F32, True) for i in (1, 2, 3, 4, 5)] + [((slot_rows(count), 128), F32, True)]
        o += [(q, BF16, False) for q in whole[1:]]
        ns = sems_needed(dims, 5)
        scratch += [dma((5,)), dma((n,)), dma((n,)), dma((n,)), dma((n,)), dma((ns,)), dma((ns,)), VM((n, slot_rows(count), 128), BF16)]
        scratch += scatter_sems(dims, len(UNIT_STARTS))
    else:
        o += [table["gsmall"] + (False,)]
    ins = [(x, True), (g, True), (valid, True)] + [(q, False) for q in arrays]
    res = run_kernel(functools.partial(layer_kernel, dims, n, count), ins, o, scratch, 0 if dims else None)
    out, dx = res[:2]
    if dims:
        gv, gmx, gh, gup, gdown, gs = res[7:13]
    else:
        gup, gh, gmx, gv, gdown = res[2:7]
        gs = res[7].reshape(n * slot_rows(count), 128)
    return out, dx, gv, gmx, gh, gup, gdown, gs


def frame_in(small, me):
    count = small.shape[0]
    line = lax.dynamic_update_slice(jnp.zeros((frame(count) * 128,), small.dtype), small, ((me * count) % 128,))
    return jnp.pad(line.reshape(frame(count), 128), ((0, slot_rows(count) - frame(count)), (0, 0)))


def frame_out(block, me, count):
    return lax.dynamic_slice(block.reshape(-1), ((me * count) % 128,), (count,))


def grid_of(n):
    return (n // 8, 2, 2)


def per_device(n, inputs, lengths, cotangent, v_weight, mx_weight, h_weight, up_weight, down_weight, small_params):
    shape = inputs.shape
    m, count = shape[0] * shape[1] * shape[2], small_params.shape[0]
    me = lax.axis_index("fsdp")
    x, g = inputs.reshape(m, D), cotangent.reshape(m, D)
    mask = (jnp.arange(shape[2]) < lengths[:, :, None]).astype(F32).reshape(m, 1)
    valid = jnp.broadcast_to(mask, (m, 128))
    arrays = (frame_in(small_params, me), v_weight, mx_weight, h_weight, up_weight, down_weight)
    dims = grid_of(n) if n == 32 else None
    if not dims:
        arrays = [lax.all_gather(a, "fsdp", axis=0, tiled=True) for a in arrays]
    out, dx, gv, gmx, gh, gup, gdown, gs = layer(dims, n, count, x, g, valid, arrays)
    if dims:
        out, dx, gv, gmx, gh, gup, gdown = settle((out, dx, gv, gmx, gh, gup, gdown))
    else:
        gv, gmx, gh, gup, gdown, gs = (
            lax.psum_scatter(a.astype(F32), "fsdp", scatter_dimension=0, tiled=True) for a in (gv, gmx, gh, gup, gdown, gs)
        )
    return out.reshape(shape), dx.reshape(shape), gv, gmx, gh, gup, gdown, frame_out(gs, me, count)


def solution(mesh):
    rows, cols = P("fsdp", None), P(None, "fsdp", None, None)
    return jax.shard_map(
        functools.partial(per_device, mesh.shape["fsdp"]),
        mesh=mesh,
        in_specs=(cols, P(None, "fsdp"), cols, rows, rows, rows, rows, rows, P("fsdp")),
        out_specs=(cols, cols, rows, rows, rows, rows, rows, P("fsdp")),
        check_vma=False,
    )
```
